32 devices in a mesh: dp: 16 (over z, x, core), tensor: 2 (over y).
Axes of the slice: x: 2, y: 2, z: 4, core: 2. Of those that a mesh axis runs over, the one named last changes fastest.
Arguments:
- tokens: bfloat16 [2048, 512], P('dp'), may hold values from -10 to 10
- lengths: int32 [16], P('dp'), may hold values from 32 to 128, as said below
- cotangent: float32 [2048, 512], P('dp'), may hold values from -6 to 6
- params: float32 [1, 2, 3157504], P(None, 'tensor', 'dp'), may hold values from -2 to 2
- shared: float32 [1, 7168], P(None, 'dp'), may hold values from -0.6 to 0.6
- first_moment: float32 [1, 2, 3157504], P(None, 'tensor', 'dp'), may hold values from -4 to 4
- second_moment: float32 [1, 2, 3157504], P(None, 'tensor', 'dp'), may hold values from 0.01 to 1
- first_shared: float32 [1, 7168], P(None, 'dp'), may hold values from -4 to 4
- second_shared: float32 [1, 7168], P(None, 'dp'), may hold values from 4.096 to 40.96
Outputs:
- result: float32 [2048, 512], P('dp')
- grad_tokens: float32 [2048, 512], P('dp')
- grad_params: float32 [1, 2, 3157504], P(None, 'tensor', 'dp')
- grad_shared: float32 [1, 7168], P(None, 'dp')
- new_params: float32 [1, 2, 3157504], P(None, 'tensor', 'dp')
- new_shared: float32 [1, 7168], P(None, 'dp')
- new_first_moment: float32 [1, 2, 3157504], P(None, 'tensor', 'dp')
- new_second_moment: float32 [1, 2, 3157504], P(None, 'tensor', 'dp')
- new_first_shared: float32 [1, 7168], P(None, 'dp')
- new_second_shared: float32 [1, 7168], P(None, 'dp')
The draws below stay inside these ranges and needn't reach their ends.
Inputs may be any that keep to these rules, and one draw needn't show every extreme that they name: Valid tokens lead each sequence. The first sequence holds 32 valid tokens and the last 128; lengths grow with the sequence index, with a jitter.
All inputs are finite; a program needn't handle non-finite values.
Results may differ from the reference program's by a relative error of at most 0.02.
Values may be sent and summed in bfloat16 or wider, within the bound.
No kernel may reach another device: no remote copies, remote signals or barrier semaphores. Data moves between devices by JAX's collectives and lax.ppermute only.
A program may use at most 128 MiB of HBM per device.

```python
import math
from functools import partial
import jax
import jax.numpy as jnp
from jax import lax

D = 512
FF = 2048
HEADS = 8
HEAD_DIM = 64
KERNEL = 31
SEQ_LEN = 128
LAYERS = 1
SEQS = 16
PARAM_RAW = 3157504
PARAM_HALF = 3157504
SHARED_LEN = 7168
N_TENSOR = 2


def draw_tokens(key, part):
    key_noise, key_pattern = jax.random.split(key)
    noise = jnp.clip(jax.random.normal(key_noise, (SEQS, SEQ_LEN, D), jnp.float32), -4.0, 4.0)
    pattern = jnp.clip(jax.random.normal(key_pattern, (D,), jnp.float32), -3.0, 3.0)
    ramp = 2.0 * jnp.arange(SEQS).astype(jnp.float32) / SEQS
    mixed = noise + ramp[:, None, None] * pattern[None, None, :]
    return mixed.reshape(SEQS * SEQ_LEN, D).astype(jnp.bfloat16)


def draw_lengths(key, part):
    seq_order = jnp.arange(SEQS)
    jitter = jax.random.randint(key, (SEQS,), 0, SEQ_LEN // 4 + 1)
    baseline = SEQ_LEN // 4 + 3 * SEQ_LEN // 4 * seq_order // SEQS
    lengths = jnp.minimum(baseline + jitter, SEQ_LEN)
    lengths = jnp.where(seq_order == 0, SEQ_LEN // 4, lengths)
    lengths = jnp.where(seq_order == SEQS - 1, SEQ_LEN, lengths)
    return lengths.astype(jnp.int32)


def draw_params(key, part):
    ff_part = FF // N_TENSOR
    att_part = HEADS * HEAD_DIM // N_TENSOR
    chan_part = D // N_TENSOR
    inv_width = D ** (-0.5)
    feed_list = [(D * ff_part, inv_width), (ff_part, 0.1), (ff_part * D, FF ** (-0.5))]
    attn_list = [(D * 3 * att_part, inv_width), (D * att_part, inv_width), (att_part * D, 0.5 * math.sqrt(SEQ_LEN) * inv_width), (att_part, 0.5), (att_part, 0.5)]
    conv_list = [(D * 2 * chan_part, inv_width), (2 * chan_part, 0.1), (KERNEL * chan_part, KERNEL ** (-0.5)), (chan_part, 0.1), (chan_part, 0.1), (chan_part, 0.1), (chan_part * D, inv_width)]
    segments = feed_list + attn_list + conv_list + feed_list
    blocks = [jnp.full((amount,), factor, jnp.float32) for amount, factor in segments]
    blocks.append(jnp.full((PARAM_HALF - PARAM_RAW,), 0.05, jnp.float32))
    scale_vec = jnp.concatenate(blocks)
    noise = jnp.clip(jax.random.normal(key, (LAYERS, N_TENSOR, PARAM_HALF), jnp.float32), -4.0, 4.0)
    return noise * scale_vec[None, None, :]


def block_scale(own_key, extent, cuts, smallest, largest):
    factor_of = 1.0
    for dim, shards_of in cuts:
        draws = jax.random.uniform(jax.random.fold_in(jax.random.fold_in(own_key, 6), dim), (shards_of,), jnp.float32, smallest / len(cuts), largest / len(cuts))
        factor_of = factor_of * jnp.repeat(jnp.exp(draws), extent[dim] // shards_of).reshape((-1,) + (1,) * (len(extent) - 1 - dim))
    return factor_of


def bell_draw(key, dims, scale, limit, cuts=(), held_as=jnp.bfloat16):
    array = jax.random.normal(key, dims, jnp.float32) * scale
    if len(cuts) > 0:
        array = block_scale(key, dims, cuts, -0.22, 0.18) * array
    return jnp.clip(array, min=-limit, max=limit).astype(held_as)


def setup_inputs(seed: int = 0) -> dict:
    key_list = jax.random.split(jax.random.key(seed), 10)
    return {
        "tokens": draw_tokens(jax.random.fold_in(key_list[9], 71), 0),
        "lengths": draw_lengths(jax.random.fold_in(key_list[9], 71), 0),
        "cotangent": bell_draw(key_list[2], (SEQS * SEQ_LEN, D), 1.0, 6.0, ((0, 16),), jnp.float32),
        "params": draw_params(jax.random.fold_in(key_list[9], 71), 0),
        "shared": bell_draw(key_list[4], (LAYERS, SHARED_LEN), 0.1, 0.6, ((1, 16),), jnp.float32),
        "first_moment": bell_draw(key_list[5], (LAYERS, N_TENSOR, PARAM_HALF), 1.0, 4.0, ((1, 2), (2, 16)), jnp.float32),
        "second_moment": jnp.clip(jnp.exp(math.log(1.0) - 4.6051702 * jax.random.uniform(key_list[6], (LAYERS, N_TENSOR, PARAM_HALF), jnp.float32) ** block_scale(key_list[6], (LAYERS, N_TENSOR, PARAM_HALF), ((1, 2), (2, 16)), -0.2, 0.2)), 0.01, 1.0),
        "first_shared": bell_draw(key_list[7], (LAYERS, SHARED_LEN), 1.0, 4.0, ((1, 16),), jnp.float32),
        "second_shared": jnp.clip(jnp.exp(math.log(40.96) - 2.30258502 * jax.random.uniform(key_list[8], (LAYERS, SHARED_LEN), jnp.float32) ** block_scale(key_list[8], (LAYERS, SHARED_LEN), ((1, 16),), -0.2, 0.2)), 4.096, 40.96),
    }


NORM_EPS = 1e-05
BATCH_EPS = 1e-05
LEARN_RATE = 0.02
BETA_ONE = 0.9
BETA_TWO = 0.999
ADAM_EPS = 1e-08
WEIGHT_DECAY = 0.1
STEP_COUNT = 5
FLOAT_PIECES = (1, 6, 7, 9, 10, 11, 12, 13, 16)

def mat_product(left, right):
    return jnp.dot(left, right, preferred_element_type=jnp.float32)

def left_transposed_matmul(left, right):
    return lax.dot_general(left, right, (((0,), (0,)), ((), ())), preferred_element_type=jnp.float32)

def right_trans_product(left, right):
    return lax.dot_general(left, right, (((1,), (1,)), ((), ())), preferred_element_type=jnp.float32)

def rounded(values):
    return lax.optimization_barrier(values.astype(jnp.bfloat16)).astype(jnp.float32)

def batched(pattern, left, right):
    return jnp.einsum(pattern, left.astype(jnp.float32), right.astype(jnp.float32))

def layer_norm(values, scaling, offset):
    centred = values - lax.optimization_barrier(jnp.mean(values, axis=-1, keepdims=True))
    spread = lax.optimization_barrier(jnp.mean(centred * centred, axis=-1, keepdims=True))
    return centred * lax.rsqrt(spread + NORM_EPS) * (1.0 + scaling) + offset

def norm_back(values, scaling, offset, d_output):
    primal_out, pull_back = jax.vjp(layer_norm, values, scaling, offset)
    return pull_back(d_output)

def silu_slope(values):
    sigma_vals = jax.nn.sigmoid(values)
    return sigma_vals * (1.0 + values * (1.0 - sigma_vals))

def position_table(seq_len, model_width):
    distance = (seq_len - 1 - jnp.arange(2 * seq_len - 1)).astype(jnp.float32)
    freq_index = jnp.arange(model_width // 2).astype(jnp.float32)
    rates = jnp.exp(freq_index * (-2.0 * math.log(10000.0) / model_width))
    angles = distance[:, None] * rates[None, :]
    table = jnp.stack([jnp.sin(angles), jnp.cos(angles)], axis=-1)
    return table.reshape(2 * seq_len - 1, model_width).astype(jnp.bfloat16)

def piece_shapes(model_width, ff_part, att_part, chan_part, kernel_len):
    feed_list = [(model_width, ff_part), (ff_part,), (ff_part, model_width)]
    attn_list = [(model_width, 3 * att_part), (model_width, att_part), (att_part, model_width), (att_part,), (att_part,)]
    conv_list = [(model_width, 2 * chan_part), (2 * chan_part,), (kernel_len, chan_part), (chan_part,), (chan_part,), (chan_part,), (chan_part, model_width)]
    return feed_list + attn_list + conv_list + feed_list

def split_pieces(buffer, shapes):
    pieces = []
    offset_at = 0
    for shape_now in shapes:
        amount = math.prod(shape_now)
        pieces.append(buffer[offset_at:offset_at + amount].reshape(shape_now))
        offset_at += amount
    return pieces

def cast_pieces(pieces):
    return [element.astype(jnp.float32) if slot_index in FLOAT_PIECES else element for slot_index, element in enumerate(pieces)]

def join_pieces(gradient_list, total_len):
    flattened = jnp.concatenate([part_grad.reshape(-1) for part_grad in gradient_list])
    return jnp.pad(flattened, (0, total_len - flattened.shape[0]))

def rel_shift(position):
    seq_len = position.shape[-2]
    index_grid = (seq_len - 1 - jnp.arange(seq_len)[:, None] + jnp.arange(seq_len)[None, :]).astype(jnp.int32)
    index_grid = jnp.broadcast_to(index_grid, position.shape[:-1] + (seq_len,))
    return jnp.take_along_axis(position, index_grid, axis=-1)

def rel_unshift(grad_shifted):
    seq_len = grad_shifted.shape[-1]
    zeros_full = jnp.zeros(grad_shifted.shape[:-1] + (2 * seq_len - 1,), jnp.float32)
    primal_out, pull_back = jax.vjp(rel_shift, zeros_full)
    return pull_back(grad_shifted.astype(jnp.float32))[0].astype(jnp.bfloat16)

def attention_scores(query_u, query_v, keys_b, pos_rows):
    content = batched('bihd,bjhd->bhij', query_u, keys_b)
    position = batched('bihd,rhd->bhir', query_v, pos_rows)
    return (content + rel_shift(position)) * (1.0 / math.sqrt(query_u.shape[-1]))

def key_mask(seq_lengths):
    return (jnp.arange(SEQ_LEN)[None, :] < seq_lengths[:, None])[:, None, None, :]

def attend_forward(query_u, query_v, keys_b, values_b, pos_rows, seq_lengths):
    scores = attention_scores(query_u, query_v, keys_b, pos_rows)
    exponent = jnp.where(key_mask(seq_lengths), jnp.exp(scores), 0.0)
    totals = lax.optimization_barrier(jnp.sum(exponent, axis=-1))
    probs = (exponent / totals[..., None]).astype(jnp.bfloat16)
    context = batched('bhij,bjhd->bihd', probs, values_b)
    return (context, jnp.log(totals))

def attend_backward(query_u, query_v, keys_b, values_b, pos_rows, seq_lengths, log_total, d_context):
    scale = 1.0 / math.sqrt(query_u.shape[-1])
    scores = attention_scores(query_u, query_v, keys_b, pos_rows)
    probs = jnp.where(key_mask(seq_lengths), jnp.exp(scores - log_total[..., None]), 0.0)
    probs_b = probs.astype(jnp.bfloat16)
    d_values = batched('bhij,bihd->bjhd', probs_b, d_context)
    d_probs = batched('bihd,bjhd->bhij', d_context, values_b)
    row_dot = lax.optimization_barrier(jnp.sum(probs * d_probs, axis=-1, keepdims=True))
    d_scores = (probs * (d_probs - row_dot) * scale).astype(jnp.bfloat16)
    d_query_u = batched('bhij,bjhd->bihd', d_scores, keys_b)
    d_keys = batched('bhij,bihd->bjhd', d_scores, query_u)
    d_position = rel_unshift(d_scores)
    d_query_v = batched('bhir,rhd->bihd', d_position, pos_rows)
    d_pos_rows = batched('bhir,bihd->rhd', d_position, query_v)
    return (d_query_u, d_query_v, d_keys, d_values, d_pos_rows)

def conv_front(valid, pre_glu, tap_weights, tap_bias):
    chan_part = pre_glu.shape[-1] // 2
    gated = pre_glu[..., :chan_part] * jax.nn.sigmoid(pre_glu[..., chan_part:]) * valid[..., None]
    kernel_len = tap_weights.shape[0]
    margin = (kernel_len - 1) // 2
    seq_len = gated.shape[-2]
    padded = jnp.pad(gated, [(0, 0), (margin, kernel_len - 1 - margin), (0, 0)])
    total = tap_bias + jnp.zeros_like(gated)
    for tap_idx in range(kernel_len):
        total = total + tap_weights[tap_idx] * padded[:, tap_idx:tap_idx + seq_len, :]
    return total

def batch_apply(conv_out, gamma_vec, beta_vec, mean_vec, inv_std):
    return jax.nn.silu((conv_out - mean_vec) * inv_std * (1.0 + gamma_vec) + beta_vec)

def feed_forward(resid, parts, first_idx, scaling, offset, b_out):
    normed = layer_norm(resid, scaling, offset).astype(jnp.bfloat16)
    branch = b_out
    per_part = []
    for pieces in parts:
        hidden_pre = mat_product(normed, pieces[first_idx]) + pieces[first_idx + 1]
        hidden = jax.nn.silu(hidden_pre).astype(jnp.bfloat16)
        branch = branch + rounded(mat_product(hidden, pieces[first_idx + 2]))
        per_part.append((hidden_pre, hidden))
    return (resid + 0.5 * branch, (normed, per_part))

def feed_back(d_resid, resid, saved, parts, first_idx, scaling, offset):
    normed, per_part = saved
    d_branch = 0.5 * d_resid
    grad_bout = lax.optimization_barrier(jnp.sum(d_branch, axis=0))
    branch_gradient_second = d_branch.astype(jnp.bfloat16)
    d_normed = jnp.zeros_like(resid)
    gradient_list = []
    for pieces, stored in zip(parts, per_part):
        hidden_pre, hidden = stored
        grad_wout = left_transposed_matmul(hidden, branch_gradient_second)
        d_pre = right_trans_product(branch_gradient_second, pieces[first_idx + 2]) * silu_slope(hidden_pre)
        grad_bin = lax.optimization_barrier(jnp.sum(d_pre, axis=0))
        d_pre_b = d_pre.astype(jnp.bfloat16)
        grad_win = left_transposed_matmul(normed, d_pre_b)
        d_normed = d_normed + rounded(right_trans_product(d_pre_b, pieces[first_idx]))
        gradient_list.append([grad_win, grad_bin, grad_wout])
    d_input, grad_scale, grad_offset = norm_back(resid, scaling, offset, d_normed)
    return (d_resid + d_input, gradient_list, [grad_scale, grad_offset, grad_bout])

def attention_forward(resid, parts, scaling, offset, b_out, lengths, table):
    seq_count = lengths.shape[0]
    normed = layer_norm(resid, scaling, offset).astype(jnp.bfloat16)
    branch = b_out
    per_part = []
    for pieces in parts:
        w_qkv, w_pos, w_att, bias_u, bias_v = pieces[3:8]
        att_part = w_att.shape[0]
        head_count = att_part // HEAD_DIM

        def to_heads(block):
            return block.reshape(seq_count, SEQ_LEN, head_count, HEAD_DIM)
        qkv_rows = mat_product(normed, w_qkv)
        query = qkv_rows[:, :att_part]
        query_u = to_heads((query + bias_u).astype(jnp.bfloat16))
        query_v = to_heads((query + bias_v).astype(jnp.bfloat16))
        keys_b = to_heads(qkv_rows[:, att_part:2 * att_part].astype(jnp.bfloat16))
        values_b = to_heads(qkv_rows[:, 2 * att_part:].astype(jnp.bfloat16))
        pos_rows = mat_product(table, w_pos).astype(jnp.bfloat16).reshape(2 * SEQ_LEN - 1, head_count, HEAD_DIM)

        def one_sequence(seq_inputs):
            query_one, query_two, keys_one, values_one, length_one = seq_inputs
            context, log_total = attend_forward(query_one[None], query_two[None], keys_one[None], values_one[None], pos_rows, length_one[None])
            return (context[0], log_total[0])
        context, log_total = lax.map(one_sequence, (query_u, query_v, keys_b, values_b, lengths))
        context_rows_second = context.reshape(seq_count * SEQ_LEN, att_part).astype(jnp.bfloat16)
        branch = branch + rounded(mat_product(context_rows_second, w_att))
        per_part.append((query_u, query_v, keys_b, values_b, pos_rows, log_total, context_rows_second))
    return (resid + branch, (normed, per_part))

def attention_back(d_resid, resid, saved, parts, scaling, offset, lengths, table):
    normed, per_part = saved
    seq_count = lengths.shape[0]
    rows_total = seq_count * SEQ_LEN
    grad_bout = lax.optimization_barrier(jnp.sum(d_resid, axis=0))
    branch_gradient_second = d_resid.astype(jnp.bfloat16)
    d_normed = jnp.zeros_like(resid)
    gradient_list = []
    for pieces, stored in zip(parts, per_part):
        w_qkv, w_pos, w_att, bias_u, bias_v = pieces[3:8]
        query_u, query_v, keys_b, values_b, pos_rows, log_total, context_rows_second = stored
        att_part = w_att.shape[0]
        attention_weight_gradient = left_transposed_matmul(context_rows_second, branch_gradient_second)
        d_context = right_trans_product(branch_gradient_second, w_att).astype(jnp.bfloat16).reshape(query_u.shape)

        def one_back(seq_inputs):
            query_one, query_two, keys_one, values_one, length_one, log_one, d_one = seq_inputs
            results = attend_backward(query_one[None], query_two[None], keys_one[None], values_one[None], pos_rows, length_one[None], log_one[None], d_one[None])
            return (results[0][0], results[1][0], results[2][0], results[3][0], results[4])
        d_query_u, d_query_v, d_keys, d_values, d_pos_seq = lax.map(one_back, (query_u, query_v, keys_b, values_b, lengths, log_total, d_context))
        d_pos_rows = lax.optimization_barrier(jnp.sum(d_pos_seq, axis=0))
        content_bias_gradient = lax.optimization_barrier(jnp.sum(d_query_u, axis=(0, 1))).reshape(att_part)
        position_bias_gradient = lax.optimization_barrier(jnp.sum(d_query_v, axis=(0, 1))).reshape(att_part)
        d_query = (d_query_u + d_query_v).reshape(rows_total, att_part)
        d_qkv = jnp.concatenate([d_query, d_keys.reshape(rows_total, att_part), d_values.reshape(rows_total, att_part)], axis=1).astype(jnp.bfloat16)
        query_key_value_weight_gradient = left_transposed_matmul(normed, d_qkv)
        position_weight_gradient = lax.dot_general(table.astype(jnp.float32), d_pos_rows.reshape(2 * SEQ_LEN - 1, att_part), (((0,), (0,)), ((), ())), precision=lax.Precision.HIGHEST)
        d_normed = d_normed + rounded(right_trans_product(d_qkv, w_qkv))
        gradient_list.append([query_key_value_weight_gradient, position_weight_gradient, attention_weight_gradient, content_bias_gradient, position_bias_gradient])
    d_input, grad_scale, grad_offset = norm_back(resid, scaling, offset, d_normed)
    return (d_resid + d_input, gradient_list, [grad_scale, grad_offset, grad_bout])

def conv_forward(resid, parts, scaling, offset, b_out, valid):
    seq_count = valid.shape[0]
    normed = layer_norm(resid, scaling, offset).astype(jnp.bfloat16)
    count_all = jnp.sum(valid)
    branch = b_out
    per_part = []
    for pieces in parts:
        w_glu, b_glu, tap_weights, tap_bias, gamma_vec, beta_vec, w_conv = pieces[8:15]
        chan_part = w_conv.shape[0]
        pre_glu = (mat_product(normed, w_glu) + b_glu).reshape(seq_count, SEQ_LEN, 2 * chan_part)
        conv_out = conv_front(valid, pre_glu, tap_weights, tap_bias)
        masked = conv_out * valid[..., None]
        mean_vec = lax.optimization_barrier(jnp.sum(masked, axis=(0, 1))) / count_all
        inv_std = lax.rsqrt(lax.optimization_barrier(jnp.sum(masked * conv_out, axis=(0, 1))) / count_all - mean_vec * mean_vec + BATCH_EPS)
        activated = batch_apply(conv_out, gamma_vec, beta_vec, mean_vec, inv_std).reshape(seq_count * SEQ_LEN, chan_part).astype(jnp.bfloat16)
        branch = branch + rounded(mat_product(activated, w_conv))
        per_part.append((pre_glu, conv_out, mean_vec, inv_std, activated))
    return (resid + branch, (normed, count_all, per_part))

def conv_back(d_resid, resid, saved, parts, scaling, offset, valid):
    normed, count_all, per_part = saved
    grad_bout = lax.optimization_barrier(jnp.sum(d_resid, axis=0))
    branch_gradient_second = d_resid.astype(jnp.bfloat16)
    d_normed = jnp.zeros_like(resid)
    gradient_list = []
    for pieces, stored in zip(parts, per_part):
        w_glu, b_glu, tap_weights, tap_bias, gamma_vec, beta_vec, w_conv = pieces[8:15]
        pre_glu, conv_out, mean_vec, inv_std, activated = stored
        grad_wconv = left_transposed_matmul(activated, branch_gradient_second)
        d_act = right_trans_product(branch_gradient_second, w_conv).reshape(conv_out.shape)
        primal_out, pull_norm = jax.vjp(batch_apply, conv_out, gamma_vec, beta_vec, mean_vec, inv_std)
        d_conv, grad_gamma, grad_beta, d_mean, d_inv = pull_norm(d_act)
        d_var = -0.5 * inv_std * inv_std * inv_std * d_inv
        d_first = (d_mean - 2.0 * mean_vec * d_var) / count_all
        d_square = d_var / count_all
        d_conv = d_conv + valid[..., None] * (d_first + 2.0 * conv_out * d_square)
        primal_two, pull_front = jax.vjp(partial(conv_front, valid), pre_glu, tap_weights, tap_bias)
        d_pre, grad_taps, grad_tbias = pull_front(d_conv)
        d_pre = d_pre.reshape(-1, d_pre.shape[-1])
        grad_bglu = lax.optimization_barrier(jnp.sum(d_pre, axis=0))
        d_pre_b = d_pre.astype(jnp.bfloat16)
        grad_wglu = left_transposed_matmul(normed, d_pre_b)
        d_normed = d_normed + rounded(right_trans_product(d_pre_b, w_glu))
        gradient_list.append([grad_wglu, grad_bglu, grad_taps, grad_tbias, grad_gamma, grad_beta, grad_wconv])
    d_input, grad_scale, grad_offset = norm_back(resid, scaling, offset, d_normed)
    return (d_resid + d_input, gradient_list, [grad_scale, grad_offset, grad_bout])

def layer_forward(resid, parts, vectors, lengths, valid, table):
    resid_a, keep_a = feed_forward(resid, parts, 0, vectors[0], vectors[1], vectors[2])
    resid_b, keep_b = attention_forward(resid_a, parts, vectors[3], vectors[4], vectors[5], lengths, table)
    resid_c, keep_c = conv_forward(resid_b, parts, vectors[6], vectors[7], vectors[8], valid)
    resid_d, keep_d = feed_forward(resid_c, parts, 15, vectors[9], vectors[10], vectors[11])
    output = layer_norm(resid_d, vectors[12], vectors[13])
    return (output, (resid, resid_a, resid_b, resid_c, resid_d), (keep_a, keep_b, keep_c, keep_d))

def layer_back(d_output, parts, vectors, lengths, valid, table, resids, keeps):
    resid, resid_a, resid_b, resid_c, resid_d = resids
    d_resid_d, grad_fscale, grad_foffset = norm_back(resid_d, vectors[12], vectors[13], d_output)
    d_resid_c, grads_d, shared_d = feed_back(d_resid_d, resid_c, keeps[3], parts, 15, vectors[9], vectors[10])
    d_resid_b, grads_c, shared_c = conv_back(d_resid_c, resid_b, keeps[2], parts, vectors[6], vectors[7], valid)
    d_resid_a, grads_b, shared_b = attention_back(d_resid_b, resid_a, keeps[1], parts, vectors[3], vectors[4], lengths, table)
    d_resid, grads_a, shared_a = feed_back(d_resid_a, resid, keeps[0], parts, 0, vectors[0], vectors[1])
    part_grads = [grads_a[part_idx] + grads_b[part_idx] + grads_c[part_idx] + grads_d[part_idx] for part_idx in range(len(parts))]
    vector_grads = shared_a + shared_b + shared_c + shared_d + [grad_fscale, grad_foffset]
    return (d_resid, part_grads, vector_grads)

def adam_update(weights, first, second, gradient_list):
    first_new = BETA_ONE * first + (1.0 - BETA_ONE) * gradient_list
    second_new = BETA_TWO * second + (1.0 - BETA_TWO) * gradient_list * gradient_list
    first_hat = first_new / (1.0 - BETA_ONE ** STEP_COUNT)
    second_hat = second_new / (1.0 - BETA_TWO ** STEP_COUNT)
    weights_new = weights - LEARN_RATE * (first_hat / (jnp.sqrt(second_hat) + ADAM_EPS) + WEIGHT_DECAY * weights)
    return (weights_new, first_new, second_new)

def reference(tokens, lengths, cotangent, params, shared, first_moment, second_moment, first_shared, second_shared):
    part_count = params.shape[1]
    shapes = piece_shapes(D, FF // part_count, HEADS * HEAD_DIM // part_count, D // part_count, KERNEL)
    valid = (jnp.arange(SEQ_LEN)[None, :] < lengths[:, None]).astype(jnp.float32)
    table = position_table(SEQ_LEN, D)
    params_b = params.astype(jnp.bfloat16)
    shared_b = shared.astype(jnp.bfloat16)
    layer_weights = []
    for layer_idx in range(LAYERS):
        parts = [cast_pieces(split_pieces(params_b[layer_idx, part_idx], shapes)) for part_idx in range(part_count)]
        vectors = [shared_b[layer_idx, row_idx * D:(row_idx + 1) * D].astype(jnp.float32) for row_idx in range(14)]
        layer_weights.append((parts, vectors))
    resid = tokens.astype(jnp.float32)
    stores = []
    for layer_idx in range(LAYERS):
        parts, vectors = layer_weights[layer_idx]
        resid_next, resids, keeps = layer_forward(resid, parts, vectors, lengths, valid, table)
        stores.append((resids, keeps))
        resid = resid_next
    result = resid
    d_resid = cotangent
    half_list = []
    shared_list = []
    for layer_idx in reversed(range(LAYERS)):
        parts, vectors = layer_weights[layer_idx]
        resids, keeps = stores[layer_idx]
        d_resid, part_grads, vector_grads = layer_back(d_resid, parts, vectors, lengths, valid, table, resids, keeps)
        half_list.insert(0, jnp.stack([join_pieces(grads_one, PARAM_HALF) for grads_one in part_grads]))
        shared_list.insert(0, join_pieces(vector_grads, SHARED_LEN))
    grad_params = jnp.stack(half_list)
    grad_shared = jnp.stack(shared_list)
    new_params, new_first, new_second = adam_update(params, first_moment, second_moment, grad_params)
    new_shared, new_first_sh, new_second_sh = adam_update(shared, first_shared, second_shared, grad_shared)
    return (result, d_resid, grad_params, grad_shared, new_params, new_shared, new_first, new_second, new_first_sh, new_second_sh)
```

```python
from functools import partial
import math

import jax
import jax.numpy as jnp
from jax import lax
from jax.experimental import pallas as pl
from jax.experimental.pallas import tpu as pltpu
from jax.sharding import PartitionSpec as P


D = 512
FF = 2048
HEADS = 8
HEAD_DIM = 64
KERNEL = 31
SEQ_LEN = 128
LAYERS = 1


NORM_EPS = 1e-05
BATCH_EPS = 1e-05
LEARN_RATE = 0.02
BETA_ONE = 0.9
BETA_TWO = 0.999
ADAM_EPS = 1e-08
WEIGHT_DECAY = 0.1
STEP_COUNT = 5
FLOAT_PIECES = (1, 6, 7, 9, 10, 11, 12, 13, 16)

LANES = 128
TILE = 16 * LANES
SHARED_ROWS = 16
BF16 = jnp.bfloat16
F32 = jnp.float32
ANY = pl.BlockSpec(memory_space=pl.ANY)
VMEM = pl.BlockSpec(memory_space=pltpu.VMEM)
SMEM = pl.BlockSpec(memory_space=pltpu.SMEM)


def round_up(value, multiple):
    return -(-value // multiple) * multiple


class Plan:
    def __init__(self, count, shard, shared_shard, shapes):
        self.count = count
        self.shard = shard
        self.shared_shard = shared_shard
        self.shapes = shapes
        self.rows_in = round_up(shard // LANES + 2, 8)
        self.rows = round_up(self.rows_in + 16, 16)
        self.block = self.rows + SHARED_ROWS
        self.flat_rows = count * shard // LANES
        self.alloc_rows = round_up(((count - 1) * shard // TILE) * 16 + self.rows, 16)
        self.shared_rows = count * shared_shard // LANES
        self.bases = []
        at = 0
        for shape in shapes:
            self.bases.append(at // LANES)
            at += math.prod(shape)


def as_matrix(shape):
    return shape if len(shape) == 2 else (1, shape[0])


def shift_body(where_ref, x_ref, s_ref, o_ref, scr):
    low, row, low_shared = where_ref[0], where_ref[1], where_ref[2]
    rows_in, rows = x_ref.shape[0], scr.shape[0]
    lane = lax.broadcasted_iota(jnp.int32, (rows_in, LANES), 1)
    scr[...] = jnp.zeros_like(scr)
    rolled = pltpu.roll(x_ref[...], low, 1)
    scr[pl.ds(row, rows_in), :] = jnp.where(lane >= low, rolled, 0.0)
    scr[pl.ds(row + 1, rows_in), :] += jnp.where(lane < low, rolled, 0.0)
    o_ref[0:rows, :] = scr[...].astype(BF16)
    lane = lax.broadcasted_iota(jnp.int32, (8, LANES), 1)
    rolled = pltpu.roll(s_ref[...], low_shared, 1)
    scr[0:16, :] = jnp.zeros((16, LANES), F32)
    scr[0:8, :] = jnp.where(lane >= low_shared, rolled, 0.0)
    scr[1:9, :] += jnp.where(lane < low_shared, rolled, 0.0)
    o_ref[rows : rows + 16, :] = scr[0:16, :].astype(BF16)


def shift_out(plan, where, flat, shared):
    padded = jnp.pad(flat, (0, plan.rows_in * LANES - plan.shard)).reshape(-1, LANES)
    padded_shared = jnp.pad(shared, (0, 8 * LANES - plan.shared_shard)).reshape(8, LANES)
    return pl.pallas_call(
        shift_body,
        out_shape=jax.ShapeDtypeStruct((plan.block, LANES), BF16),
        in_specs=[SMEM, VMEM, VMEM],
        out_specs=VMEM,
        scratch_shapes=[pltpu.VMEM((plan.rows, LANES), F32)],
        name="shift_out",
    )(where, padded, padded_shared)


def unshift_body(where_ref, g_ref, o_ref, s_ref):
    low, row, low_shared = where_ref[0], where_ref[1], where_ref[2]
    rows_in = o_ref.shape[0]
    rows = g_ref.shape[0] - SHARED_ROWS
    lane = lax.broadcasted_iota(jnp.int32, (rows_in, LANES), 1)
    back = lax.rem(LANES - low, LANES)
    first = pltpu.roll(g_ref[pl.ds(row, rows_in), :], back, 1)
    second = pltpu.roll(g_ref[pl.ds(row + 1, rows_in), :], back, 1)
    o_ref[...] = jnp.where(lane < LANES - low, first, second)
    lane = lax.broadcasted_iota(jnp.int32, (8, LANES), 1)
    back = lax.rem(LANES - low_shared, LANES)
    first = pltpu.roll(g_ref[rows : rows + 8, :], back, 1)
    second = pltpu.roll(g_ref[rows + 1 : rows + 9, :], back, 1)
    s_ref[...] = jnp.where(lane < LANES - low_shared, first, second)


def unshift_in(plan, where, block):
    rows, shared = pl.pallas_call(
        unshift_body,
        out_shape=(
            jax.ShapeDtypeStruct((plan.rows_in, LANES), F32),
            jax.ShapeDtypeStruct((8, LANES), F32),
        ),
        in_specs=[SMEM, VMEM],
        out_specs=(VMEM, VMEM),
        name="unshift_in",
    )(where, block)
    return rows.reshape(-1)[: plan.shard], shared.reshape(-1)[: plan.shared_shard]


def chunked(total, width):
    step = total
    while step > 128 and step % 2 == 0:
        step //= 2
    return step


def unpack_body(plan, n_in, idx_ref, *refs):
    ins = refs[:n_in]
    outs = refs[n_in : n_in + len(plan.shapes) + 1]
    stk, flat, shf, sem = refs[n_in + len(plan.shapes) + 1 :]
    copies = []
    for at in range(plan.count):
        src = ins[at] if n_in > 1 else ins[0].at[at]
        copies.append(pltpu.make_async_copy(src, stk.at[idx_ref[at]], sem.at[at]))
    for copy in copies:
        copy.start()
    for copy in copies:
        copy.wait()
    flat[0:16, :] = jnp.zeros((16, LANES), F32)
    shf[...] = jnp.zeros_like(shf)

    def place(at, carry):
        start = pl.multiple_of((at * plan.shard) // TILE * 16, 16)
        flat[pl.ds(start, 16), :] += stk[at, 0:16, :].astype(F32)
        flat[pl.ds(start + 16, plan.rows - 16), :] = stk[at, 16 : plan.rows, :].astype(F32)
        return carry

    lax.fori_loop(0, plan.count, place, 0)
    for at in range(plan.count):
        base = at * plan.shared_shard // LANES
        shf[base : base + 16, :] += stk[at, plan.rows : plan.rows + 16, :].astype(F32)
    for shape, base, out in zip(plan.shapes, plan.bases, outs):
        rows, width = as_matrix(shape)
        cols = width // LANES
        step = chunked(rows, cols)
        for col in range(cols):
            if step == rows:
                if rows == 1:
                    part = flat[base + col : base + col + 1, :]
                else:
                    part = flat[pl.ds(base + col, rows, stride=cols), :]
                out[:, col * LANES : (col + 1) * LANES] = part.astype(out.dtype)
            else:

                def move(k, carry, col=col, base=base, cols=cols, step=step, out=out):
                    at = pl.multiple_of(k * (step * cols), 8) + (base + col)
                    part = flat[pl.ds(at, step, stride=cols), :]
                    to = pl.multiple_of(k * step, step)
                    out[pl.ds(to, step), col * LANES : (col + 1) * LANES] = part.astype(out.dtype)
                    return carry

                lax.fori_loop(0, rows // step, move, 0)
    shared_out = outs[-1]
    cols = D // LANES
    for col in range(cols):
        shared_out[:, col * LANES : (col + 1) * LANES] = shf[
            pl.ds(col, shared_out.shape[0], stride=cols), :
        ]


def unpack(plan, idx, blocks):
    outs = [
        jax.ShapeDtypeStruct(as_matrix(shape), F32 if at in FLOAT_PIECES else BF16)
        for at, shape in enumerate(plan.shapes)
    ]
    outs.append(jax.ShapeDtypeStruct((14, D), F32))
    return pl.pallas_call(
        partial(unpack_body, plan, len(blocks)),
        out_shape=outs,
        in_specs=[SMEM] + [ANY] * len(blocks),
        out_specs=[VMEM] * len(outs),
        scratch_shapes=[
            pltpu.VMEM((plan.count, plan.block, LANES), BF16),
            pltpu.VMEM((plan.alloc_rows, LANES), F32),
            pltpu.VMEM((plan.shared_rows + 16, LANES), F32),
            pltpu.SemaphoreType.DMA((plan.count,)),
        ],
        name="unpack",
    )(idx, *blocks)


def pack_body(plan, idx_ref, *refs):
    n_in = len(plan.shapes) + 1
    ins = refs[:n_in]
    outs = refs[n_in : n_in + plan.count]
    stk, flat, shf, sem = refs[n_in + plan.count :]
    tail = plan.flat_rows // 8 * 8
    flat[tail:, :] = jnp.zeros((plan.alloc_rows - tail, LANES), F32)
    for shape, base, src in zip(plan.shapes, plan.bases, ins):
        rows, width = as_matrix(shape)
        cols = width // LANES
        step = chunked(rows, cols)
        for col in range(cols):
            if step == rows:
                part = src[:, col * LANES : (col + 1) * LANES].astype(F32)
                if rows == 1:
                    flat[base + col : base + col + 1, :] = part
                else:
                    flat[pl.ds(base + col, rows, stride=cols), :] = part
            else:

                def move(k, carry, col=col, base=base, cols=cols, step=step, src=src):
                    at = pl.multiple_of(k * (step * cols), 8) + (base + col)
                    frm = pl.multiple_of(k * step, step)
                    flat[pl.ds(at, step, stride=cols), :] = src[
                        pl.ds(frm, step), col * LANES : (col + 1) * LANES
                    ].astype(F32)
                    return carry

                lax.fori_loop(0, rows // step, move, 0)
    shf[...] = jnp.zeros_like(shf)
    cols = D // LANES
    for col in range(cols):
        shf[pl.ds(col, 14, stride=cols), :] = ins[-1][:, col * LANES : (col + 1) * LANES]

    def place(at, carry):
        start = pl.multiple_of((at * plan.shard) // TILE * 16, 16)
        stk[at, 0 : plan.rows, :] = flat[pl.ds(start, plan.rows), :].astype(BF16)
        return carry

    lax.fori_loop(0, plan.count, place, 0)
    for at in range(plan.count):
        base = at * plan.shared_shard // LANES
        stk[at, plan.rows : plan.rows + 16, :] = shf[base : base + 16, :].astype(BF16)
    copies = [
        pltpu.make_async_copy(stk.at[idx_ref[at]], outs[at], sem.at[at])
        for at in range(plan.count)
    ]
    for copy in copies:
        copy.start()
    for copy in copies:
        copy.wait()


def pack(plan, idx, piece_grads, shared_grad):
    pieces = [grad.reshape(as_matrix(shape)) for grad, shape in zip(piece_grads, plan.shapes)]
    block = jax.ShapeDtypeStruct((plan.block, LANES), BF16)
    return pl.pallas_call(
        partial(pack_body, plan),
        out_shape=[block] * plan.count,
        in_specs=[SMEM] + [VMEM] * (len(pieces) + 1),
        out_specs=[ANY] * plan.count,
        scratch_shapes=[
            pltpu.VMEM((plan.count, plan.block, LANES), BF16),
            pltpu.VMEM((plan.alloc_rows, LANES), F32),
            pltpu.VMEM((plan.shared_rows + 16, LANES), F32),
            pltpu.SemaphoreType.DMA((plan.count,)),
        ],
        compiler_params=pltpu.CompilerParams(vmem_limit_bytes=60 * 1024 * 1024),
        name="pack",
    )(idx, *pieces, shared_grad)


def permute(value, count, target, axis="dp"):
    return lax.ppermute(value, axis, [(at, target(at)) for at in range(count)])


def z_next(at):
    return (at + 4) % 16


def block_order(count):
    me = lax.axis_index("dp")
    if count != 16:
        return jnp.arange(count, dtype=jnp.int32)
    z, x, core = me // 4, (me // 2) % 2, me % 2
    order = []
    for back in range(4):
        for flip_x in range(2):
            for flip_core in range(2):
                order.append(
                    ((z + 4 - back) % 4) * 4 + (x ^ flip_x) * 2 + (core ^ flip_core)
                )
    return jnp.stack(order).astype(jnp.int32)


def gather_blocks(count, own):
    if count != 16:
        return [lax.all_gather(own, "dp", axis=0)]
    blocks = []
    current = own
    for back in range(4):
        other = permute(current, 16, lambda at: at ^ 2)
        upcoming = permute(current, 16, z_next) if back < 3 else None
        for block in (current, other):
            blocks.append(block)
            blocks.append(permute(block, 16, lambda at: at ^ 1))
        current = upcoming
    return blocks


def add_blocks(first, second):
    return (first.astype(F32) + second.astype(F32)).astype(BF16)


def scatter_blocks(count, blocks):
    if count != 16:
        return lax.psum_scatter(
            jnp.stack(blocks).astype(F32), "dp", scatter_dimension=0, tiled=False
        )
    running = None
    for back in (1, 2, 3, 0):
        halves = []
        for flip_x in (1, 0):
            keep, send = blocks[back * 4 + flip_x * 2], blocks[back * 4 + flip_x * 2 + 1]
            halves.append(add_blocks(keep, permute(send, 16, lambda at: at ^ 1)))
        column = add_blocks(halves[1], permute(halves[0], 16, lambda at: at ^ 2))
        if running is None:
            running = column
        else:
            arrived = permute(running, 16, z_next)
            if back == 0:
                return column.astype(F32) + arrived.astype(F32)
            running = add_blocks(column, arrived)


def dp_sum(value):
    count = lax.axis_size("dp")
    bit = 1
    while bit < count:
        steps = [bit, 2 * bit, 3 * bit] if 4 * bit <= count else [bit]
        parts = [permute(value, count, lambda at, step=step: at ^ step) for step in steps]
        value = sum(parts, value)
        bit *= 4 if len(steps) == 3 else 2
    return value


def tensor_total(partial_sum):
    own = partial_sum.astype(BF16)
    other = permute(own, lax.axis_size("tensor"), lambda at: at ^ 1, "tensor")
    return own.astype(F32) + other.astype(F32)


tensor_back_total = tensor_total


def mat_product(left, right):
    return jnp.dot(left, right, preferred_element_type=jnp.float32)


def left_transposed_matmul(left, right):
    return lax.dot_general(
        left, right, (((0,), (0,)), ((), ())), preferred_element_type=jnp.float32
    )


def right_trans_product(left, right):
    return lax.dot_general(
        left, right, (((1,), (1,)), ((), ())), preferred_element_type=jnp.float32
    )


def layer_norm(values, scaling, offset):
    centred = values - jnp.mean(values, axis=-1, keepdims=True)
    spread = jnp.mean(centred * centred, axis=-1, keepdims=True)
    return centred * lax.rsqrt(spread + NORM_EPS) * (1.0 + scaling) + offset


def norm_back(values, scaling, offset, d_output):
    primal_out, pull_back = jax.vjp(layer_norm, values, scaling, offset)
    return pull_back(d_output)


def silu_slope(values):
    sigma_vals = jax.nn.sigmoid(values)
    return sigma_vals * (1.0 + values * (1.0 - sigma_vals))


def position_table(seq_len, model_width):
    distance = (seq_len - 1 - jnp.arange(2 * seq_len - 1)).astype(jnp.float32)
    freq_index = jnp.arange(model_width // 2).astype(jnp.float32)
    rates = jnp.exp(freq_index * (-2.0 * math.log(10000.0) / model_width))
    angles = distance[:, None] * rates[None, :]
    table = jnp.stack([jnp.sin(angles), jnp.cos(angles)], axis=-1)
    return table.reshape(2 * seq_len - 1, model_width).astype(jnp.bfloat16)


def piece_shapes(model_width, ff_part, att_part, chan_part, kernel_len):
    feed_list = [(model_width, ff_part), (ff_part,), (ff_part, model_width)]
    attn_list = [
        (model_width, 3 * att_part),
        (model_width, att_part),
        (att_part, model_width),
        (att_part,),
        (att_part,),
    ]
    conv_list = [
        (model_width, 2 * chan_part),
        (2 * chan_part,),
        (kernel_len, chan_part),
        (chan_part,),
        (chan_part,),
        (chan_part,),
        (chan_part, model_width),
    ]
    return feed_list + attn_list + conv_list + feed_list


def rel_shift(position):
    leading = position.shape[:-2]
    seq_len = position.shape[-2]
    span_len = position.shape[-1]
    padded = jnp.pad(position, [(0, 0)] * len(leading) + [(0, 0), (0, 1)])
    flattened = padded.reshape(leading + (seq_len * (span_len + 1),))
    flattened = flattened[..., seq_len - 1 : seq_len - 1 + seq_len * span_len]
    return flattened.reshape(leading + (seq_len, span_len))[..., :seq_len]


def rel_unshift(grad_shifted):
    leading = grad_shifted.shape[:-2]
    seq_len = grad_shifted.shape[-1]
    span_len = 2 * seq_len - 1
    widened = jnp.pad(grad_shifted, [(0, 0)] * len(leading) + [(0, 0), (0, span_len - seq_len)])
    flattened = widened.reshape(leading + (seq_len * span_len,))
    flattened = jnp.pad(flattened, [(0, 0)] * len(leading) + [(seq_len - 1, 1)])
    return flattened.reshape(leading + (seq_len, span_len + 1))[..., :span_len]


def attention_scores(query_u, query_v, keys_b, pos_rows):
    content = jnp.einsum("bihd,bjhd->bhij", query_u, keys_b, preferred_element_type=jnp.float32)
    position = jnp.einsum("bihd,rhd->bhir", query_v, pos_rows, preferred_element_type=jnp.float32)
    return (content + rel_shift(position)) * (1.0 / math.sqrt(query_u.shape[-1]))


def key_mask(seq_lengths):
    return (jnp.arange(SEQ_LEN)[None, :] < seq_lengths[:, None])[:, None, None, :]


def conv_front(valid, pre_glu, tap_weights, tap_bias):
    chan_part = pre_glu.shape[-1] // 2
    gated = pre_glu[..., :chan_part] * jax.nn.sigmoid(pre_glu[..., chan_part:]) * valid[..., None]
    kernel_len = tap_weights.shape[0]
    margin = (kernel_len - 1) // 2
    filters = tap_weights.reshape(kernel_len, 1, chan_part)
    summed = lax.conv_general_dilated(
        gated,
        filters,
        (1,),
        [(margin, kernel_len - 1 - margin)],
        dimension_numbers=("NWC", "WIO", "NWC"),
        feature_group_count=chan_part,
        precision=lax.Precision.HIGHEST,
    )
    return summed + tap_bias


def batch_apply(conv_out, gamma_vec, beta_vec, mean_vec, inv_std):
    return jax.nn.silu((conv_out - mean_vec) * inv_std * (1.0 + gamma_vec) + beta_vec)


def feed_forward(resid, w_in, b_in, w_out, scaling, offset, b_out):
    normed = layer_norm(resid, scaling, offset).astype(jnp.bfloat16)
    hidden_pre = mat_product(normed, w_in) + b_in
    hidden = jax.nn.silu(hidden_pre).astype(jnp.bfloat16)
    branch = tensor_total(mat_product(hidden, w_out)) + b_out
    return (resid + 0.5 * branch, (normed, hidden_pre, hidden))


def feed_back(d_resid, resid, saved, w_in, w_out, scaling, offset):
    normed, hidden_pre, hidden = saved
    d_branch = 0.5 * d_resid
    grad_bout = jnp.sum(d_branch, axis=0)
    branch_gradient_second = d_branch.astype(jnp.bfloat16)
    grad_wout = left_transposed_matmul(hidden, branch_gradient_second)
    d_pre = right_trans_product(branch_gradient_second, w_out) * silu_slope(hidden_pre)
    grad_bin = jnp.sum(d_pre, axis=0)
    d_pre_b = d_pre.astype(jnp.bfloat16)
    grad_win = left_transposed_matmul(normed, d_pre_b)
    d_normed = tensor_back_total(right_trans_product(d_pre_b, w_in))
    d_input, grad_scale, grad_offset = norm_back(resid, scaling, offset, d_normed)
    return (
        d_resid + d_input,
        [grad_win, grad_bin, grad_wout],
        [grad_scale, grad_offset, grad_bout],
    )


def attention_forward(resid, weights, scaling, offset, b_out, lengths, table):
    w_qkv, w_pos, w_att, bias_u, bias_v = weights
    seq_count = lengths.shape[0]
    att_part = w_att.shape[0]
    head_count = att_part // HEAD_DIM

    def to_heads(block):
        return block.reshape(seq_count, SEQ_LEN, head_count, HEAD_DIM)

    normed = layer_norm(resid, scaling, offset).astype(jnp.bfloat16)
    qkv_rows = mat_product(normed, w_qkv)
    query = qkv_rows[:, :att_part]
    query_u = to_heads((query + bias_u).astype(jnp.bfloat16))
    query_v = to_heads((query + bias_v).astype(jnp.bfloat16))
    keys_b = to_heads(qkv_rows[:, att_part : 2 * att_part].astype(jnp.bfloat16))
    values_b = to_heads(qkv_rows[:, 2 * att_part :].astype(jnp.bfloat16))
    pos_rows = (
        mat_product(table, w_pos)
        .astype(jnp.bfloat16)
        .reshape(2 * SEQ_LEN - 1, head_count, HEAD_DIM)
    )
    scores = attention_scores(query_u, query_v, keys_b, pos_rows)
    exponent = jnp.where(key_mask(lengths), jnp.exp(scores), 0.0)
    totals = jnp.sum(exponent, axis=-1)
    log_total = jnp.log(totals)
    probs = (exponent / totals[..., None]).astype(jnp.bfloat16)
    context = jnp.einsum("bhij,bjhd->bihd", probs, values_b, preferred_element_type=jnp.float32)
    context_rows_second = context.reshape(seq_count * SEQ_LEN, att_part).astype(jnp.bfloat16)
    branch = tensor_total(mat_product(context_rows_second, w_att)) + b_out
    return (
        resid + branch,
        (normed, query_u, query_v, keys_b, values_b, pos_rows, log_total, context_rows_second),
    )


def attention_back(d_resid, resid, saved, weights, scaling, offset, lengths, table):
    normed, query_u, query_v, keys_b, values_b, pos_rows, log_total, context_rows_second = saved
    w_qkv, w_pos, w_att, bias_u, bias_v = weights
    seq_count = lengths.shape[0]
    att_part = w_att.shape[0]
    rows_total = seq_count * SEQ_LEN
    scale = 1.0 / math.sqrt(HEAD_DIM)
    grad_bout = jnp.sum(d_resid, axis=0)
    branch_gradient_second = d_resid.astype(jnp.bfloat16)
    attention_weight_gradient = left_transposed_matmul(context_rows_second, branch_gradient_second)
    d_context = (
        right_trans_product(branch_gradient_second, w_att)
        .astype(jnp.bfloat16)
        .reshape(query_u.shape)
    )
    scores = attention_scores(query_u, query_v, keys_b, pos_rows)
    probs = jnp.where(key_mask(lengths), jnp.exp(scores - log_total[..., None]), 0.0)
    probs_b = probs.astype(jnp.bfloat16)
    d_values = jnp.einsum("bhij,bihd->bjhd", probs_b, d_context, preferred_element_type=jnp.float32)
    d_probs = jnp.einsum("bihd,bjhd->bhij", d_context, values_b, preferred_element_type=jnp.float32)
    row_dot = jnp.sum(probs * d_probs, axis=-1, keepdims=True)
    d_scores = (probs * (d_probs - row_dot) * scale).astype(jnp.bfloat16)
    d_query_u = jnp.einsum("bhij,bjhd->bihd", d_scores, keys_b, preferred_element_type=jnp.float32)
    d_keys = jnp.einsum("bhij,bihd->bjhd", d_scores, query_u, preferred_element_type=jnp.float32)
    d_position = rel_unshift(d_scores)
    d_query_v = jnp.einsum(
        "bhir,rhd->bihd", d_position, pos_rows, preferred_element_type=jnp.float32
    )
    d_pos_rows = jnp.einsum(
        "bhir,bihd->rhd", d_position, query_v, preferred_element_type=jnp.float32
    )
    content_bias_gradient = jnp.sum(d_query_u, axis=(0, 1)).reshape(att_part)
    position_bias_gradient = jnp.sum(d_query_v, axis=(0, 1)).reshape(att_part)
    d_query = (d_query_u + d_query_v).reshape(rows_total, att_part)
    d_qkv = jnp.concatenate(
        [d_query, d_keys.reshape(rows_total, att_part), d_values.reshape(rows_total, att_part)],
        axis=1,
    ).astype(jnp.bfloat16)
    query_key_value_weight_gradient = left_transposed_matmul(normed, d_qkv)
    position_weight_gradient = lax.dot_general(
        table.astype(jnp.float32),
        d_pos_rows.reshape(2 * SEQ_LEN - 1, att_part),
        (((0,), (0,)), ((), ())),
        precision=lax.Precision.HIGHEST,
    )
    d_normed = tensor_back_total(right_trans_product(d_qkv, w_qkv))
    d_input, grad_scale, grad_offset = norm_back(resid, scaling, offset, d_normed)
    return (
        d_resid + d_input,
        [
            query_key_value_weight_gradient,
            position_weight_gradient,
            attention_weight_gradient,
            content_bias_gradient,
            position_bias_gradient,
        ],
        [grad_scale, grad_offset, grad_bout],
    )


def conv_forward(resid, weights, scaling, offset, b_out, valid):
    w_glu, b_glu, tap_weights, tap_bias, gamma_vec, beta_vec, w_conv = weights
    seq_count = valid.shape[0]
    chan_part = w_conv.shape[0]
    normed = layer_norm(resid, scaling, offset).astype(jnp.bfloat16)
    pre_glu = (mat_product(normed, w_glu) + b_glu).reshape(seq_count, SEQ_LEN, 2 * chan_part)
    conv_out = conv_front(valid, pre_glu, tap_weights, tap_bias)
    masked = conv_out * valid[..., None]
    stats = dp_sum(
        jnp.stack(
            [
                jnp.sum(masked, axis=(0, 1)),
                jnp.sum(masked * conv_out, axis=(0, 1)),
                jnp.broadcast_to(jnp.sum(valid), (chan_part,)),
            ]
        )
    )
    first_sum, square_sum, count_all = stats[0], stats[1], stats[2]
    mean_vec = first_sum / count_all
    inv_std = lax.rsqrt(square_sum / count_all - mean_vec * mean_vec + BATCH_EPS)
    activated = (
        batch_apply(conv_out, gamma_vec, beta_vec, mean_vec, inv_std)
        .reshape(seq_count * SEQ_LEN, chan_part)
        .astype(jnp.bfloat16)
    )
    branch = tensor_total(mat_product(activated, w_conv)) + b_out
    return (resid + branch, (normed, pre_glu, conv_out, mean_vec, inv_std, count_all, activated))


def conv_back(d_resid, resid, saved, weights, scaling, offset, valid):
    normed, pre_glu, conv_out, mean_vec, inv_std, count_all, activated = saved
    w_glu, b_glu, tap_weights, tap_bias, gamma_vec, beta_vec, w_conv = weights
    grad_bout = jnp.sum(d_resid, axis=0)
    branch_gradient_second = d_resid.astype(jnp.bfloat16)
    grad_wconv = left_transposed_matmul(activated, branch_gradient_second)
    d_act = right_trans_product(branch_gradient_second, w_conv).reshape(conv_out.shape)
    primal_out, pull_norm = jax.vjp(batch_apply, conv_out, gamma_vec, beta_vec, mean_vec, inv_std)
    d_conv, grad_gamma, grad_beta, d_mean, d_inv = pull_norm(d_act)
    sums = dp_sum(jnp.stack([d_mean, d_inv]))
    d_mean, d_inv = sums[0], sums[1]
    d_var = -0.5 * inv_std * inv_std * inv_std * d_inv
    d_first = (d_mean - 2.0 * mean_vec * d_var) / count_all
    d_square = d_var / count_all
    d_conv = d_conv + valid[..., None] * (d_first + 2.0 * conv_out * d_square)
    primal_two, pull_front = jax.vjp(partial(conv_front, valid), pre_glu, tap_weights, tap_bias)
    d_pre, grad_taps, grad_tbias = pull_front(d_conv)
    d_pre = d_pre.reshape(-1, d_pre.shape[-1])
    grad_bglu = jnp.sum(d_pre, axis=0)
    d_pre_b = d_pre.astype(jnp.bfloat16)
    grad_wglu = left_transposed_matmul(normed, d_pre_b)
    d_normed = tensor_back_total(right_trans_product(d_pre_b, w_glu))
    d_input, grad_scale, grad_offset = norm_back(resid, scaling, offset, d_normed)
    return (
        d_resid + d_input,
        [grad_wglu, grad_bglu, grad_taps, grad_tbias, grad_gamma, grad_beta, grad_wconv],
        [grad_scale, grad_offset, grad_bout],
    )


def layer_forward(resid, pieces, vectors, lengths, valid, table):
    resid_a, keep_a = feed_forward(
        resid, pieces[0], pieces[1], pieces[2], vectors[0], vectors[1], vectors[2]
    )
    resid_b, keep_b = attention_forward(
        resid_a, pieces[3:8], vectors[3], vectors[4], vectors[5], lengths, table
    )
    resid_c, keep_c = conv_forward(resid_b, pieces[8:15], vectors[6], vectors[7], vectors[8], valid)
    resid_d, keep_d = feed_forward(
        resid_c, pieces[15], pieces[16], pieces[17], vectors[9], vectors[10], vectors[11]
    )
    output = layer_norm(resid_d, vectors[12], vectors[13])
    return (output, (resid, resid_a, resid_b, resid_c, resid_d), (keep_a, keep_b, keep_c, keep_d))


def layer_back(d_output, pieces, vectors, lengths, valid, table, resids, keeps):
    resid, resid_a, resid_b, resid_c, resid_d = resids
    d_resid_d, grad_fscale, grad_foffset = norm_back(resid_d, vectors[12], vectors[13], d_output)
    d_resid_c, grads_d, shared_d = feed_back(
        d_resid_d, resid_c, keeps[3], pieces[15], pieces[17], vectors[9], vectors[10]
    )
    d_resid_b, grads_c, shared_c = conv_back(
        d_resid_c, resid_b, keeps[2], pieces[8:15], vectors[6], vectors[7], valid
    )
    d_resid_a, grads_b, shared_b = attention_back(
        d_resid_b, resid_a, keeps[1], pieces[3:8], vectors[3], vectors[4], lengths, table
    )
    d_resid, grads_a, shared_a = feed_back(
        d_resid_a, resid, keeps[0], pieces[0], pieces[2], vectors[0], vectors[1]
    )
    piece_grads = grads_a + grads_b + grads_c + grads_d
    vector_grads = shared_a + shared_b + shared_c + shared_d + [grad_fscale, grad_foffset]
    return (d_resid, piece_grads, vector_grads)


def adam_update(weights, first, second, gradient_list):
    first_new = BETA_ONE * first + (1.0 - BETA_ONE) * gradient_list
    second_new = BETA_TWO * second + (1.0 - BETA_TWO) * gradient_list * gradient_list
    first_hat = first_new / (1.0 - BETA_ONE**STEP_COUNT)
    second_hat = second_new / (1.0 - BETA_TWO**STEP_COUNT)
    weights_new = weights - LEARN_RATE * (
        first_hat / (jnp.sqrt(second_hat) + ADAM_EPS) + WEIGHT_DECAY * weights
    )
    return (weights_new, first_new, second_new)


def local(
    tokens,
    lengths,
    cotangent,
    params,
    shared,
    first_moment,
    second_moment,
    first_shared,
    second_shared,
):
    part_count = lax.axis_size("tensor")
    shapes = piece_shapes(
        D, FF // part_count, HEADS * HEAD_DIM // part_count, D // part_count, KERNEL
    )
    count = lax.axis_size("dp")
    plan = Plan(count, params.shape[2], shared.shape[1], shapes)
    me = lax.axis_index("dp")
    start = me * plan.shard % TILE
    where = jnp.stack([start % LANES, start // LANES, me * plan.shared_shard % LANES]).astype(
        jnp.int32
    )
    order = block_order(count)
    own = shift_out(plan, where, params.reshape(-1), shared.reshape(-1))
    unpacked = unpack(plan, order, gather_blocks(count, own))
    pieces = [piece.reshape(shape) for piece, shape in zip(unpacked[:-1], shapes)]
    vectors = [unpacked[-1][at] for at in range(14)]
    valid = (jnp.arange(SEQ_LEN)[None, :] < lengths[:, None]).astype(F32)
    table = position_table(SEQ_LEN, D)
    resid = tokens.astype(F32)
    result, resids, keeps = layer_forward(resid, pieces, vectors, lengths, valid, table)
    d_resid, piece_grads, vector_grads = layer_back(
        cotangent, pieces, vectors, lengths, valid, table, resids, keeps
    )
    blocks = pack(plan, order, piece_grads, jnp.stack(vector_grads))
    grad_flat, grad_shared = unshift_in(plan, where, scatter_blocks(count, blocks))
    grad_params = grad_flat.reshape(params.shape)
    grad_shared = grad_shared.reshape(shared.shape)
    new_params, new_first, new_second = adam_update(
        params, first_moment, second_moment, grad_params
    )
    new_shared, new_first_sh, new_second_sh = adam_update(
        shared, first_shared, second_shared, grad_shared
    )
    return (
        result,
        d_resid,
        grad_params,
        grad_shared,
        new_params,
        new_shared,
        new_first,
        new_second,
        new_first_sh,
        new_second_sh,
    )


def solution(mesh):
    in_specs = (
        P("dp", None),
        P("dp"),
        P("dp", None),
        P(None, "tensor", "dp"),
        P(None, "dp"),
        P(None, "tensor", "dp"),
        P(None, "tensor", "dp"),
        P(None, "dp"),
        P(None, "dp"),
    )
    out_specs = (
        P("dp", None),
        P("dp", None),
        P(None, "tensor", "dp"),
        P(None, "dp"),
        P(None, "tensor", "dp"),
        P(None, "dp"),
        P(None, "tensor", "dp"),
        P(None, "tensor", "dp"),
        P(None, "dp"),
        P(None, "dp"),
    )
    return jax.shard_map(local, mesh=mesh, in_specs=in_specs, out_specs=out_specs, check_vma=False)
```

```python
from functools import partial
import math

import jax
import jax.numpy as jnp
from jax import lax
from jax.experimental import pallas as pl
from jax.experimental.pallas import tpu as pltpu
from jax.sharding import PartitionSpec as P


D = 512
FF = 2048
HEADS = 8
HEAD_DIM = 64
KERNEL = 31
SEQ_LEN = 128
LAYERS = 1


NORM_EPS = 1e-05
BATCH_EPS = 1e-05
LEARN_RATE = 0.02
BETA_ONE = 0.9
BETA_TWO = 0.999
ADAM_EPS = 1e-08
WEIGHT_DECAY = 0.1
STEP_COUNT = 5
FLOAT_PIECES = (1, 6, 7, 9, 10, 11, 12, 13, 16)

LANES = 128
TILE = 16 * LANES
SHARED_ROWS = 16
BF16 = jnp.bfloat16
F32 = jnp.float32
ANY = pl.BlockSpec(memory_space=pl.ANY)
VMEM = pl.BlockSpec(memory_space=pltpu.VMEM)
SMEM = pl.BlockSpec(memory_space=pltpu.SMEM)


def round_up(value, multiple):
    return -(-value // multiple) * multiple


class Plan:
    def __init__(self, count, shard, shared_shard, shapes):
        self.count = count
        self.shard = shard
        self.shared_shard = shared_shard
        self.shapes = shapes
        self.rows_in = round_up(shard // LANES + 2, 8)
        self.rows = round_up(self.rows_in + 16, 16)
        self.block = self.rows + SHARED_ROWS
        self.flat_rows = count * shard // LANES
        self.alloc_rows = round_up(((count - 1) * shard // TILE) * 16 + self.rows, 16)
        self.shared_rows = count * shared_shard // LANES
        self.bases = []
        at = 0
        for shape in shapes:
            self.bases.append(at // LANES)
            at += math.prod(shape)


def as_matrix(shape):
    return shape if len(shape) == 2 else (1, shape[0])


def split_flat(length):
    return [
        (at // LANES, slice(at, min(at + LANES, length)), min(LANES, length - at))
        for at in range(0, length, LANES)
    ]


def shift_body(plan, where_ref, x_ref, s_ref, o_ref, rows_scr, scr):
    low, row, low_shared = where_ref[0], where_ref[1], where_ref[2]
    rows_in, rows = plan.rows_in, plan.rows
    whole = plan.shard // 1024

    def load(at, carry):
        part = x_ref[0, :, pl.ds(pl.multiple_of(at * 1024, 1024), 1024)]
        rows_scr[pl.ds(pl.multiple_of(at * 8, 8), 8), :] = part.reshape(8, LANES)
        return carry

    lax.fori_loop(0, whole, load, 0, unroll=4)
    rows_scr[whole * 8 :, :] = jnp.zeros((rows_in - whole * 8, LANES), F32)
    for at, cols, lanes in split_flat(plan.shard):
        if at >= whole * 8:
            rows_scr[at : at + 1, 0:lanes] = x_ref[0, :, cols]
    scr[rows - 32 :, :] = jnp.zeros((32, LANES), F32)
    scr[0:16, :] = jnp.zeros((16, LANES), F32)
    lane = lax.broadcasted_iota(jnp.int32, (rows_in, LANES), 1)
    rolled = pltpu.roll(rows_scr[...], low, 1)
    scr[pl.ds(row, rows_in), :] = jnp.where(lane >= low, rolled, 0.0)
    scr[pl.ds(row + rows_in, 1), :] = jnp.zeros((1, LANES), F32)
    scr[pl.ds(row + 1, rows_in), :] += jnp.where(lane < low, rolled, 0.0)
    o_ref[0:rows, :] = scr[...].astype(BF16)
    rows_scr[0:8, :] = jnp.zeros((8, LANES), F32)
    for at, cols, lanes in split_flat(plan.shared_shard):
        rows_scr[at : at + 1, 0:lanes] = s_ref[:, cols]
    lane = lax.broadcasted_iota(jnp.int32, (8, LANES), 1)
    rolled = pltpu.roll(rows_scr[0:8, :], low_shared, 1)
    scr[0:16, :] = jnp.zeros((16, LANES), F32)
    scr[0:8, :] = jnp.where(lane >= low_shared, rolled, 0.0)
    scr[1:9, :] += jnp.where(lane < low_shared, rolled, 0.0)
    o_ref[rows : rows + 16, :] = scr[0:16, :].astype(BF16)


def shift_out(plan, where, flat, shared):
    return pl.pallas_call(
        partial(shift_body, plan),
        out_shape=jax.ShapeDtypeStruct((plan.block, LANES), BF16),
        in_specs=[SMEM, VMEM, VMEM],
        out_specs=VMEM,
        scratch_shapes=[
            pltpu.VMEM((plan.rows_in, LANES), F32),
            pltpu.VMEM((plan.rows, LANES), F32),
        ],
        name="shift_out",
    )(where, flat, shared)


def finish_body(plan, n_in, where_ref, *refs):
    blocks = refs[:n_in]
    p_ref, m_ref, v_ref, ps_ref, ms_ref, vs_ref = refs[n_in : n_in + 6]
    outs = refs[n_in + 6 : n_in + 14]
    acc, rows_scr = refs[n_in + 14 :]
    low, row, low_shared = where_ref[0], where_ref[1], where_ref[2]
    rows_in, rows = plan.rows_in, plan.rows
    total = blocks[0][...].astype(F32)
    for block in blocks[1:]:
        total = total + block[...].astype(F32)
    acc[0 : plan.block, :] = total
    lane = lax.broadcasted_iota(jnp.int32, (rows_in, LANES), 1)
    back = lax.rem(LANES - low, LANES)
    first = pltpu.roll(acc[pl.ds(row, rows_in), :], back, 1)
    second = pltpu.roll(acc[pl.ds(row + 1, rows_in), :], back, 1)
    rows_scr[...] = jnp.where(lane < LANES - low, first, second)

    def update(grad, at, ins, out):
        weights, one, two = (ref[at] for ref in ins)
        for ref, value in zip(out, (grad,) + adam_update(weights, one, two, grad)):
            ref[at] = value

    main_in, main_out = (p_ref, m_ref, v_ref), outs[0:4]
    whole = plan.shard // 1024

    def step(at, carry):
        grad = rows_scr[pl.ds(pl.multiple_of(at * 8, 8), 8), :].reshape(1, 1024)
        cols = pl.ds(pl.multiple_of(at * 1024, 1024), 1024)
        update(grad, (0, slice(None), cols), main_in, main_out)
        return carry

    lax.fori_loop(0, whole, step, 0, unroll=4)
    for at, cols, lanes in split_flat(plan.shard):
        if at >= whole * 8:
            update(rows_scr[at : at + 1, 0:lanes], (0, slice(None), cols), main_in, main_out)
    lane = lax.broadcasted_iota(jnp.int32, (8, LANES), 1)
    back = lax.rem(LANES - low_shared, LANES)
    first = pltpu.roll(acc[rows : rows + 8, :], back, 1)
    second = pltpu.roll(acc[rows + 1 : rows + 9, :], back, 1)
    rows_scr[0:8, :] = jnp.where(lane < LANES - low_shared, first, second)
    for at, cols, lanes in split_flat(plan.shared_shard):
        update(
            rows_scr[at : at + 1, 0:lanes],
            (slice(None), cols),
            (ps_ref, ms_ref, vs_ref),
            outs[4:8],
        )


def finish(plan, where, blocks, flats, shareds):
    flat = jax.ShapeDtypeStruct(flats[0].shape, F32)
    shared = jax.ShapeDtypeStruct(shareds[0].shape, F32)
    return pl.pallas_call(
        partial(finish_body, plan, len(blocks)),
        out_shape=[flat] * 4 + [shared] * 4,
        in_specs=[SMEM] + [VMEM] * (len(blocks) + 6),
        out_specs=[VMEM] * 8,
        scratch_shapes=[
            pltpu.VMEM((plan.block, LANES), F32),
            pltpu.VMEM((plan.rows_in, LANES), F32),
        ],
        name="finish",
    )(where, *blocks, *flats, *shareds)


def chunked(total, width):
    step = total
    while step > 128 and step % 2 == 0:
        step //= 2
    return step


def largest_step(total, limit):
    return max(step for step in range(1, limit + 1) if total % step == 0)


def unpack_body(plan, n_in, idx_ref, *refs):
    ins = refs[:n_in]
    outs = refs[n_in : n_in + len(plan.shapes) + 1]
    flat, shf = refs[n_in + len(plan.shapes) + 1 :]
    full = plan.shard // TILE
    step_rows = 16 * largest_step(full - 1, 20)
    zero = jnp.zeros((16, LANES), F32)
    for at in range(plan.count):
        start = at * plan.shard // TILE * 16
        for tile in (0, full, full + 1):
            flat[start + tile * 16 : start + tile * 16 + 16, :] = zero
    shf[...] = jnp.zeros_like(shf)

    def place(src, owner):
        start = pl.multiple_of((owner * plan.shard) // TILE * 16, 16)

        def move(k, carry):
            at = pl.multiple_of(16 + k * step_rows, 16)
            flat[pl.ds(start + at, step_rows), :] = src[pl.ds(at, step_rows), :].astype(F32)
            return carry

        lax.fori_loop(0, (full - 1) * 16 // step_rows, move, 0)
        for tile in (0, full, full + 1):
            rows = pl.ds(pl.multiple_of(start + tile * 16, 16), 16)
            flat[rows, :] += src[tile * 16 : tile * 16 + 16, :].astype(F32)
        rows = pl.ds((owner * plan.shared_shard) // LANES, 16)
        shf[rows, :] += src[plan.rows : plan.rows + 16, :].astype(F32)

    if n_in > 1:
        for at in range(plan.count):
            place(ins[at], idx_ref[at])
    else:
        for at in range(plan.count):
            place(ins[0].at[at], at)
    for shape, base, out in zip(plan.shapes, plan.bases, outs):
        rows, width = as_matrix(shape)
        cols = width // LANES
        step = chunked(rows, cols)
        for col in range(cols):
            if step == rows:
                if rows == 1:
                    part = flat[base + col : base + col + 1, :]
                else:
                    part = flat[pl.ds(base + col, rows, stride=cols), :]
                out[:, col * LANES : (col + 1) * LANES] = part.astype(out.dtype)
            else:

                def move(k, carry, col=col, base=base, cols=cols, step=step, out=out):
                    at = pl.multiple_of(k * (step * cols), 8) + (base + col)
                    part = flat[pl.ds(at, step, stride=cols), :]
                    to = pl.multiple_of(k * step, step)
                    out[pl.ds(to, step), col * LANES : (col + 1) * LANES] = part.astype(out.dtype)
                    return carry

                lax.fori_loop(0, rows // step, move, 0)
    shared_out = outs[-1]
    cols = D // LANES
    for col in range(cols):
        shared_out[:, col * LANES : (col + 1) * LANES] = shf[
            pl.ds(col, shared_out.shape[0], stride=cols), :
        ]


def unpack(plan, idx, blocks):
    outs = [
        jax.ShapeDtypeStruct(as_matrix(shape), F32 if at in FLOAT_PIECES else BF16)
        for at, shape in enumerate(plan.shapes)
    ]
    outs.append(jax.ShapeDtypeStruct((14, D), F32))
    return pl.pallas_call(
        partial(unpack_body, plan, len(blocks)),
        out_shape=outs,
        in_specs=[SMEM] + [VMEM] * len(blocks),
        out_specs=[VMEM] * len(outs),
        scratch_shapes=[
            pltpu.VMEM((plan.alloc_rows, LANES), F32),
            pltpu.VMEM((plan.shared_rows + 16, LANES), F32),
        ],
        compiler_params=pltpu.CompilerParams(vmem_limit_bytes=48 * 1024 * 1024),
        name="unpack",
    )(idx, *blocks)


def pack_body(plan, idx_ref, *refs):
    n_in = len(plan.shapes) + 1
    ins = refs[:n_in]
    outs = refs[n_in : n_in + plan.count]
    stk, flat, shf, sem = refs[n_in + plan.count :]
    tail = plan.flat_rows // 8 * 8
    flat[tail:, :] = jnp.zeros((plan.alloc_rows - tail, LANES), F32)
    for shape, base, src in zip(plan.shapes, plan.bases, ins):
        rows, width = as_matrix(shape)
        cols = width // LANES
        step = chunked(rows, cols)
        for col in range(cols):
            if step == rows:
                part = src[:, col * LANES : (col + 1) * LANES].astype(F32)
                if rows == 1:
                    flat[base + col : base + col + 1, :] = part
                else:
                    flat[pl.ds(base + col, rows, stride=cols), :] = part
            else:

                def move(k, carry, col=col, base=base, cols=cols, step=step, src=src):
                    at = pl.multiple_of(k * (step * cols), 8) + (base + col)
                    frm = pl.multiple_of(k * step, step)
                    flat[pl.ds(at, step, stride=cols), :] = src[
                        pl.ds(frm, step), col * LANES : (col + 1) * LANES
                    ].astype(F32)
                    return carry

                lax.fori_loop(0, rows // step, move, 0)
    shf[...] = jnp.zeros_like(shf)
    cols = D // LANES
    for col in range(cols):
        shf[pl.ds(col, 14, stride=cols), :] = ins[-1][:, col * LANES : (col + 1) * LANES]

    def place(at, carry):
        start = pl.multiple_of((at * plan.shard) // TILE * 16, 16)
        stk[at, 0 : plan.rows, :] = flat[pl.ds(start, plan.rows), :].astype(BF16)
        return carry

    lax.fori_loop(0, plan.count, place, 0)
    for at in range(plan.count):
        base = at * plan.shared_shard // LANES
        stk[at, plan.rows : plan.rows + 16, :] = shf[base : base + 16, :].astype(BF16)
    copies = [
        pltpu.make_async_copy(stk.at[idx_ref[at]], outs[at], sem.at[at])
        for at in range(plan.count)
    ]
    for copy in copies:
        copy.start()
    for copy in copies:
        copy.wait()


def pack(plan, idx, piece_grads, shared_grad):
    pieces = [grad.reshape(as_matrix(shape)) for grad, shape in zip(piece_grads, plan.shapes)]
    block = jax.ShapeDtypeStruct((plan.block, LANES), BF16)
    return pl.pallas_call(
        partial(pack_body, plan),
        out_shape=[block] * plan.count,
        in_specs=[SMEM] + [VMEM] * (len(pieces) + 1),
        out_specs=[ANY] * plan.count,
        scratch_shapes=[
            pltpu.VMEM((plan.count, plan.block, LANES), BF16),
            pltpu.VMEM((plan.alloc_rows, LANES), F32),
            pltpu.VMEM((plan.shared_rows + 16, LANES), F32),
            pltpu.SemaphoreType.DMA((plan.count,)),
        ],
        compiler_params=pltpu.CompilerParams(vmem_limit_bytes=60 * 1024 * 1024),
        name="pack",
    )(idx, *pieces, shared_grad)


def permute(value, count, target, axis="dp"):
    return lax.ppermute(value, axis, [(at, target(at)) for at in range(count)])


def z_next(at):
    return (at + 4) % 16


def block_order(count):
    me = lax.axis_index("dp")
    if count != 16:
        return jnp.arange(count, dtype=jnp.int32)
    z, x, core = me // 4, (me // 2) % 2, me % 2
    order = []
    for back in range(4):
        for flip_x in range(2):
            for flip_core in range(2):
                order.append(
                    ((z + 4 - back) % 4) * 4 + (x ^ flip_x) * 2 + (core ^ flip_core)
                )
    return jnp.stack(order).astype(jnp.int32)


def across_core(value):
    return permute(value, 16, lambda at: at ^ 1)


def across_x(value):
    return permute(value, 16, lambda at: at ^ 2)


def along_z(value):
    return permute(value, 16, z_next)


def half_rows(block):
    return block.shape[0] // 32 * 16


def gather_blocks(count, own, alongside):
    if count != 16:
        return [lax.all_gather(own, "dp", axis=0)], alongside
    ring, column = [own], []
    for _ in range(3):
        upcoming, other, alongside = lax.optimization_barrier(
            (along_z(ring[-1]), across_x(ring[-1]), alongside)
        )
        ring.append(upcoming)
        column.append(other)
    half = half_rows(own)
    first, second = across_x(ring[3][:half]), along_z(column[2][half:])
    blocks = []
    for mine, other in zip(ring, column):
        for block in (mine, other):
            blocks += [block, across_core(block)]
    blocks += [ring[3], across_core(ring[3])]
    last = jnp.concatenate([first, second], axis=0)
    return blocks + [last, across_core(last)], alongside


def add_blocks(*blocks):
    return sum(block.astype(F32) for block in blocks).astype(BF16)


def scatter_blocks(count, blocks):
    if count != 16:
        return [
            lax.psum_scatter(jnp.stack(blocks).astype(F32), "dp", scatter_dimension=0, tiled=False)
        ]

    def pair(back, flip_x):
        at = back * 4 + flip_x * 2
        return add_blocks(blocks[at], across_core(blocks[at + 1]))

    half = half_rows(blocks[0])
    far = pair(1, 1)
    first, second = across_x(far[:half]), along_z(far[half:])
    first, second = lax.optimization_barrier((first, second))
    near = pair(1, 0)
    running = jnp.concatenate([add_blocks(near[:half], first), near[half:]], axis=0)
    far = pair(2, 1)
    far = jnp.concatenate([far[:half], add_blocks(far[half:], second)], axis=0)
    for back in (2, 3, 0):
        arrived, other = lax.optimization_barrier((along_z(running), across_x(far)))
        if back == 0:
            return [pair(0, 0), other, arrived]
        running = add_blocks(pair(back, 0), other, arrived)
        far = pair((back + 1) % 4, 1)


def dp_sum(value):
    count = lax.axis_size("dp")
    bit = 1
    while bit < count:
        steps = [bit, 2 * bit, 3 * bit] if 4 * bit <= count else [bit]
        parts = [permute(value, count, lambda at, step=step: at ^ step) for step in steps]
        value = sum(parts, value)
        bit *= 4 if len(steps) == 3 else 2
    return value


def tensor_total(partial_sum):
    own = partial_sum.astype(BF16)
    other = permute(own, lax.axis_size("tensor"), lambda at: at ^ 1, "tensor")
    return own.astype(F32) + other.astype(F32)


tensor_back_total = tensor_total


def mat_product(left, right):
    return jnp.dot(left, right, preferred_element_type=jnp.float32)


def left_transposed_matmul(left, right):
    return lax.dot_general(
        left, right, (((0,), (0,)), ((), ())), preferred_element_type=jnp.float32
    )


def right_trans_product(left, right):
    return lax.dot_general(
        left, right, (((1,), (1,)), ((), ())), preferred_element_type=jnp.float32
    )


def layer_norm(values, scaling, offset):
    centred = values - jnp.mean(values, axis=-1, keepdims=True)
    spread = jnp.mean(centred * centred, axis=-1, keepdims=True)
    return centred * lax.rsqrt(spread + NORM_EPS) * (1.0 + scaling) + offset


def norm_back(values, scaling, offset, d_output):
    primal_out, pull_back = jax.vjp(layer_norm, values, scaling, offset)
    return pull_back(d_output)


def silu_slope(values):
    sigma_vals = jax.nn.sigmoid(values)
    return sigma_vals * (1.0 + values * (1.0 - sigma_vals))


def position_table(seq_len, model_width):
    distance = (seq_len - 1 - jnp.arange(2 * seq_len - 1)).astype(jnp.float32)
    freq_index = jnp.arange(model_width // 2).astype(jnp.float32)
    rates = jnp.exp(freq_index * (-2.0 * math.log(10000.0) / model_width))
    angles = distance[:, None] * rates[None, :]
    table = jnp.stack([jnp.sin(angles), jnp.cos(angles)], axis=-1)
    return table.reshape(2 * seq_len - 1, model_width).astype(jnp.bfloat16)


def piece_shapes(model_width, ff_part, att_part, chan_part, kernel_len):
    feed_list = [(model_width, ff_part), (ff_part,), (ff_part, model_width)]
    attn_list = [
        (model_width, 3 * att_part),
        (model_width, att_part),
        (att_part, model_width),
        (att_part,),
        (att_part,),
    ]
    conv_list = [
        (model_width, 2 * chan_part),
        (2 * chan_part,),
        (kernel_len, chan_part),
        (chan_part,),
        (chan_part,),
        (chan_part,),
        (chan_part, model_width),
    ]
    return feed_list + attn_list + conv_list + feed_list


def rel_shift(position):
    leading = position.shape[:-2]
    seq_len = position.shape[-2]
    span_len = position.shape[-1]
    padded = jnp.pad(position, [(0, 0)] * len(leading) + [(0, 0), (0, 1)])
    flattened = padded.reshape(leading + (seq_len * (span_len + 1),))
    flattened = flattened[..., seq_len - 1 : seq_len - 1 + seq_len * span_len]
    return flattened.reshape(leading + (seq_len, span_len))[..., :seq_len]


def rel_unshift(grad_shifted):
    leading = grad_shifted.shape[:-2]
    seq_len = grad_shifted.shape[-1]
    span_len = 2 * seq_len - 1
    widened = jnp.pad(grad_shifted, [(0, 0)] * len(leading) + [(0, 0), (0, span_len - seq_len)])
    flattened = widened.reshape(leading + (seq_len * span_len,))
    flattened = jnp.pad(flattened, [(0, 0)] * len(leading) + [(seq_len - 1, 1)])
    return flattened.reshape(leading + (seq_len, span_len + 1))[..., :span_len]


def attention_scores(query_u, query_v, keys_b, pos_rows):
    content = jnp.einsum("bihd,bjhd->bhij", query_u, keys_b, preferred_element_type=jnp.float32)
    position = jnp.einsum("bihd,rhd->bhir", query_v, pos_rows, preferred_element_type=jnp.float32)
    return (content + rel_shift(position)) * (1.0 / math.sqrt(query_u.shape[-1]))


def key_mask(seq_lengths):
    return (jnp.arange(SEQ_LEN)[None, :] < seq_lengths[:, None])[:, None, None, :]


def conv_front(valid, pre_glu, tap_weights, tap_bias):
    chan_part = pre_glu.shape[-1] // 2
    gated = pre_glu[..., :chan_part] * jax.nn.sigmoid(pre_glu[..., chan_part:]) * valid[..., None]
    kernel_len = tap_weights.shape[0]
    margin = (kernel_len - 1) // 2
    filters = tap_weights.reshape(kernel_len, 1, chan_part)
    summed = lax.conv_general_dilated(
        gated,
        filters,
        (1,),
        [(margin, kernel_len - 1 - margin)],
        dimension_numbers=("NWC", "WIO", "NWC"),
        feature_group_count=chan_part,
        precision=lax.Precision.HIGHEST,
    )
    return summed + tap_bias


def batch_apply(conv_out, gamma_vec, beta_vec, mean_vec, inv_std):
    return jax.nn.silu((conv_out - mean_vec) * inv_std * (1.0 + gamma_vec) + beta_vec)


def feed_forward(resid, w_in, b_in, w_out, scaling, offset, b_out):
    normed = layer_norm(resid, scaling, offset).astype(jnp.bfloat16)
    hidden_pre = mat_product(normed, w_in) + b_in
    hidden = jax.nn.silu(hidden_pre).astype(jnp.bfloat16)
    branch = tensor_total(mat_product(hidden, w_out)) + b_out
    return (resid + 0.5 * branch, (normed, hidden_pre, hidden))


def feed_back(d_resid, resid, saved, w_in, w_out, scaling, offset):
    normed, hidden_pre, hidden = saved
    d_branch = 0.5 * d_resid
    grad_bout = jnp.sum(d_branch, axis=0)
    branch_gradient_second = d_branch.astype(jnp.bfloat16)
    grad_wout = left_transposed_matmul(hidden, branch_gradient_second)
    d_pre = right_trans_product(branch_gradient_second, w_out) * silu_slope(hidden_pre)
    grad_bin = jnp.sum(d_pre, axis=0)
    d_pre_b = d_pre.astype(jnp.bfloat16)
    grad_win = left_transposed_matmul(normed, d_pre_b)
    d_normed = tensor_back_total(right_trans_product(d_pre_b, w_in))
    d_input, grad_scale, grad_offset = norm_back(resid, scaling, offset, d_normed)
    return (
        d_resid + d_input,
        [grad_win, grad_bin, grad_wout],
        [grad_scale, grad_offset, grad_bout],
    )


def attention_forward(resid, weights, scaling, offset, b_out, lengths, table):
    w_qkv, w_pos, w_att, bias_u, bias_v = weights
    seq_count = lengths.shape[0]
    att_part = w_att.shape[0]
    head_count = att_part // HEAD_DIM

    def to_heads(block):
        return block.reshape(seq_count, SEQ_LEN, head_count, HEAD_DIM)

    normed = layer_norm(resid, scaling, offset).astype(jnp.bfloat16)
    qkv_rows = mat_product(normed, w_qkv)
    query = qkv_rows[:, :att_part]
    query_u = to_heads((query + bias_u).astype(jnp.bfloat16))
    query_v = to_heads((query + bias_v).astype(jnp.bfloat16))
    keys_b = to_heads(qkv_rows[:, att_part : 2 * att_part].astype(jnp.bfloat16))
    values_b = to_heads(qkv_rows[:, 2 * att_part :].astype(jnp.bfloat16))
    pos_rows = (
        mat_product(table, w_pos)
        .astype(jnp.bfloat16)
        .reshape(2 * SEQ_LEN - 1, head_count, HEAD_DIM)
    )
    scores = attention_scores(query_u, query_v, keys_b, pos_rows)
    exponent = jnp.where(key_mask(lengths), jnp.exp(scores), 0.0)
    totals = jnp.sum(exponent, axis=-1)
    log_total = jnp.log(totals)
    probs = (exponent / totals[..., None]).astype(jnp.bfloat16)
    context = jnp.einsum("bhij,bjhd->bihd", probs, values_b, preferred_element_type=jnp.float32)
    context_rows_second = context.reshape(seq_count * SEQ_LEN, att_part).astype(jnp.bfloat16)
    branch = tensor_total(mat_product(context_rows_second, w_att)) + b_out
    return (
        resid + branch,
        (normed, query_u, query_v, keys_b, values_b, pos_rows, log_total, context_rows_second),
    )


def attention_back(d_resid, resid, saved, weights, scaling, offset, lengths, table):
    normed, query_u, query_v, keys_b, values_b, pos_rows, log_total, context_rows_second = saved
    w_qkv, w_pos, w_att, bias_u, bias_v = weights
    seq_count = lengths.shape[0]
    att_part = w_att.shape[0]
    rows_total = seq_count * SEQ_LEN
    scale = 1.0 / math.sqrt(HEAD_DIM)
    grad_bout = jnp.sum(d_resid, axis=0)
    branch_gradient_second = d_resid.astype(jnp.bfloat16)
    attention_weight_gradient = left_transposed_matmul(context_rows_second, branch_gradient_second)
    d_context = (
        right_trans_product(branch_gradient_second, w_att)
        .astype(jnp.bfloat16)
        .reshape(query_u.shape)
    )
    scores = attention_scores(query_u, query_v, keys_b, pos_rows)
    probs = jnp.where(key_mask(lengths), jnp.exp(scores - log_total[..., None]), 0.0)
    probs_b = probs.astype(jnp.bfloat16)
    d_values = jnp.einsum("bhij,bihd->bjhd", probs_b, d_context, preferred_element_type=jnp.float32)
    d_probs = jnp.einsum("bihd,bjhd->bhij", d_context, values_b, preferred_element_type=jnp.float32)
    row_dot = jnp.sum(probs * d_probs, axis=-1, keepdims=True)
    d_scores = (probs * (d_probs - row_dot) * scale).astype(jnp.bfloat16)
    d_query_u = jnp.einsum("bhij,bjhd->bihd", d_scores, keys_b, preferred_element_type=jnp.float32)
    d_keys = jnp.einsum("bhij,bihd->bjhd", d_scores, query_u, preferred_element_type=jnp.float32)
    d_position = rel_unshift(d_scores)
    d_query_v = jnp.einsum(
        "bhir,rhd->bihd", d_position, pos_rows, preferred_element_type=jnp.float32
    )
    d_pos_rows = jnp.einsum(
        "bhir,bihd->rhd", d_position, query_v, preferred_element_type=jnp.float32
    )
    content_bias_gradient = jnp.sum(d_query_u, axis=(0, 1)).reshape(att_part)
    position_bias_gradient = jnp.sum(d_query_v, axis=(0, 1)).reshape(att_part)
    d_query = (d_query_u + d_query_v).reshape(rows_total, att_part)
    d_qkv = jnp.concatenate(
        [d_query, d_keys.reshape(rows_total, att_part), d_values.reshape(rows_total, att_part)],
        axis=1,
    ).astype(jnp.bfloat16)
    query_key_value_weight_gradient = left_transposed_matmul(normed, d_qkv)
    position_weight_gradient = lax.dot_general(
        table.astype(jnp.float32),
        d_pos_rows.reshape(2 * SEQ_LEN - 1, att_part),
        (((0,), (0,)), ((), ())),
        precision=lax.Precision.HIGHEST,
    )
    d_normed = tensor_back_total(right_trans_product(d_qkv, w_qkv))
    d_input, grad_scale, grad_offset = norm_back(resid, scaling, offset, d_normed)
    return (
        d_resid + d_input,
        [
            query_key_value_weight_gradient,
            position_weight_gradient,
            attention_weight_gradient,
            content_bias_gradient,
            position_bias_gradient,
        ],
        [grad_scale, grad_offset, grad_bout],
    )


def conv_forward(resid, weights, scaling, offset, b_out, valid):
    w_glu, b_glu, tap_weights, tap_bias, gamma_vec, beta_vec, w_conv = weights
    seq_count = valid.shape[0]
    chan_part = w_conv.shape[0]
    normed = layer_norm(resid, scaling, offset).astype(jnp.bfloat16)
    pre_glu = (mat_product(normed, w_glu) + b_glu).reshape(seq_count, SEQ_LEN, 2 * chan_part)
    conv_out = conv_front(valid, pre_glu, tap_weights, tap_bias)
    masked = conv_out * valid[..., None]
    stats = dp_sum(
        jnp.stack(
            [
                jnp.sum(masked, axis=(0, 1)),
                jnp.sum(masked * conv_out, axis=(0, 1)),
                jnp.broadcast_to(jnp.sum(valid), (chan_part,)),
            ]
        )
    )
    first_sum, square_sum, count_all = stats[0], stats[1], stats[2]
    mean_vec = first_sum / count_all
    inv_std = lax.rsqrt(square_sum / count_all - mean_vec * mean_vec + BATCH_EPS)
    activated = (
        batch_apply(conv_out, gamma_vec, beta_vec, mean_vec, inv_std)
        .reshape(seq_count * SEQ_LEN, chan_part)
        .astype(jnp.bfloat16)
    )
    branch = tensor_total(mat_product(activated, w_conv)) + b_out
    return (resid + branch, (normed, pre_glu, conv_out, mean_vec, inv_std, count_all, activated))


def conv_back(d_resid, resid, saved, weights, scaling, offset, valid):
    normed, pre_glu, conv_out, mean_vec, inv_std, count_all, activated = saved
    w_glu, b_glu, tap_weights, tap_bias, gamma_vec, beta_vec, w_conv = weights
    grad_bout = jnp.sum(d_resid, axis=0)
    branch_gradient_second = d_resid.astype(jnp.bfloat16)
    grad_wconv = left_transposed_matmul(activated, branch_gradient_second)
    d_act = right_trans_product(branch_gradient_second, w_conv).reshape(conv_out.shape)
    primal_out, pull_norm = jax.vjp(batch_apply, conv_out, gamma_vec, beta_vec, mean_vec, inv_std)
    d_conv, grad_gamma, grad_beta, d_mean, d_inv = pull_norm(d_act)
    sums = dp_sum(jnp.stack([d_mean, d_inv]))
    d_mean, d_inv = sums[0], sums[1]
    d_var = -0.5 * inv_std * inv_std * inv_std * d_inv
    d_first = (d_mean - 2.0 * mean_vec * d_var) / count_all
    d_square = d_var / count_all
    d_conv = d_conv + valid[..., None] * (d_first + 2.0 * conv_out * d_square)
    primal_two, pull_front = jax.vjp(partial(conv_front, valid), pre_glu, tap_weights, tap_bias)
    d_pre, grad_taps, grad_tbias = pull_front(d_conv)
    d_pre = d_pre.reshape(-1, d_pre.shape[-1])
    grad_bglu = jnp.sum(d_pre, axis=0)
    d_pre_b = d_pre.astype(jnp.bfloat16)
    grad_wglu = left_transposed_matmul(normed, d_pre_b)
    d_normed = tensor_back_total(right_trans_product(d_pre_b, w_glu))
    d_input, grad_scale, grad_offset = norm_back(resid, scaling, offset, d_normed)
    return (
        d_resid + d_input,
        [grad_wglu, grad_bglu, grad_taps, grad_tbias, grad_gamma, grad_beta, grad_wconv],
        [grad_scale, grad_offset, grad_bout],
    )


def layer_forward(resid, pieces, vectors, lengths, valid, table):
    resid_a, keep_a = feed_forward(
        resid, pieces[0], pieces[1], pieces[2], vectors[0], vectors[1], vectors[2]
    )
    resid_b, keep_b = attention_forward(
        resid_a, pieces[3:8], vectors[3], vectors[4], vectors[5], lengths, table
    )
    resid_c, keep_c = conv_forward(resid_b, pieces[8:15], vectors[6], vectors[7], vectors[8], valid)
    resid_d, keep_d = feed_forward(
        resid_c, pieces[15], pieces[16], pieces[17], vectors[9], vectors[10], vectors[11]
    )
    output = layer_norm(resid_d, vectors[12], vectors[13])
    return (output, (resid, resid_a, resid_b, resid_c, resid_d), (keep_a, keep_b, keep_c, keep_d))


def layer_back(d_output, pieces, vectors, lengths, valid, table, resids, keeps):
    resid, resid_a, resid_b, resid_c, resid_d = resids
    d_resid_d, grad_fscale, grad_foffset = norm_back(resid_d, vectors[12], vectors[13], d_output)
    d_resid_c, grads_d, shared_d = feed_back(
        d_resid_d, resid_c, keeps[3], pieces[15], pieces[17], vectors[9], vectors[10]
    )
    d_resid_b, grads_c, shared_c = conv_back(
        d_resid_c, resid_b, keeps[2], pieces[8:15], vectors[6], vectors[7], valid
    )
    d_resid_a, grads_b, shared_b = attention_back(
        d_resid_b, resid_a, keeps[1], pieces[3:8], vectors[3], vectors[4], lengths, table
    )
    d_resid, grads_a, shared_a = feed_back(
        d_resid_a, resid, keeps[0], pieces[0], pieces[2], vectors[0], vectors[1]
    )
    piece_grads = grads_a + grads_b + grads_c + grads_d
    vector_grads = shared_a + shared_b + shared_c + shared_d + [grad_fscale, grad_foffset]
    return (d_resid, piece_grads, vector_grads)


def adam_update(weights, first, second, gradient_list):
    first_new = BETA_ONE * first + (1.0 - BETA_ONE) * gradient_list
    second_new = BETA_TWO * second + (1.0 - BETA_TWO) * gradient_list * gradient_list
    first_hat = first_new / (1.0 - BETA_ONE**STEP_COUNT)
    second_hat = second_new / (1.0 - BETA_TWO**STEP_COUNT)
    weights_new = weights - LEARN_RATE * (
        first_hat / (jnp.sqrt(second_hat) + ADAM_EPS) + WEIGHT_DECAY * weights
    )
    return (weights_new, first_new, second_new)


def local(
    tokens,
    lengths,
    cotangent,
    params,
    shared,
    first_moment,
    second_moment,
    first_shared,
    second_shared,
):
    part_count = lax.axis_size("tensor")
    shapes = piece_shapes(
        D, FF // part_count, HEADS * HEAD_DIM // part_count, D // part_count, KERNEL
    )
    count = lax.axis_size("dp")
    plan = Plan(count, params.shape[2], shared.shape[1], shapes)
    me = lax.axis_index("dp")
    start = me * plan.shard % TILE
    where = jnp.stack([start % LANES, start // LANES, me * plan.shared_shard % LANES]).astype(
        jnp.int32
    )
    order = block_order(count)
    own = shift_out(plan, where, params.reshape(1, 1, -1), shared)
    table = position_table(SEQ_LEN, D)
    gathered, table = gather_blocks(count, own, table)
    unpacked = unpack(plan, order, gathered)
    pieces = [piece.reshape(shape) for piece, shape in zip(unpacked[:-1], shapes)]
    vectors = [unpacked[-1][at] for at in range(14)]
    valid = (jnp.arange(SEQ_LEN)[None, :] < lengths[:, None]).astype(F32)
    resid = tokens.astype(F32)
    result, resids, keeps = layer_forward(resid, pieces, vectors, lengths, valid, table)
    d_resid, piece_grads, vector_grads = layer_back(
        cotangent, pieces, vectors, lengths, valid, table, resids, keeps
    )
    blocks = pack(plan, order, piece_grads, jnp.stack(vector_grads))
    (
        grad_params,
        new_params,
        new_first,
        new_second,
        grad_shared,
        new_shared,
        new_first_sh,
        new_second_sh,
    ) = finish(
        plan,
        where,
        scatter_blocks(count, blocks),
        (params, first_moment, second_moment),
        (shared, first_shared, second_shared),
    )
    return (
        result,
        d_resid,
        grad_params,
        grad_shared,
        new_params,
        new_shared,
        new_first,
        new_second,
        new_first_sh,
        new_second_sh,
    )


def solution(mesh):
    in_specs = (
        P("dp", None),
        P("dp"),
        P("dp", None),
        P(None, "tensor", "dp"),
        P(None, "dp"),
        P(None, "tensor", "dp"),
        P(None, "tensor", "dp"),
        P(None, "dp"),
        P(None, "dp"),
    )
    out_specs = (
        P("dp", None),
        P("dp", None),
        P(None, "tensor", "dp"),
        P(None, "dp"),
        P(None, "tensor", "dp"),
        P(None, "dp"),
        P(None, "tensor", "dp"),
        P(None, "tensor", "dp"),
        P(None, "dp"),
        P(None, "dp"),
    )
    return jax.shard_map(local, mesh=mesh, in_specs=in_specs, out_specs=out_specs, check_vma=False)
```

```python
from functools import partial
import math

import jax
import jax.numpy as jnp
from jax import lax
from jax.experimental import pallas as pl
from jax.experimental.pallas import tpu as pltpu
from jax.sharding import PartitionSpec as P


D = 512
FF = 2048
HEADS = 8
HEAD_DIM = 64
KERNEL = 31
SEQ_LEN = 128


NORM_EPS = 1e-05
BATCH_EPS = 1e-05
LEARN_RATE = 0.02
BETA_ONE = 0.9
BETA_TWO = 0.999
ADAM_EPS = 1e-08
WEIGHT_DECAY = 0.1
STEP_COUNT = 5
FLOAT_PIECES = (1, 6, 7, 9, 10, 11, 12, 13, 16)

LANES = 128
TILE = 16 * LANES
SHARED_ROWS = 16
BF16 = jnp.bfloat16
F32 = jnp.float32
ANY = pl.BlockSpec(memory_space=pl.ANY)
VMEM = pl.BlockSpec(memory_space=pltpu.VMEM)
SMEM = pl.BlockSpec(memory_space=pltpu.SMEM)


def round_up(value, multiple):
    return -(-value // multiple) * multiple


class Plan:
    def __init__(self, count, shard, shared_shard, shapes):
        self.count = count
        self.shard = shard
        self.shared_shard = shared_shard
        self.shapes = shapes
        self.rows_in = round_up(shard // LANES + 2, 8)
        self.rows = round_up(self.rows_in + 16, 16)
        self.block = self.rows + SHARED_ROWS
        self.half = self.block * 4 // 11 // 16 * 16
        self.sizes = (self.half, self.block - self.half)
        self.flat_rows = count * shard // LANES
        self.alloc_rows = round_up(((count - 1) * shard // TILE) * 16 + self.rows, 16)
        self.shared_rows = count * shared_shard // LANES
        self.bases = []
        at = 0
        for shape in shapes:
            self.bases.append(at // LANES)
            at += math.prod(shape)


def as_matrix(shape):
    return shape if len(shape) == 2 else (1, shape[0])


def split_flat(length):
    return [
        (at // LANES, slice(at, min(at + LANES, length)), min(LANES, length - at))
        for at in range(0, length, LANES)
    ]


def shift_body(plan, where_ref, x_ref, s_ref, a_ref, b_ref, rows_scr, scr):
    low, row, low_shared = where_ref[0], where_ref[1], where_ref[2]
    rows_in, rows = plan.rows_in, plan.rows
    whole = plan.shard // 1024

    def load(at, carry):
        part = x_ref[0, :, pl.ds(pl.multiple_of(at * 1024, 1024), 1024)]
        rows_scr[pl.ds(pl.multiple_of(at * 8, 8), 8), :] = part.reshape(8, LANES)
        return carry

    lax.fori_loop(0, whole, load, 0, unroll=4)
    rows_scr[whole * 8 :, :] = jnp.zeros((rows_in - whole * 8, LANES), F32)
    for at, cols, lanes in split_flat(plan.shard):
        if at >= whole * 8:
            rows_scr[at : at + 1, 0:lanes] = x_ref[0, :, cols]
    scr[rows - 32 :, :] = jnp.zeros((32, LANES), F32)
    scr[0:16, :] = jnp.zeros((16, LANES), F32)
    lane = lax.broadcasted_iota(jnp.int32, (rows_in, LANES), 1)
    rolled = pltpu.roll(rows_scr[...], low, 1)
    scr[pl.ds(row, rows_in), :] = jnp.where(lane >= low, rolled, 0.0)
    scr[pl.ds(row + rows_in, 1), :] = jnp.zeros((1, LANES), F32)
    scr[pl.ds(row + 1, rows_in), :] += jnp.where(lane < low, rolled, 0.0)
    half = plan.half
    a_ref[...] = scr[0:half, :].astype(BF16)
    b_ref[0 : rows - half, :] = scr[half:, :].astype(BF16)
    rows_scr[0:8, :] = jnp.zeros((8, LANES), F32)
    for at, cols, lanes in split_flat(plan.shared_shard):
        rows_scr[at : at + 1, 0:lanes] = s_ref[:, cols]
    lane = lax.broadcasted_iota(jnp.int32, (8, LANES), 1)
    rolled = pltpu.roll(rows_scr[0:8, :], low_shared, 1)
    scr[0:16, :] = jnp.zeros((16, LANES), F32)
    scr[0:8, :] = jnp.where(lane >= low_shared, rolled, 0.0)
    scr[1:9, :] += jnp.where(lane < low_shared, rolled, 0.0)
    b_ref[rows - half : rows - half + 16, :] = scr[0:16, :].astype(BF16)


def shift_out(plan, where, flat, shared):
    return pl.pallas_call(
        partial(shift_body, plan),
        out_shape=[jax.ShapeDtypeStruct((size, LANES), BF16) for size in plan.sizes],
        in_specs=[SMEM, VMEM, VMEM],
        out_specs=[VMEM] * 2,
        scratch_shapes=[
            pltpu.VMEM((plan.rows_in, LANES), F32),
            pltpu.VMEM((plan.rows, LANES), F32),
        ],
        name="shift_out",
    )(where, flat, shared)


def finish_body(plan, n_in, where_ref, *refs):
    blocks = refs[:n_in]
    p_ref, m_ref, v_ref, ps_ref, ms_ref, vs_ref = refs[n_in : n_in + 6]
    outs = refs[n_in + 6 : n_in + 14]
    acc, rows_scr = refs[n_in + 14 :]
    low, row, low_shared = where_ref[0], where_ref[1], where_ref[2]
    rows_in, rows = plan.rows_in, plan.rows
    each = n_in // 2
    for at, rows_of in enumerate((slice(0, plan.half), slice(plan.half, plan.block))):
        parts = [block[...].astype(F32) for block in blocks[at * each : at * each + each]]
        acc[rows_of, :] = sum(parts[1:], parts[0])
    lane = lax.broadcasted_iota(jnp.int32, (rows_in, LANES), 1)
    back = lax.rem(LANES - low, LANES)
    first = pltpu.roll(acc[pl.ds(row, rows_in), :], back, 1)
    second = pltpu.roll(acc[pl.ds(row + 1, rows_in), :], back, 1)
    rows_scr[...] = jnp.where(lane < LANES - low, first, second)

    def update(grad, at, ins, out):
        weights, one, two = (ref[at] for ref in ins)
        for ref, value in zip(out, (grad,) + adam_update(weights, one, two, grad)):
            ref[at] = value

    main_in, main_out = (p_ref, m_ref, v_ref), outs[0:4]
    whole = plan.shard // 1024

    def step(at, carry):
        grad = rows_scr[pl.ds(pl.multiple_of(at * 8, 8), 8), :].reshape(1, 1024)
        cols = pl.ds(pl.multiple_of(at * 1024, 1024), 1024)
        update(grad, (0, slice(None), cols), main_in, main_out)
        return carry

    lax.fori_loop(0, whole, step, 0, unroll=4)
    for at, cols, lanes in split_flat(plan.shard):
        if at >= whole * 8:
            update(rows_scr[at : at + 1, 0:lanes], (0, slice(None), cols), main_in, main_out)
    lane = lax.broadcasted_iota(jnp.int32, (8, LANES), 1)
    back = lax.rem(LANES - low_shared, LANES)
    first = pltpu.roll(acc[rows : rows + 8, :], back, 1)
    second = pltpu.roll(acc[rows + 1 : rows + 9, :], back, 1)
    rows_scr[0:8, :] = jnp.where(lane < LANES - low_shared, first, second)
    for at, cols, lanes in split_flat(plan.shared_shard):
        update(
            rows_scr[at : at + 1, 0:lanes],
            (slice(None), cols),
            (ps_ref, ms_ref, vs_ref),
            outs[4:8],
        )


def finish(plan, where, blocks, flats, shareds):
    flat = jax.ShapeDtypeStruct(flats[0].shape, F32)
    shared = jax.ShapeDtypeStruct(shareds[0].shape, F32)
    return pl.pallas_call(
        partial(finish_body, plan, len(blocks)),
        out_shape=[flat] * 4 + [shared] * 4,
        in_specs=[SMEM] + [VMEM] * (len(blocks) + 6),
        out_specs=[VMEM] * 8,
        scratch_shapes=[
            pltpu.VMEM((plan.block, LANES), F32),
            pltpu.VMEM((plan.rows_in, LANES), F32),
        ],
        name="finish",
    )(where, *blocks, *flats, *shareds)


def chunked(total):
    step = total
    while step > 128 and step % 2 == 0:
        step //= 2
    return step


def largest_step(total, limit):
    return max(step for step in range(1, limit + 1) if total % step == 0)


def unpack_body(plan, n_in, idx_ref, *refs):
    ins = refs[:n_in]
    outs = refs[n_in : n_in + len(plan.shapes) + 1]
    flat, shf = refs[n_in + len(plan.shapes) + 1 :]
    full = plan.shard // TILE
    zero = jnp.zeros((16, LANES), F32)
    for at in range(plan.count):
        start = at * plan.shard // TILE * 16
        for tile in (0, full, full + 1):
            flat[start + tile * 16 : start + tile * 16 + 16, :] = zero
    shf[...] = jnp.zeros_like(shf)

    def place(first, second, owner):
        start = pl.multiple_of((owner * plan.shard) // TILE * 16, 16)
        edge = plan.half // 16
        for src, begin, end, origin in ((first, 1, edge, 0), (second, edge, full, edge)):
            step = largest_step(end - begin, 25)

            def move(k, carry, src=src, begin=begin, origin=origin, step=step):
                to = pl.multiple_of(start + begin * 16 + k * (step * 16), 16)
                frm = pl.multiple_of((begin - origin) * 16 + k * (step * 16), 16)
                flat[pl.ds(to, step * 16), :] = src[pl.ds(frm, step * 16), :].astype(F32)
                return carry

            lax.fori_loop(0, (end - begin) // step, move, 0)
        for src, at, tile in (
            (first, 0, 0),
            (second, full - edge, full),
            (second, full + 1 - edge, full + 1),
        ):
            rows = pl.ds(pl.multiple_of(start + tile * 16, 16), 16)
            flat[rows, :] += src[at * 16 : at * 16 + 16, :].astype(F32)
        rows = pl.ds((owner * plan.shared_shard) // LANES, 16)
        at = plan.rows - plan.half
        shf[rows, :] += second[at : at + 16, :].astype(F32)

    if n_in > 2:
        for at in range(plan.count):
            place(ins[2 * at], ins[2 * at + 1], idx_ref[at])
    else:
        for at in range(plan.count):
            place(ins[0].at[at], ins[1].at[at], at)
    for shape, base, out in zip(plan.shapes, plan.bases, outs):
        rows, width = as_matrix(shape)
        cols = width // LANES
        step = chunked(rows)
        for col in range(cols):
            if step == rows:
                if rows == 1:
                    part = flat[base + col : base + col + 1, :]
                else:
                    part = flat[pl.ds(base + col, rows, stride=cols), :]
                out[:, col * LANES : (col + 1) * LANES] = part.astype(out.dtype)
            else:

                def move(k, carry, col=col, base=base, cols=cols, step=step, out=out):
                    at = pl.multiple_of(k * (step * cols), 8) + (base + col)
                    part = flat[pl.ds(at, step, stride=cols), :]
                    to = pl.multiple_of(k * step, step)
                    out[pl.ds(to, step), col * LANES : (col + 1) * LANES] = part.astype(out.dtype)
                    return carry

                lax.fori_loop(0, rows // step, move, 0)
    shared_out = outs[-1]
    cols = D // LANES
    for col in range(cols):
        shared_out[:, col * LANES : (col + 1) * LANES] = shf[
            pl.ds(col, shared_out.shape[0], stride=cols), :
        ]


def unpack(plan, idx, blocks):
    outs = [
        jax.ShapeDtypeStruct(as_matrix(shape), F32 if at in FLOAT_PIECES else BF16)
        for at, shape in enumerate(plan.shapes)
    ]
    outs.append(jax.ShapeDtypeStruct((14, D), F32))
    return pl.pallas_call(
        partial(unpack_body, plan, len(blocks)),
        out_shape=outs,
        in_specs=[SMEM] + [VMEM] * len(blocks),
        out_specs=[VMEM] * len(outs),
        scratch_shapes=[
            pltpu.VMEM((plan.alloc_rows, LANES), F32),
            pltpu.VMEM((plan.shared_rows + 16, LANES), F32),
        ],
        compiler_params=pltpu.CompilerParams(vmem_limit_bytes=48 * 1024 * 1024),
        name="unpack",
    )(idx, *blocks)


def pack_body(plan, idx_ref, *refs):
    n_in = len(plan.shapes) + 1
    ins = refs[:n_in]
    outs = refs[n_in : n_in + 2 * plan.count]
    flat, shf = refs[n_in + 2 * plan.count :]
    tail = plan.flat_rows // 8 * 8
    flat[tail:, :] = jnp.zeros((plan.alloc_rows - tail, LANES), F32)
    for shape, base, src in zip(plan.shapes, plan.bases, ins):
        rows, width = as_matrix(shape)
        cols = width // LANES
        step = chunked(rows)
        for col in range(cols):
            if step == rows:
                part = src[:, col * LANES : (col + 1) * LANES].astype(F32)
                if rows == 1:
                    flat[base + col : base + col + 1, :] = part
                else:
                    flat[pl.ds(base + col, rows, stride=cols), :] = part
            else:

                def move(k, carry, col=col, base=base, cols=cols, step=step, src=src):
                    at = pl.multiple_of(k * (step * cols), 8) + (base + col)
                    frm = pl.multiple_of(k * step, step)
                    flat[pl.ds(at, step, stride=cols), :] = src[
                        pl.ds(frm, step), col * LANES : (col + 1) * LANES
                    ].astype(F32)
                    return carry

                lax.fori_loop(0, rows // step, move, 0)
    shf[...] = jnp.zeros_like(shf)
    cols = D // LANES
    for col in range(cols):
        shf[pl.ds(col, 14, stride=cols), :] = ins[-1][:, col * LANES : (col + 1) * LANES]

    half = plan.half
    for at in range(plan.count):
        owner = idx_ref[at]
        start = pl.multiple_of((owner * plan.shard) // TILE * 16, 16)
        for out, begin, end in ((outs[2 * at], 0, half), (outs[2 * at + 1], half, plan.rows)):
            step = 16 * largest_step((end - begin) // 16, 25)

            def move(k, carry, out=out, begin=begin, step=step, start=start):
                to = pl.multiple_of(k * step, 16)
                frm = pl.multiple_of(start + begin + k * step, 16)
                out[pl.ds(to, step), :] = flat[pl.ds(frm, step), :].astype(BF16)
                return carry

            lax.fori_loop(0, (end - begin) // step, move, 0)
        rows = pl.ds((owner * plan.shared_shard) // LANES, 16)
        outs[2 * at + 1][plan.rows - half : plan.block - half, :] = shf[rows, :].astype(BF16)


def pack(plan, idx, piece_grads, shared_grad):
    pieces = [
        grad.reshape(as_matrix(shape)).astype(F32 if at in FLOAT_PIECES else BF16)
        for at, (grad, shape) in enumerate(zip(piece_grads, plan.shapes))
    ]
    halves = [jax.ShapeDtypeStruct((size, LANES), BF16) for size in plan.sizes]
    return pl.pallas_call(
        partial(pack_body, plan),
        out_shape=halves * plan.count,
        in_specs=[SMEM] + [VMEM] * (len(pieces) + 1),
        out_specs=[VMEM] * (2 * plan.count),
        scratch_shapes=[
            pltpu.VMEM((plan.alloc_rows, LANES), F32),
            pltpu.VMEM((plan.shared_rows + 16, LANES), F32),
        ],
        compiler_params=pltpu.CompilerParams(vmem_limit_bytes=48 * 1024 * 1024),
        name="pack",
    )(idx, *pieces, shared_grad)


def permute(value, count, target, axis="dp"):
    return lax.ppermute(value, axis, [(at, target(at)) for at in range(count)])


def z_next(at):
    return (at + 4) % 16


def block_order(count):
    me = lax.axis_index("dp")
    if count != 16:
        return jnp.arange(count, dtype=jnp.int32)
    z, x, core = me // 4, (me // 2) % 2, me % 2
    order = []
    for back in range(4):
        for flip_x in range(2):
            for flip_core in range(2):
                order.append(
                    ((z + 4 - back) % 4) * 4 + (x ^ flip_x) * 2 + (core ^ flip_core)
                )
    return jnp.stack(order).astype(jnp.int32)


def across_core(value):
    return permute(value, 16, lambda at: at ^ 1)


def across_x(value):
    return permute(value, 16, lambda at: at ^ 2)


def along_z(value):
    return permute(value, 16, z_next)


def gather_blocks(count, own, alongside):
    if count != 16:
        return [lax.all_gather(half, "dp", axis=0) for half in own], alongside
    ring = [[half] for half in own]
    column = [[], []]
    for step in range(3):
        for part in range(2):
            upcoming, other = along_z(ring[part][-1]), across_x(ring[part][-1])
            if step == 0 and part == 0:
                upcoming, other, alongside = lax.optimization_barrier(
                    (upcoming, other, alongside)
                )
            elif part == 0:
                upcoming, other = lax.optimization_barrier((upcoming, other))
            else:
                upcoming, other, _ = lax.optimization_barrier((upcoming, other, ring[0][-1]))
            ring[part].append(upcoming)
            column[part].append(other)
    column[0].append(across_x(ring[0][3]))
    column[1].append(along_z(column[1][2]))
    blocks = []
    for step in range(4):
        for side in (ring, column):
            mine = [side[0][step], side[1][step]]
            blocks += mine + [across_core(half) for half in mine]
    return blocks, alongside


def add_blocks(*blocks):
    return sum(block.astype(F32) for block in blocks).astype(BF16)


def scatter_blocks(count, blocks):
    if count != 16:
        return [
            lax.psum_scatter(
                jnp.stack(blocks[part::2]).astype(F32), "dp", scatter_dimension=0, tiled=False
            )
            for part in range(2)
        ]

    def pair(back, flip_x, part):
        at = (back * 4 + flip_x * 2) * 2 + part
        return [blocks[at], across_core(blocks[at + 2])]

    moved = (across_x(add_blocks(*pair(1, 1, 0))), along_z(add_blocks(*pair(1, 1, 1))))
    running = [add_blocks(*pair(1, 0, 0), moved[0]), add_blocks(*pair(1, 0, 1))]
    far = [add_blocks(*pair(2, 1, 0)), add_blocks(*pair(2, 1, 1), moved[1])]
    final, before = [], moved[0]
    for back in (2, 3, 0):
        for part in range(2):
            arrived, other, before = lax.optimization_barrier(
                (along_z(running[part]), across_x(far[part]), before)
            )
            before = arrived
            if back == 0:
                final += pair(0, 0, part) + [other, arrived]
                continue
            running[part] = add_blocks(*pair(back, 0, part), other, arrived)
            far[part] = add_blocks(*pair((back + 1) % 4, 1, part))
    return final


def dp_sum(value):
    count = lax.axis_size("dp")
    bit = 1
    while bit < count:
        steps = [bit, 2 * bit, 3 * bit] if 4 * bit <= count else [bit]
        parts = [permute(value, count, lambda at, step=step: at ^ step) for step in steps]
        value = sum(parts, value)
        bit *= 4 if len(steps) == 3 else 2
    return value


def tensor_total(partial_sum):
    own = partial_sum.astype(BF16)
    other = permute(own, lax.axis_size("tensor"), lambda at: at ^ 1, "tensor")
    return own.astype(F32) + other.astype(F32)


tensor_back_total = tensor_total


def mat_product(left, right):
    return jnp.dot(left, right, preferred_element_type=jnp.float32)


def left_transposed_matmul(left, right):
    return lax.dot_general(
        left, right, (((0,), (0,)), ((), ())), preferred_element_type=jnp.float32
    )


def right_trans_product(left, right):
    return lax.dot_general(
        left, right, (((1,), (1,)), ((), ())), preferred_element_type=jnp.float32
    )


def layer_norm(values, scaling, offset):
    centred = values - jnp.mean(values, axis=-1, keepdims=True)
    spread = jnp.mean(centred * centred, axis=-1, keepdims=True)
    return centred * lax.rsqrt(spread + NORM_EPS) * (1.0 + scaling) + offset


def norm_back(values, scaling, offset, d_output):
    _, pull_back = jax.vjp(layer_norm, values, scaling, offset)
    return pull_back(d_output)


def silu_slope(values):
    sigma_vals = jax.nn.sigmoid(values)
    return sigma_vals * (1.0 + values * (1.0 - sigma_vals))


def position_table(seq_len, model_width):
    column = jnp.arange(model_width)
    freq_index = (column // 2).astype(jnp.float32)
    rates = jnp.exp(freq_index * (-2.0 * math.log(10000.0) / model_width))
    parts = 2 * seq_len // 16
    coarse = (16 * (parts // 2 - 1 - jnp.arange(parts))).astype(jnp.float32)[:, None] * rates
    fine = (15 - jnp.arange(16)).astype(jnp.float32)[:, None] * rates
    even = column % 2 == 0
    sin_c, cos_c = jnp.sin(coarse), jnp.cos(coarse)
    first, second = lax.optimization_barrier(
        (jnp.where(even, sin_c, cos_c), jnp.where(even, cos_c, -sin_c))
    )
    sin_f, cos_f = lax.optimization_barrier((jnp.sin(fine), jnp.cos(fine)))
    table = first[:, None] * cos_f[None] + second[:, None] * sin_f[None]
    return table.reshape(2 * seq_len, model_width)[: 2 * seq_len - 1].astype(jnp.bfloat16)


def piece_shapes(model_width, ff_part, att_part, chan_part, kernel_len):
    feed_list = [(model_width, ff_part), (ff_part,), (ff_part, model_width)]
    attn_list = [
        (model_width, 3 * att_part),
        (model_width, att_part),
        (att_part, model_width),
        (att_part,),
        (att_part,),
    ]
    conv_list = [
        (model_width, 2 * chan_part),
        (2 * chan_part,),
        (kernel_len, chan_part),
        (chan_part,),
        (chan_part,),
        (chan_part,),
        (chan_part, model_width),
    ]
    return feed_list + attn_list + conv_list + feed_list


def rel_shift(position):
    leading = position.shape[:-2]
    seq_len = position.shape[-2]
    span_len = position.shape[-1]
    padded = jnp.pad(position, [(0, 0)] * len(leading) + [(0, 0), (0, 1)])
    flattened = padded.reshape(leading + (seq_len * (span_len + 1),))
    flattened = flattened[..., seq_len - 1 : seq_len - 1 + seq_len * span_len]
    return flattened.reshape(leading + (seq_len, span_len))[..., :seq_len]


def rel_unshift(grad_shifted):
    leading = grad_shifted.shape[:-2]
    seq_len = grad_shifted.shape[-1]
    span_len = 2 * seq_len - 1
    widened = jnp.pad(grad_shifted, [(0, 0)] * len(leading) + [(0, 0), (0, span_len - seq_len)])
    flattened = widened.reshape(leading + (seq_len * span_len,))
    flattened = jnp.pad(flattened, [(0, 0)] * len(leading) + [(seq_len - 1, 1)])
    return flattened.reshape(leading + (seq_len, span_len + 1))[..., :span_len]


def attention_scores(query_u, query_v, keys_b, pos_rows):
    content = jnp.einsum("bihd,bjhd->bhij", query_u, keys_b, preferred_element_type=jnp.float32)
    position = jnp.einsum("bihd,rhd->bhir", query_v, pos_rows, preferred_element_type=jnp.float32)
    return (content + rel_shift(position)) * (1.0 / math.sqrt(query_u.shape[-1]))


def key_mask(seq_lengths):
    return (jnp.arange(SEQ_LEN)[None, :] < seq_lengths[:, None])[:, None, None, :]


def conv_front(valid, pre_glu, tap_weights, tap_bias):
    chan_part = pre_glu.shape[-1] // 2
    gated = pre_glu[..., :chan_part] * jax.nn.sigmoid(pre_glu[..., chan_part:]) * valid[..., None]
    kernel_len = tap_weights.shape[0]
    margin = (kernel_len - 1) // 2
    filters = tap_weights.reshape(kernel_len, 1, chan_part)
    summed = lax.conv_general_dilated(
        gated,
        filters,
        (1,),
        [(margin, kernel_len - 1 - margin)],
        dimension_numbers=("NWC", "WIO", "NWC"),
        feature_group_count=chan_part,
        precision=lax.Precision.HIGHEST,
    )
    return summed + tap_bias


def batch_apply(conv_out, gamma_vec, beta_vec, mean_vec, inv_std):
    return jax.nn.silu((conv_out - mean_vec) * inv_std * (1.0 + gamma_vec) + beta_vec)


def feed_forward(resid, w_in, b_in, w_out, scaling, offset, b_out):
    normed = layer_norm(resid, scaling, offset).astype(jnp.bfloat16)
    hidden_pre = mat_product(normed, w_in) + b_in
    hidden = jax.nn.silu(hidden_pre).astype(jnp.bfloat16)
    branch = tensor_total(mat_product(hidden, w_out)) + b_out
    return (resid + 0.5 * branch, (normed, hidden_pre, hidden))


def feed_back(d_resid, resid, saved, w_in, w_out, scaling, offset):
    normed, hidden_pre, hidden = saved
    d_branch = 0.5 * d_resid
    grad_bout = jnp.sum(d_branch, axis=0)
    branch_gradient_second = d_branch.astype(jnp.bfloat16)
    grad_wout = left_transposed_matmul(hidden, branch_gradient_second)
    d_pre = right_trans_product(branch_gradient_second, w_out) * silu_slope(hidden_pre)
    grad_bin = jnp.sum(d_pre, axis=0)
    d_pre_b = d_pre.astype(jnp.bfloat16)
    grad_win = left_transposed_matmul(normed, d_pre_b)
    d_normed = tensor_back_total(right_trans_product(d_pre_b, w_in))
    d_input, grad_scale, grad_offset = norm_back(resid, scaling, offset, d_normed)
    return (
        d_resid + d_input,
        [grad_win, grad_bin, grad_wout],
        [grad_scale, grad_offset, grad_bout],
    )


def attention_forward(resid, weights, scaling, offset, b_out, lengths, table):
    w_qkv, w_pos, w_att, bias_u, bias_v = weights
    seq_count = lengths.shape[0]
    att_part = w_att.shape[0]
    head_count = att_part // HEAD_DIM

    def to_heads(block):
        return block.reshape(seq_count, SEQ_LEN, head_count, HEAD_DIM)

    normed = layer_norm(resid, scaling, offset).astype(jnp.bfloat16)
    qkv_rows = mat_product(normed, w_qkv)
    query = qkv_rows[:, :att_part]
    query_u = to_heads((query + bias_u).astype(jnp.bfloat16))
    query_v = to_heads((query + bias_v).astype(jnp.bfloat16))
    keys_b = to_heads(qkv_rows[:, att_part : 2 * att_part].astype(jnp.bfloat16))
    values_b = to_heads(qkv_rows[:, 2 * att_part :].astype(jnp.bfloat16))
    pos_rows = (
        mat_product(table, w_pos)
        .astype(jnp.bfloat16)
        .reshape(2 * SEQ_LEN - 1, head_count, HEAD_DIM)
    )
    scores = attention_scores(query_u, query_v, keys_b, pos_rows)
    exponent = jnp.where(key_mask(lengths), jnp.exp(scores), 0.0)
    totals = jnp.sum(exponent, axis=-1)
    log_total = jnp.log(totals)
    probs = (exponent / totals[..., None]).astype(jnp.bfloat16)
    context = jnp.einsum("bhij,bjhd->bihd", probs, values_b, preferred_element_type=jnp.float32)
    context_rows_second = context.reshape(seq_count * SEQ_LEN, att_part).astype(jnp.bfloat16)
    branch = tensor_total(mat_product(context_rows_second, w_att)) + b_out
    return (
        resid + branch,
        (normed, query_u, query_v, keys_b, values_b, pos_rows, log_total, context_rows_second),
    )


def attention_back(d_resid, resid, saved, weights, scaling, offset, lengths, table):
    normed, query_u, query_v, keys_b, values_b, pos_rows, log_total, context_rows_second = saved
    w_qkv, _, w_att, _, _ = weights
    seq_count = lengths.shape[0]
    att_part = w_att.shape[0]
    rows_total = seq_count * SEQ_LEN
    scale = 1.0 / math.sqrt(HEAD_DIM)
    grad_bout = jnp.sum(d_resid, axis=0)
    branch_gradient_second = d_resid.astype(jnp.bfloat16)
    attention_weight_gradient = left_transposed_matmul(context_rows_second, branch_gradient_second)
    d_context = (
        right_trans_product(branch_gradient_second, w_att)
        .astype(jnp.bfloat16)
        .reshape(query_u.shape)
    )
    scores = attention_scores(query_u, query_v, keys_b, pos_rows)
    probs = jnp.where(key_mask(lengths), jnp.exp(scores - log_total[..., None]), 0.0)
    probs_b = probs.astype(jnp.bfloat16)
    d_values = jnp.einsum("bhij,bihd->bjhd", probs_b, d_context, preferred_element_type=jnp.float32)
    d_probs = jnp.einsum("bihd,bjhd->bhij", d_context, values_b, preferred_element_type=jnp.float32)
    row_dot = jnp.sum(probs * d_probs, axis=-1, keepdims=True)
    d_scores = (probs * (d_probs - row_dot) * scale).astype(jnp.bfloat16)
    d_query_u = jnp.einsum("bhij,bjhd->bihd", d_scores, keys_b, preferred_element_type=jnp.float32)
    d_keys = jnp.einsum("bhij,bihd->bjhd", d_scores, query_u, preferred_element_type=jnp.float32)
    d_position = rel_unshift(d_scores)
    d_query_v = jnp.einsum(
        "bhir,rhd->bihd", d_position, pos_rows, preferred_element_type=jnp.float32
    )
    d_pos_rows = jnp.einsum(
        "bhir,bihd->rhd", d_position, query_v, preferred_element_type=jnp.float32
    )
    content_bias_gradient = jnp.sum(d_query_u, axis=(0, 1)).reshape(att_part)
    position_bias_gradient = jnp.sum(d_query_v, axis=(0, 1)).reshape(att_part)
    d_query = (d_query_u + d_query_v).reshape(rows_total, att_part)
    d_qkv = jnp.concatenate(
        [d_query, d_keys.reshape(rows_total, att_part), d_values.reshape(rows_total, att_part)],
        axis=1,
    ).astype(jnp.bfloat16)
    query_key_value_weight_gradient = left_transposed_matmul(normed, d_qkv)
    position_weight_gradient = lax.dot_general(
        table.astype(jnp.float32),
        d_pos_rows.reshape(2 * SEQ_LEN - 1, att_part),
        (((0,), (0,)), ((), ())),
        precision=lax.Precision.HIGHEST,
    )
    d_normed = tensor_back_total(right_trans_product(d_qkv, w_qkv))
    d_input, grad_scale, grad_offset = norm_back(resid, scaling, offset, d_normed)
    return (
        d_resid + d_input,
        [
            query_key_value_weight_gradient,
            position_weight_gradient,
            attention_weight_gradient,
            content_bias_gradient,
            position_bias_gradient,
        ],
        [grad_scale, grad_offset, grad_bout],
    )


def conv_forward(resid, weights, scaling, offset, b_out, valid):
    w_glu, b_glu, tap_weights, tap_bias, gamma_vec, beta_vec, w_conv = weights
    seq_count = valid.shape[0]
    chan_part = w_conv.shape[0]
    normed = layer_norm(resid, scaling, offset).astype(jnp.bfloat16)
    pre_glu = (mat_product(normed, w_glu) + b_glu).reshape(seq_count, SEQ_LEN, 2 * chan_part)
    conv_out = conv_front(valid, pre_glu, tap_weights, tap_bias)
    masked = conv_out * valid[..., None]
    stats = dp_sum(
        jnp.stack(
            [
                jnp.sum(masked, axis=(0, 1)),
                jnp.sum(masked * conv_out, axis=(0, 1)),
                jnp.broadcast_to(jnp.sum(valid), (chan_part,)),
            ]
        )
    )
    first_sum, square_sum, count_all = stats[0], stats[1], stats[2]
    mean_vec = first_sum / count_all
    inv_std = lax.rsqrt(square_sum / count_all - mean_vec * mean_vec + BATCH_EPS)
    activated = (
        batch_apply(conv_out, gamma_vec, beta_vec, mean_vec, inv_std)
        .reshape(seq_count * SEQ_LEN, chan_part)
        .astype(jnp.bfloat16)
    )
    branch = tensor_total(mat_product(activated, w_conv)) + b_out
    return (resid + branch, (normed, pre_glu, conv_out, mean_vec, inv_std, count_all, activated))


def conv_back(d_resid, resid, saved, weights, scaling, offset, valid):
    normed, pre_glu, conv_out, mean_vec, inv_std, count_all, activated = saved
    w_glu, _, tap_weights, tap_bias, gamma_vec, beta_vec, w_conv = weights
    grad_bout = jnp.sum(d_resid, axis=0)
    branch_gradient_second = d_resid.astype(jnp.bfloat16)
    grad_wconv = left_transposed_matmul(activated, branch_gradient_second)
    d_act = right_trans_product(branch_gradient_second, w_conv).reshape(conv_out.shape)
    _, pull_norm = jax.vjp(batch_apply, conv_out, gamma_vec, beta_vec, mean_vec, inv_std)
    d_conv, grad_gamma, grad_beta, d_mean, d_inv = pull_norm(d_act)
    sums = dp_sum(jnp.stack([d_mean, d_inv]))
    d_mean, d_inv = sums[0], sums[1]
    d_var = -0.5 * inv_std * inv_std * inv_std * d_inv
    d_first = (d_mean - 2.0 * mean_vec * d_var) / count_all
    d_square = d_var / count_all
    d_conv = d_conv + valid[..., None] * (d_first + 2.0 * conv_out * d_square)
    _, pull_front = jax.vjp(partial(conv_front, valid), pre_glu, tap_weights, tap_bias)
    d_pre, grad_taps, grad_tbias = pull_front(d_conv)
    d_pre = d_pre.reshape(-1, d_pre.shape[-1])
    grad_bglu = jnp.sum(d_pre, axis=0)
    d_pre_b = d_pre.astype(jnp.bfloat16)
    grad_wglu = left_transposed_matmul(normed, d_pre_b)
    d_normed = tensor_back_total(right_trans_product(d_pre_b, w_glu))
    d_input, grad_scale, grad_offset = norm_back(resid, scaling, offset, d_normed)
    return (
        d_resid + d_input,
        [grad_wglu, grad_bglu, grad_taps, grad_tbias, grad_gamma, grad_beta, grad_wconv],
        [grad_scale, grad_offset, grad_bout],
    )


def layer_forward(resid, pieces, vectors, lengths, valid, table):
    resid_a, keep_a = feed_forward(
        resid, pieces[0], pieces[1], pieces[2], vectors[0], vectors[1], vectors[2]
    )
    resid_b, keep_b = attention_forward(
        resid_a, pieces[3:8], vectors[3], vectors[4], vectors[5], lengths, table
    )
    resid_c, keep_c = conv_forward(resid_b, pieces[8:15], vectors[6], vectors[7], vectors[8], valid)
    resid_d, keep_d = feed_forward(
        resid_c, pieces[15], pieces[16], pieces[17], vectors[9], vectors[10], vectors[11]
    )
    output = layer_norm(resid_d, vectors[12], vectors[13])
    return (output, (resid, resid_a, resid_b, resid_c, resid_d), (keep_a, keep_b, keep_c, keep_d))


def layer_back(d_output, pieces, vectors, lengths, valid, table, resids, keeps):
    resid, resid_a, resid_b, resid_c, resid_d = resids
    d_resid_d, grad_fscale, grad_foffset = norm_back(resid_d, vectors[12], vectors[13], d_output)
    d_resid_c, grads_d, shared_d = feed_back(
        d_resid_d, resid_c, keeps[3], pieces[15], pieces[17], vectors[9], vectors[10]
    )
    d_resid_b, grads_c, shared_c = conv_back(
        d_resid_c, resid_b, keeps[2], pieces[8:15], vectors[6], vectors[7], valid
    )
    d_resid_a, grads_b, shared_b = attention_back(
        d_resid_b, resid_a, keeps[1], pieces[3:8], vectors[3], vectors[4], lengths, table
    )
    d_resid, grads_a, shared_a = feed_back(
        d_resid_a, resid, keeps[0], pieces[0], pieces[2], vectors[0], vectors[1]
    )
    piece_grads = grads_a + grads_b + grads_c + grads_d
    vector_grads = shared_a + shared_b + shared_c + shared_d + [grad_fscale, grad_foffset]
    return (d_resid, piece_grads, vector_grads)


def adam_update(weights, first, second, gradient_list):
    first_new = BETA_ONE * first + (1.0 - BETA_ONE) * gradient_list
    second_new = BETA_TWO * second + (1.0 - BETA_TWO) * gradient_list * gradient_list
    first_hat = first_new / (1.0 - BETA_ONE**STEP_COUNT)
    second_hat = second_new / (1.0 - BETA_TWO**STEP_COUNT)
    weights_new = weights - LEARN_RATE * (
        first_hat / (jnp.sqrt(second_hat) + ADAM_EPS) + WEIGHT_DECAY * weights
    )
    return (weights_new, first_new, second_new)


def local(
    tokens,
    lengths,
    cotangent,
    params,
    shared,
    first_moment,
    second_moment,
    first_shared,
    second_shared,
):
    part_count = lax.axis_size("tensor")
    shapes = piece_shapes(
        D, FF // part_count, HEADS * HEAD_DIM // part_count, D // part_count, KERNEL
    )
    count = lax.axis_size("dp")
    plan = Plan(count, params.shape[2], shared.shape[1], shapes)
    me = lax.axis_index("dp")
    start = me * plan.shard % TILE
    where = jnp.stack([start % LANES, start // LANES, me * plan.shared_shard % LANES]).astype(
        jnp.int32
    )
    order = block_order(count)
    own = shift_out(plan, where, params.reshape(1, 1, -1), shared)
    table = position_table(SEQ_LEN, D)
    gathered, table = gather_blocks(count, own, table)
    unpacked = unpack(plan, order, gathered)
    pieces = [piece.reshape(shape) for piece, shape in zip(unpacked[:-1], shapes)]
    vectors = [unpacked[-1][at] for at in range(14)]
    valid = (jnp.arange(SEQ_LEN)[None, :] < lengths[:, None]).astype(F32)
    resid = tokens.astype(F32)
    result, resids, keeps = layer_forward(resid, pieces, vectors, lengths, valid, table)
    d_resid, piece_grads, vector_grads = layer_back(
        cotangent, pieces, vectors, lengths, valid, table, resids, keeps
    )
    blocks = pack(plan, order, piece_grads, jnp.stack(vector_grads))
    (
        grad_params,
        new_params,
        new_first,
        new_second,
        grad_shared,
        new_shared,
        new_first_sh,
        new_second_sh,
    ) = finish(
        plan,
        where,
        scatter_blocks(count, blocks),
        (params, first_moment, second_moment),
        (shared, first_shared, second_shared),
    )
    return (
        result,
        d_resid,
        grad_params,
        grad_shared,
        new_params,
        new_shared,
        new_first,
        new_second,
        new_first_sh,
        new_second_sh,
    )


def solution(mesh):
    in_specs = (
        P("dp", None),
        P("dp"),
        P("dp", None),
        P(None, "tensor", "dp"),
        P(None, "dp"),
        P(None, "tensor", "dp"),
        P(None, "tensor", "dp"),
        P(None, "dp"),
        P(None, "dp"),
    )
    out_specs = (
        P("dp", None),
        P("dp", None),
        P(None, "tensor", "dp"),
        P(None, "dp"),
        P(None, "tensor", "dp"),
        P(None, "dp"),
        P(None, "tensor", "dp"),
        P(None, "tensor", "dp"),
        P(None, "dp"),
        P(None, "dp"),
    )
    return jax.shard_map(local, mesh=mesh, in_specs=in_specs, out_specs=out_specs, check_vma=False)
```

```python
from functools import partial
import math

import jax
import jax.numpy as jnp
from jax import lax
from jax.experimental import pallas as pl
from jax.experimental.pallas import tpu as pltpu
from jax.sharding import PartitionSpec as P


D = 512
FF = 2048
HEADS = 8
HEAD_DIM = 64
KERNEL = 31
SEQ_LEN = 128


NORM_EPS = 1e-05
BATCH_EPS = 1e-05
LEARN_RATE = 0.02
BETA_ONE = 0.9
BETA_TWO = 0.999
ADAM_EPS = 1e-08
WEIGHT_DECAY = 0.1
STEP_COUNT = 5
FLOAT_PIECES = (1, 6, 7, 9, 10, 11, 12, 13, 16)

LANES = 128
TILE = 16 * LANES
SHARED_ROWS = 16
BF16 = jnp.bfloat16
F32 = jnp.float32
ANY = pl.BlockSpec(memory_space=pl.ANY)
VMEM = pl.BlockSpec(memory_space=pltpu.VMEM)
SMEM = pl.BlockSpec(memory_space=pltpu.SMEM)


def round_up(value, multiple):
    return -(-value // multiple) * multiple


class Plan:
    def __init__(self, count, shard, shared_shard, shapes):
        self.count = count
        self.shard = shard
        self.shared_shard = shared_shard
        self.shapes = shapes
        self.rows_in = round_up(shard // LANES + 2, 8)
        self.rows = round_up(self.rows_in + 16, 16)
        self.block = self.rows + SHARED_ROWS
        self.half = self.block * 4 // 11 // 16 * 16
        self.sizes = (self.half, self.block - self.half)
        self.flat_rows = count * shard // LANES
        self.alloc_rows = round_up(((count - 1) * shard // TILE) * 16 + self.rows, 16)
        self.shared_rows = count * shared_shard // LANES
        self.bases = []
        at = 0
        for shape in shapes:
            self.bases.append(at // LANES)
            at += math.prod(shape)


def as_matrix(shape):
    return shape if len(shape) == 2 else (1, shape[0])


def split_flat(length):
    return [
        (at // LANES, slice(at, min(at + LANES, length)), min(LANES, length - at))
        for at in range(0, length, LANES)
    ]


def shift_body(plan, where_ref, x_ref, s_ref, a_ref, b_ref, rows_scr, scr):
    low, row, low_shared = where_ref[0], where_ref[1], where_ref[2]
    rows_in, rows = plan.rows_in, plan.rows
    whole = plan.shard // 1024

    def load(at, carry):
        part = x_ref[0, :, pl.ds(pl.multiple_of(at * 1024, 1024), 1024)]
        rows_scr[pl.ds(pl.multiple_of(at * 8, 8), 8), :] = part.reshape(8, LANES)
        return carry

    lax.fori_loop(0, whole, load, 0, unroll=4)
    rows_scr[whole * 8 :, :] = jnp.zeros((rows_in - whole * 8, LANES), F32)
    for at, cols, lanes in split_flat(plan.shard):
        if at >= whole * 8:
            rows_scr[at : at + 1, 0:lanes] = x_ref[0, :, cols]
    scr[rows - 32 :, :] = jnp.zeros((32, LANES), F32)
    scr[0:16, :] = jnp.zeros((16, LANES), F32)
    lane = lax.broadcasted_iota(jnp.int32, (rows_in, LANES), 1)
    rolled = pltpu.roll(rows_scr[...], low, 1)
    scr[pl.ds(row, rows_in), :] = jnp.where(lane >= low, rolled, 0.0)
    scr[pl.ds(row + rows_in, 1), :] = jnp.zeros((1, LANES), F32)
    scr[pl.ds(row + 1, rows_in), :] += jnp.where(lane < low, rolled, 0.0)
    half = plan.half
    a_ref[...] = scr[0:half, :].astype(BF16)
    b_ref[0 : rows - half, :] = scr[half:, :].astype(BF16)
    rows_scr[0:8, :] = jnp.zeros((8, LANES), F32)
    for at, cols, lanes in split_flat(plan.shared_shard):
        rows_scr[at : at + 1, 0:lanes] = s_ref[:, cols]
    lane = lax.broadcasted_iota(jnp.int32, (8, LANES), 1)
    rolled = pltpu.roll(rows_scr[0:8, :], low_shared, 1)
    scr[0:16, :] = jnp.zeros((16, LANES), F32)
    scr[0:8, :] = jnp.where(lane >= low_shared, rolled, 0.0)
    scr[1:9, :] += jnp.where(lane < low_shared, rolled, 0.0)
    b_ref[rows - half : rows - half + 16, :] = scr[0:16, :].astype(BF16)


def shift_out(plan, where, flat, shared):
    return pl.pallas_call(
        partial(shift_body, plan),
        out_shape=[jax.ShapeDtypeStruct((size, LANES), BF16) for size in plan.sizes],
        in_specs=[SMEM, VMEM, VMEM],
        out_specs=[VMEM] * 2,
        scratch_shapes=[
            pltpu.VMEM((plan.rows_in, LANES), F32),
            pltpu.VMEM((plan.rows, LANES), F32),
        ],
        name="shift_out",
    )(where, flat, shared)


def finish_body(plan, n_in, where_ref, *refs):
    blocks = refs[:n_in]
    p_ref, m_ref, v_ref, ps_ref, ms_ref, vs_ref = refs[n_in : n_in + 6]
    outs = refs[n_in + 6 : n_in + 14]
    acc, rows_scr = refs[n_in + 14 :]
    low, row, low_shared = where_ref[0], where_ref[1], where_ref[2]
    rows_in, rows = plan.rows_in, plan.rows
    each = n_in // 2
    for at, rows_of in enumerate((slice(0, plan.half), slice(plan.half, plan.block))):
        parts = [block[...].astype(F32) for block in blocks[at * each : at * each + each]]
        acc[rows_of, :] = sum(parts[1:], parts[0])
    lane = lax.broadcasted_iota(jnp.int32, (rows_in, LANES), 1)
    back = lax.rem(LANES - low, LANES)
    first = pltpu.roll(acc[pl.ds(row, rows_in), :], back, 1)
    second = pltpu.roll(acc[pl.ds(row + 1, rows_in), :], back, 1)
    rows_scr[...] = jnp.where(lane < LANES - low, first, second)

    def update(grad, at, ins, out):
        weights, one, two = (ref[at] for ref in ins)
        for ref, value in zip(out, (grad,) + adam_update(weights, one, two, grad)):
            ref[at] = value

    main_in, main_out = (p_ref, m_ref, v_ref), outs[0:4]
    whole = plan.shard // 1024

    def step(at, carry):
        grad = rows_scr[pl.ds(pl.multiple_of(at * 8, 8), 8), :].reshape(1, 1024)
        cols = pl.ds(pl.multiple_of(at * 1024, 1024), 1024)
        update(grad, (0, slice(None), cols), main_in, main_out)
        return carry

    lax.fori_loop(0, whole, step, 0, unroll=4)
    for at, cols, lanes in split_flat(plan.shard):
        if at >= whole * 8:
            update(rows_scr[at : at + 1, 0:lanes], (0, slice(None), cols), main_in, main_out)
    lane = lax.broadcasted_iota(jnp.int32, (8, LANES), 1)
    back = lax.rem(LANES - low_shared, LANES)
    first = pltpu.roll(acc[rows : rows + 8, :], back, 1)
    second = pltpu.roll(acc[rows + 1 : rows + 9, :], back, 1)
    rows_scr[0:8, :] = jnp.where(lane < LANES - low_shared, first, second)
    for at, cols, lanes in split_flat(plan.shared_shard):
        update(
            rows_scr[at : at + 1, 0:lanes],
            (slice(None), cols),
            (ps_ref, ms_ref, vs_ref),
            outs[4:8],
        )


def finish(plan, where, blocks, flats, shareds):
    flat = jax.ShapeDtypeStruct(flats[0].shape, F32)
    shared = jax.ShapeDtypeStruct(shareds[0].shape, F32)
    return pl.pallas_call(
        partial(finish_body, plan, len(blocks)),
        out_shape=[flat] * 4 + [shared] * 4,
        in_specs=[SMEM] + [VMEM] * (len(blocks) + 6),
        out_specs=[VMEM] * 8,
        scratch_shapes=[
            pltpu.VMEM((plan.block, LANES), F32),
            pltpu.VMEM((plan.rows_in, LANES), F32),
        ],
        name="finish",
    )(where, *blocks, *flats, *shareds)


def chunked(total):
    step = total
    while step > 128 and step % 2 == 0:
        step //= 2
    return step


def largest_step(total, limit):
    return max(step for step in range(1, limit + 1) if total % step == 0)


def widen(plan, first, second, owner, origin, flat):
    full = plan.shard // TILE
    start = pl.multiple_of((owner * plan.shard) // TILE * 16 - origin, 16)
    edge = plan.half // 16
    for src, begin, end, base in ((first, 1, edge, 0), (second, edge, full, edge)):
        step = largest_step(end - begin, 25)

        def move(k, carry, src=src, begin=begin, base=base, step=step):
            to = pl.multiple_of(start + begin * 16 + k * (step * 16), 16)
            frm = pl.multiple_of((begin - base) * 16 + k * (step * 16), 16)
            flat[pl.ds(to, step * 16), :] = src[pl.ds(frm, step * 16), :].astype(F32)
            return carry

        lax.fori_loop(0, (end - begin) // step, move, 0)
    for src, at, tile in (
        (first, 0, 0),
        (second, full - edge, full),
        (second, full + 1 - edge, full + 1),
    ):
        rows = pl.ds(pl.multiple_of(start + tile * 16, 16), 16)
        flat[rows, :] += src[at * 16 : at * 16 + 16, :].astype(F32)


def unpack_body(plan, which, n_in, low, high, with_shared, idx_ref, *refs):
    ins = refs[:n_in]
    outs = refs[n_in : n_in + len(which)]
    flat, shf = refs[-2:]
    origin = low * plan.shard // TILE * 16
    full = plan.shard // TILE
    zero = jnp.zeros((16, LANES), F32)
    for at in range(low, high + 1):
        start = at * plan.shard // TILE * 16 - origin
        for tile in (0, full, full + 1):
            flat[start + tile * 16 : start + tile * 16 + 16, :] = zero
    for at in range(plan.count):
        if n_in > 2:
            owner, first, second = idx_ref[at], ins[2 * at], ins[2 * at + 1]
        else:
            owner, first, second = at, ins[0].at[at], ins[1].at[at]

        widen(plan, first, second, owner, origin, flat)

    for at, out in zip(which, outs):
        base = plan.bases[at] - origin
        rows, width = as_matrix(plan.shapes[at])
        cols = width // LANES
        step = chunked(rows)
        for col in range(cols):
            span = slice(col * LANES, (col + 1) * LANES)
            if rows == 1:
                out[:, span] = flat[base + col : base + col + 1, :].astype(out.dtype)
            elif step == rows:
                out[:, span] = flat[pl.ds(base + col, rows, stride=cols), :].astype(out.dtype)
            else:

                def move(k, carry, col=col, base=base, cols=cols, step=step, out=out, span=span):
                    frm = pl.multiple_of(k * (step * cols), 8) + (base + col)
                    to = pl.multiple_of(k * step, step)
                    part = flat[pl.ds(frm, step, stride=cols), :]
                    out[pl.ds(to, step), span] = part.astype(out.dtype)
                    return carry

                lax.fori_loop(0, rows // step, move, 0)
    if with_shared:
        shared_out = refs[-3]
        shf[...] = jnp.zeros_like(shf)
        for at in range(plan.count):
            owner, second = (idx_ref[at], ins[2 * at + 1]) if n_in > 2 else (at, ins[1].at[at])
            rows = pl.ds((owner * plan.shared_shard) // LANES, 16)
            frm = plan.rows - plan.half
            shf[rows, :] += second[frm : frm + 16, :].astype(F32)
        cols = D // LANES
        for col in range(cols):
            shared_out[:, col * LANES : (col + 1) * LANES] = shf[pl.ds(col, 14, stride=cols), :]


def unpack(plan, idx, blocks, which, with_shared):
    low = plan.bases[which[0]] * LANES // plan.shard
    last = plan.bases[which[-1]] * LANES + math.prod(plan.shapes[which[-1]]) - 1
    high = last // plan.shard
    rows = high * plan.shard // TILE * 16 + plan.rows - low * plan.shard // TILE * 16
    outs = [
        jax.ShapeDtypeStruct(as_matrix(plan.shapes[at]), F32 if at in FLOAT_PIECES else BF16)
        for at in which
    ]
    if with_shared:
        outs.append(jax.ShapeDtypeStruct((14, D), F32))
    return pl.pallas_call(
        partial(unpack_body, plan, tuple(which), len(blocks), low, high, with_shared),
        out_shape=outs,
        in_specs=[SMEM] + [VMEM] * len(blocks),
        out_specs=[VMEM] * len(outs),
        scratch_shapes=[
            pltpu.VMEM((rows, LANES), F32),
            pltpu.VMEM((plan.shared_rows + 16, LANES), F32),
        ],
        compiler_params=pltpu.CompilerParams(vmem_limit_bytes=48 * 1024 * 1024),
        cost_estimate=pl.CostEstimate(
            flops=0, bytes_accessed=rows * 2048, transcendentals=0
        ),
    )(idx, *blocks)


def largest_step(total, limit):
    return max(step for step in range(1, limit + 1) if total % step == 0)


def pack_body(plan, idx_ref, *refs):
    n_in = len(plan.shapes) + 1
    ins = refs[:n_in]
    outs = refs[n_in : n_in + 2 * plan.count]
    flat, shf = refs[n_in + 2 * plan.count :]
    tail = plan.flat_rows // 8 * 8
    flat[tail:, :] = jnp.zeros((plan.alloc_rows - tail, LANES), F32)
    for shape, base, src in zip(plan.shapes, plan.bases, ins):
        rows, width = as_matrix(shape)
        cols = width // LANES
        step = chunked(rows)
        for col in range(cols):
            if step == rows:
                part = src[:, col * LANES : (col + 1) * LANES].astype(F32)
                if rows == 1:
                    flat[base + col : base + col + 1, :] = part
                else:
                    flat[pl.ds(base + col, rows, stride=cols), :] = part
            else:

                def move(k, carry, col=col, base=base, cols=cols, step=step, src=src):
                    at = pl.multiple_of(k * (step * cols), 8) + (base + col)
                    frm = pl.multiple_of(k * step, step)
                    flat[pl.ds(at, step, stride=cols), :] = src[
                        pl.ds(frm, step), col * LANES : (col + 1) * LANES
                    ].astype(F32)
                    return carry

                lax.fori_loop(0, rows // step, move, 0)
    shf[...] = jnp.zeros_like(shf)
    cols = D // LANES
    for col in range(cols):
        shf[pl.ds(col, 14, stride=cols), :] = ins[-1][:, col * LANES : (col + 1) * LANES]

    half = plan.half
    for at in range(plan.count):
        owner = idx_ref[at]
        start = pl.multiple_of((owner * plan.shard) // TILE * 16, 16)
        for out, begin, end in ((outs[2 * at], 0, half), (outs[2 * at + 1], half, plan.rows)):
            step = 16 * largest_step((end - begin) // 16, 25)

            def move(k, carry, out=out, begin=begin, step=step, start=start):
                to = pl.multiple_of(k * step, 16)
                frm = pl.multiple_of(start + begin + k * step, 16)
                out[pl.ds(to, step), :] = flat[pl.ds(frm, step), :].astype(BF16)
                return carry

            lax.fori_loop(0, (end - begin) // step, move, 0)
        rows = pl.ds((owner * plan.shared_shard) // LANES, 16)
        outs[2 * at + 1][plan.rows - half : plan.block - half, :] = shf[rows, :].astype(BF16)


def pack(plan, idx, piece_grads, shared_grad):
    pieces = [
        grad.reshape(as_matrix(shape)).astype(F32 if at in FLOAT_PIECES else BF16)
        for at, (grad, shape) in enumerate(zip(piece_grads, plan.shapes))
    ]
    halves = [jax.ShapeDtypeStruct((size, LANES), BF16) for size in plan.sizes]
    return pl.pallas_call(
        partial(pack_body, plan),
        out_shape=halves * plan.count,
        in_specs=[SMEM] + [VMEM] * (len(pieces) + 1),
        out_specs=[VMEM] * (2 * plan.count),
        scratch_shapes=[
            pltpu.VMEM((plan.alloc_rows, LANES), F32),
            pltpu.VMEM((plan.shared_rows + 16, LANES), F32),
        ],
        compiler_params=pltpu.CompilerParams(vmem_limit_bytes=48 * 1024 * 1024),
        name="pack",
    )(idx, *pieces, shared_grad)


def permute(value, count, target, axis="dp"):
    return lax.ppermute(value, axis, [(at, target(at)) for at in range(count)])


def gray(value):
    return value ^ (value >> 1)


def z_next(at):
    return gray((gray(at // 4) + 1) % 4) * 4 + at % 4


def block_order(count):
    me = lax.axis_index("dp")
    if count != 16:
        return jnp.arange(count, dtype=jnp.int32)
    z, x, core = me // 4, (me // 2) % 2, me % 2
    order = []
    for back in range(4):
        for flip_x in range(2):
            for flip_core in range(2):
                order.append(
                    gray((gray(z) + 4 - back) % 4) * 4 + (x ^ flip_x) * 2 + (core ^ flip_core)
                )
    return jnp.stack(order).astype(jnp.int32)


def across_core(value):
    return permute(value, 16, lambda at: at ^ 1)


def across_x(value):
    return permute(value, 16, lambda at: at ^ 2)


def along_z(value):
    return permute(value, 16, z_next)


def gather_blocks(count, own, alongside):
    if count != 16:
        return [lax.all_gather(half, "dp", axis=0) for half in own], alongside
    ring = [[half] for half in own]
    column = [[], []]
    for step in range(3):
        for part in range(2):
            upcoming, other = along_z(ring[part][-1]), across_x(ring[part][-1])
            if step == 0 and part == 0:
                upcoming, other, alongside = lax.optimization_barrier(
                    (upcoming, other, alongside)
                )
            elif part == 0:
                upcoming, other = lax.optimization_barrier((upcoming, other))
            else:
                upcoming, other, _ = lax.optimization_barrier((upcoming, other, ring[0][-1]))
            ring[part].append(upcoming)
            column[part].append(other)
    column[0].append(across_x(ring[0][3]))
    column[1].append(along_z(column[1][2]))
    blocks = []
    for step in range(4):
        for side in (ring, column):
            mine = [side[0][step], side[1][step]]
            blocks += mine + [across_core(half) for half in mine]
    return blocks, alongside


def add_blocks(*blocks):
    return sum(block.astype(F32) for block in blocks).astype(BF16)


def scatter_blocks(count, blocks):
    if count != 16:
        return [
            lax.psum_scatter(
                jnp.stack(blocks[part::2]).astype(F32), "dp", scatter_dimension=0, tiled=False
            )
            for part in range(2)
        ]

    def pair(back, flip_x, part):
        at = (back * 4 + flip_x * 2) * 2 + part
        return [blocks[at], across_core(blocks[at + 2])]

    sent = [pair(1, 1, part) for part in range(2)]
    *blocks, sent[0][1], sent[1][1] = lax.optimization_barrier((*blocks, sent[0][1], sent[1][1]))
    moved = (across_x(add_blocks(*sent[0])), along_z(add_blocks(*sent[1])))
    running = [add_blocks(*pair(1, 0, 0), moved[0]), add_blocks(*pair(1, 0, 1))]
    far = [add_blocks(*pair(2, 1, 0)), add_blocks(*pair(2, 1, 1), moved[1])]
    final, before = [], moved[0]
    for back in (2, 3, 0):
        for part in range(2):
            arrived, other, before = lax.optimization_barrier(
                (along_z(running[part]), across_x(far[part]), before)
            )
            before = arrived
            if back == 0:
                final += pair(0, 0, part) + [other, arrived]
                continue
            running[part] = add_blocks(*pair(back, 0, part), other, arrived)
            far[part] = add_blocks(*pair((back + 1) % 4, 1, part))
    return final


def dp_sum(value):
    count = lax.axis_size("dp")
    bit = 1
    while bit < count:
        steps = [bit, 2 * bit, 3 * bit] if 4 * bit <= count else [bit]
        parts = [permute(value, count, lambda at, step=step: at ^ step) for step in steps]
        value = sum(parts, value)
        bit *= 4 if len(steps) == 3 else 2
    return value


def tensor_total(partial_sum):
    own = partial_sum.astype(BF16)
    other = permute(own, lax.axis_size("tensor"), lambda at: at ^ 1, "tensor")
    return own.astype(F32) + other.astype(F32)


def mat_product(left, right):
    return jnp.dot(left, right, preferred_element_type=jnp.float32)


def left_transposed_matmul(left, right):
    return lax.dot_general(
        left, right, (((0,), (0,)), ((), ())), preferred_element_type=jnp.float32
    )


def right_trans_product(left, right):
    return lax.dot_general(
        left, right, (((1,), (1,)), ((), ())), preferred_element_type=jnp.float32
    )


def layer_norm(values, scaling, offset):
    centred = values - jnp.mean(values, axis=-1, keepdims=True)
    spread = jnp.mean(centred * centred, axis=-1, keepdims=True)
    return centred * lax.rsqrt(spread + NORM_EPS) * (1.0 + scaling) + offset


def norm_back(values, scaling, offset, d_output):
    _, pull_back = jax.vjp(layer_norm, values, scaling, offset)
    return pull_back(d_output)


def silu_slope(values):
    sigma_vals = jax.nn.sigmoid(values)
    return sigma_vals * (1.0 + values * (1.0 - sigma_vals))


def position_table(seq_len, model_width):
    column = jnp.arange(model_width)
    freq_index = (column // 2).astype(jnp.float32)
    rates = jnp.exp(freq_index * (-2.0 * math.log(10000.0) / model_width))
    parts = 2 * seq_len // 16
    coarse = (16 * (parts // 2 - 1 - jnp.arange(parts))).astype(jnp.float32)[:, None] * rates
    fine = (15 - jnp.arange(16)).astype(jnp.float32)[:, None] * rates
    even = column % 2 == 0
    sin_c, cos_c = jnp.sin(coarse), jnp.cos(coarse)
    first, second = lax.optimization_barrier(
        (jnp.where(even, sin_c, cos_c), jnp.where(even, cos_c, -sin_c))
    )
    sin_f, cos_f = lax.optimization_barrier((jnp.sin(fine), jnp.cos(fine)))
    table = first[:, None] * cos_f[None] + second[:, None] * sin_f[None]
    return table.reshape(2 * seq_len, model_width)[: 2 * seq_len - 1].astype(jnp.bfloat16)


def piece_shapes(model_width, ff_part, att_part, chan_part, kernel_len):
    feed_list = [(model_width, ff_part), (ff_part,), (ff_part, model_width)]
    attn_list = [
        (model_width, 3 * att_part),
        (model_width, att_part),
        (att_part, model_width),
        (att_part,),
        (att_part,),
    ]
    conv_list = [
        (model_width, 2 * chan_part),
        (2 * chan_part,),
        (kernel_len, chan_part),
        (chan_part,),
        (chan_part,),
        (chan_part,),
        (chan_part, model_width),
    ]
    return feed_list + attn_list + conv_list + feed_list


def rel_shift(position):
    leading = position.shape[:-2]
    seq_len = position.shape[-2]
    span_len = position.shape[-1]
    padded = jnp.pad(position, [(0, 0)] * len(leading) + [(0, 0), (0, 1)])
    flattened = padded.reshape(leading + (seq_len * (span_len + 1),))
    flattened = flattened[..., seq_len - 1 : seq_len - 1 + seq_len * span_len]
    return flattened.reshape(leading + (seq_len, span_len))[..., :seq_len]


def rel_unshift(grad_shifted):
    leading = grad_shifted.shape[:-2]
    seq_len = grad_shifted.shape[-1]
    span_len = 2 * seq_len - 1
    widened = jnp.pad(grad_shifted, [(0, 0)] * len(leading) + [(0, 0), (0, span_len - seq_len)])
    flattened = widened.reshape(leading + (seq_len * span_len,))
    flattened = jnp.pad(flattened, [(0, 0)] * len(leading) + [(seq_len - 1, 1)])
    return flattened.reshape(leading + (seq_len, span_len + 1))[..., :span_len]


def attention_scores(query_u, query_v, keys_b, pos_rows):
    content = jnp.einsum("bihd,bjhd->bhij", query_u, keys_b, preferred_element_type=jnp.float32)
    position = jnp.einsum("bihd,rhd->bhir", query_v, pos_rows, preferred_element_type=jnp.float32)
    return (content + rel_shift(position)) * (1.0 / math.sqrt(query_u.shape[-1]))


def key_mask(seq_lengths):
    return (jnp.arange(SEQ_LEN)[None, :] < seq_lengths[:, None])[:, None, None, :]


def conv_front(valid, pre_glu, tap_weights, tap_bias):
    chan_part = pre_glu.shape[-1] // 2
    gated = pre_glu[..., :chan_part] * jax.nn.sigmoid(pre_glu[..., chan_part:]) * valid[..., None]
    kernel_len = tap_weights.shape[0]
    margin = (kernel_len - 1) // 2
    filters = tap_weights.reshape(kernel_len, 1, chan_part)
    summed = lax.conv_general_dilated(
        gated,
        filters,
        (1,),
        [(margin, kernel_len - 1 - margin)],
        dimension_numbers=("NWC", "WIO", "NWC"),
        feature_group_count=chan_part,
        precision=lax.Precision.HIGHEST,
    )
    return summed + tap_bias


def batch_apply(conv_out, gamma_vec, beta_vec, mean_vec, inv_std):
    return jax.nn.silu((conv_out - mean_vec) * inv_std * (1.0 + gamma_vec) + beta_vec)


def feed_forward(resid, w_in, b_in, w_out, scaling, offset, b_out):
    normed = layer_norm(resid, scaling, offset).astype(jnp.bfloat16)
    hidden_pre = mat_product(normed, w_in) + b_in
    hidden = jax.nn.silu(hidden_pre).astype(jnp.bfloat16)
    branch = tensor_total(mat_product(hidden, w_out)) + b_out
    return (resid + 0.5 * branch, (normed, hidden_pre, hidden))


def feed_back(d_resid, resid, saved, w_in, w_out, scaling, offset):
    normed, hidden_pre, hidden = saved
    d_branch = 0.5 * d_resid
    grad_bout = jnp.sum(d_branch, axis=0)
    branch_gradient_second = d_branch.astype(jnp.bfloat16)
    grad_wout = left_transposed_matmul(hidden, branch_gradient_second)
    d_pre = right_trans_product(branch_gradient_second, w_out) * silu_slope(hidden_pre)
    grad_bin = jnp.sum(d_pre, axis=0)
    d_pre_b = d_pre.astype(jnp.bfloat16)
    grad_win = left_transposed_matmul(normed, d_pre_b)
    d_normed = tensor_total(right_trans_product(d_pre_b, w_in))
    d_input, grad_scale, grad_offset = norm_back(resid, scaling, offset, d_normed)
    return (
        d_resid + d_input,
        [grad_win, grad_bin, grad_wout],
        [grad_scale, grad_offset, grad_bout],
    )


def attention_forward(resid, weights, scaling, offset, b_out, lengths, table):
    w_qkv, w_pos, w_att, bias_u, bias_v = weights
    seq_count = lengths.shape[0]
    att_part = w_att.shape[0]
    head_count = att_part // HEAD_DIM

    def to_heads(block):
        return block.reshape(seq_count, SEQ_LEN, head_count, HEAD_DIM)

    normed = layer_norm(resid, scaling, offset).astype(jnp.bfloat16)
    qkv_rows = mat_product(normed, w_qkv)
    query = qkv_rows[:, :att_part]
    query_u = to_heads((query + bias_u).astype(jnp.bfloat16))
    query_v = to_heads((query + bias_v).astype(jnp.bfloat16))
    keys_b = to_heads(qkv_rows[:, att_part : 2 * att_part].astype(jnp.bfloat16))
    values_b = to_heads(qkv_rows[:, 2 * att_part :].astype(jnp.bfloat16))
    pos_rows = (
        mat_product(table, w_pos)
        .astype(jnp.bfloat16)
        .reshape(2 * SEQ_LEN - 1, head_count, HEAD_DIM)
    )
    scores = attention_scores(query_u, query_v, keys_b, pos_rows)
    exponent = jnp.where(key_mask(lengths), jnp.exp(scores), 0.0)
    totals = jnp.sum(exponent, axis=-1)
    log_total = jnp.log(totals)
    probs = (exponent / totals[..., None]).astype(jnp.bfloat16)
    context = jnp.einsum("bhij,bjhd->bihd", probs, values_b, preferred_element_type=jnp.float32)
    context_rows_second = context.reshape(seq_count * SEQ_LEN, att_part).astype(jnp.bfloat16)
    branch = tensor_total(mat_product(context_rows_second, w_att)) + b_out
    return (
        resid + branch,
        (normed, query_u, query_v, keys_b, values_b, pos_rows, log_total, context_rows_second),
    )


def attention_back(d_resid, resid, saved, weights, scaling, offset, lengths, table):
    normed, query_u, query_v, keys_b, values_b, pos_rows, log_total, context_rows_second = saved
    w_qkv, _, w_att, _, _ = weights
    seq_count = lengths.shape[0]
    att_part = w_att.shape[0]
    rows_total = seq_count * SEQ_LEN
    scale = 1.0 / math.sqrt(HEAD_DIM)
    grad_bout = jnp.sum(d_resid, axis=0)
    branch_gradient_second = d_resid.astype(jnp.bfloat16)
    attention_weight_gradient = left_transposed_matmul(context_rows_second, branch_gradient_second)
    d_context = (
        right_trans_product(branch_gradient_second, w_att)
        .astype(jnp.bfloat16)
        .reshape(query_u.shape)
    )
    scores = attention_scores(query_u, query_v, keys_b, pos_rows)
    probs = jnp.where(key_mask(lengths), jnp.exp(scores - log_total[..., None]), 0.0)
    probs_b = probs.astype(jnp.bfloat16)
    d_values = jnp.einsum("bhij,bihd->bjhd", probs_b, d_context, preferred_element_type=jnp.float32)
    d_probs = jnp.einsum("bihd,bjhd->bhij", d_context, values_b, preferred_element_type=jnp.float32)
    row_dot = jnp.sum(probs * d_probs, axis=-1, keepdims=True)
    d_scores = (probs * (d_probs - row_dot) * scale).astype(jnp.bfloat16)
    d_query_u = jnp.einsum("bhij,bjhd->bihd", d_scores, keys_b, preferred_element_type=jnp.float32)
    d_keys = jnp.einsum("bhij,bihd->bjhd", d_scores, query_u, preferred_element_type=jnp.float32)
    d_position = rel_unshift(d_scores)
    d_query_v = jnp.einsum(
        "bhir,rhd->bihd", d_position, pos_rows, preferred_element_type=jnp.float32
    )
    d_pos_rows = jnp.einsum(
        "bhir,bihd->rhd", d_position, query_v, preferred_element_type=jnp.float32
    )
    content_bias_gradient = jnp.sum(d_query_u, axis=(0, 1)).reshape(att_part)
    position_bias_gradient = jnp.sum(d_query_v, axis=(0, 1)).reshape(att_part)
    d_query = (d_query_u + d_query_v).reshape(rows_total, att_part)
    d_qkv = jnp.concatenate(
        [d_query, d_keys.reshape(rows_total, att_part), d_values.reshape(rows_total, att_part)],
        axis=1,
    ).astype(jnp.bfloat16)
    query_key_value_weight_gradient = left_transposed_matmul(normed, d_qkv)
    position_weight_gradient = lax.dot_general(
        table.astype(jnp.float32),
        d_pos_rows.reshape(2 * SEQ_LEN - 1, att_part),
        (((0,), (0,)), ((), ())),
        precision=lax.Precision.HIGHEST,
    )
    d_normed = tensor_total(right_trans_product(d_qkv, w_qkv))
    d_input, grad_scale, grad_offset = norm_back(resid, scaling, offset, d_normed)
    return (
        d_resid + d_input,
        [
            query_key_value_weight_gradient,
            position_weight_gradient,
            attention_weight_gradient,
            content_bias_gradient,
            position_bias_gradient,
        ],
        [grad_scale, grad_offset, grad_bout],
    )


def conv_forward(resid, weights, scaling, offset, b_out, valid):
    w_glu, b_glu, tap_weights, tap_bias, gamma_vec, beta_vec, w_conv = weights
    seq_count = valid.shape[0]
    chan_part = w_conv.shape[0]
    normed = layer_norm(resid, scaling, offset).astype(jnp.bfloat16)
    pre_glu = (mat_product(normed, w_glu) + b_glu).reshape(seq_count, SEQ_LEN, 2 * chan_part)
    conv_out = conv_front(valid, pre_glu, tap_weights, tap_bias)
    masked = conv_out * valid[..., None]
    stats = dp_sum(
        jnp.stack(
            [
                jnp.sum(masked, axis=(0, 1)),
                jnp.sum(masked * conv_out, axis=(0, 1)),
                jnp.broadcast_to(jnp.sum(valid), (chan_part,)),
            ]
        )
    )
    first_sum, square_sum, count_all = stats[0], stats[1], stats[2]
    mean_vec = first_sum / count_all
    inv_std = lax.rsqrt(square_sum / count_all - mean_vec * mean_vec + BATCH_EPS)
    activated = (
        batch_apply(conv_out, gamma_vec, beta_vec, mean_vec, inv_std)
        .reshape(seq_count * SEQ_LEN, chan_part)
        .astype(jnp.bfloat16)
    )
    branch = tensor_total(mat_product(activated, w_conv)) + b_out
    return (resid + branch, (normed, pre_glu, conv_out, mean_vec, inv_std, count_all, activated))


def conv_back(d_resid, resid, saved, weights, scaling, offset, valid):
    normed, pre_glu, conv_out, mean_vec, inv_std, count_all, activated = saved
    w_glu, _, tap_weights, tap_bias, gamma_vec, beta_vec, w_conv = weights
    grad_bout = jnp.sum(d_resid, axis=0)
    branch_gradient_second = d_resid.astype(jnp.bfloat16)
    grad_wconv = left_transposed_matmul(activated, branch_gradient_second)
    d_act = right_trans_product(branch_gradient_second, w_conv).reshape(conv_out.shape)
    _, pull_norm = jax.vjp(batch_apply, conv_out, gamma_vec, beta_vec, mean_vec, inv_std)
    d_conv, grad_gamma, grad_beta, d_mean, d_inv = pull_norm(d_act)
    sums = dp_sum(jnp.stack([d_mean, d_inv]))
    d_mean, d_inv = sums[0], sums[1]
    d_var = -0.5 * inv_std * inv_std * inv_std * d_inv
    d_first = (d_mean - 2.0 * mean_vec * d_var) / count_all
    d_square = d_var / count_all
    d_conv = d_conv + valid[..., None] * (d_first + 2.0 * conv_out * d_square)
    _, pull_front = jax.vjp(partial(conv_front, valid), pre_glu, tap_weights, tap_bias)
    d_pre, grad_taps, grad_tbias = pull_front(d_conv)
    d_pre = d_pre.reshape(-1, d_pre.shape[-1])
    grad_bglu = jnp.sum(d_pre, axis=0)
    d_pre_b = d_pre.astype(jnp.bfloat16)
    grad_wglu = left_transposed_matmul(normed, d_pre_b)
    d_normed = tensor_total(right_trans_product(d_pre_b, w_glu))
    d_input, grad_scale, grad_offset = norm_back(resid, scaling, offset, d_normed)
    return (
        d_resid + d_input,
        [grad_wglu, grad_bglu, grad_taps, grad_tbias, grad_gamma, grad_beta, grad_wconv],
        [grad_scale, grad_offset, grad_bout],
    )


def layer_forward(resid, pieces, vectors, lengths, valid, table):
    resid_a, keep_a = feed_forward(
        resid, pieces[0], pieces[1], pieces[2], vectors[0], vectors[1], vectors[2]
    )
    resid_b, keep_b = attention_forward(
        resid_a, pieces[3:8], vectors[3], vectors[4], vectors[5], lengths, table
    )
    resid_c, keep_c = conv_forward(resid_b, pieces[8:15], vectors[6], vectors[7], vectors[8], valid)
    resid_d, keep_d = feed_forward(
        resid_c, pieces[15], pieces[16], pieces[17], vectors[9], vectors[10], vectors[11]
    )
    output = layer_norm(resid_d, vectors[12], vectors[13])
    return (output, (resid, resid_a, resid_b, resid_c, resid_d), (keep_a, keep_b, keep_c, keep_d))


def layer_back(d_output, pieces, vectors, lengths, valid, table, resids, keeps):
    resid, resid_a, resid_b, resid_c, resid_d = resids
    d_resid_d, grad_fscale, grad_foffset = norm_back(resid_d, vectors[12], vectors[13], d_output)
    d_resid_c, grads_d, shared_d = feed_back(
        d_resid_d, resid_c, keeps[3], pieces[15], pieces[17], vectors[9], vectors[10]
    )
    d_resid_b, grads_c, shared_c = conv_back(
        d_resid_c, resid_b, keeps[2], pieces[8:15], vectors[6], vectors[7], valid
    )
    d_resid_a, grads_b, shared_b = attention_back(
        d_resid_b, resid_a, keeps[1], pieces[3:8], vectors[3], vectors[4], lengths, table
    )
    d_resid, grads_a, shared_a = feed_back(
        d_resid_a, resid, keeps[0], pieces[0], pieces[2], vectors[0], vectors[1]
    )
    piece_grads = grads_a + grads_b + grads_c + grads_d
    vector_grads = shared_a + shared_b + shared_c + shared_d + [grad_fscale, grad_foffset]
    return (d_resid, piece_grads, vector_grads)


def adam_update(weights, first, second, gradient_list):
    first_new = BETA_ONE * first + (1.0 - BETA_ONE) * gradient_list
    second_new = BETA_TWO * second + (1.0 - BETA_TWO) * gradient_list * gradient_list
    first_hat = first_new / (1.0 - BETA_ONE**STEP_COUNT)
    second_hat = second_new / (1.0 - BETA_TWO**STEP_COUNT)
    weights_new = weights - LEARN_RATE * (
        first_hat / (jnp.sqrt(second_hat) + ADAM_EPS) + WEIGHT_DECAY * weights
    )
    return (weights_new, first_new, second_new)


def local(
    tokens,
    lengths,
    cotangent,
    params,
    shared,
    first_moment,
    second_moment,
    first_shared,
    second_shared,
):
    part_count = lax.axis_size("tensor")
    shapes = piece_shapes(
        D, FF // part_count, HEADS * HEAD_DIM // part_count, D // part_count, KERNEL
    )
    count = lax.axis_size("dp")
    plan = Plan(count, params.shape[2], shared.shape[1], shapes)
    me = lax.axis_index("dp")
    start = me * plan.shard % TILE
    where = jnp.stack([start % LANES, start // LANES, me * plan.shared_shard % LANES]).astype(
        jnp.int32
    )
    order = block_order(count)
    own = shift_out(plan, where, params.reshape(1, 1, -1), shared)
    table = position_table(SEQ_LEN, D)
    gathered, table = gather_blocks(count, own, table)
    *unpacked, vector_rows = unpack(plan, order, gathered, range(len(shapes)), True)
    pieces = [piece.reshape(shape) for piece, shape in zip(unpacked, shapes)]
    vectors = [vector_rows[at] for at in range(14)]
    valid = (jnp.arange(SEQ_LEN)[None, :] < lengths[:, None]).astype(F32)
    resid = tokens.astype(F32)
    result, resids, keeps = layer_forward(resid, pieces, vectors, lengths, valid, table)
    d_resid, piece_grads, vector_grads = layer_back(
        cotangent, pieces, vectors, lengths, valid, table, resids, keeps
    )
    blocks = pack(plan, order, piece_grads, jnp.stack(vector_grads))
    (
        grad_params,
        new_params,
        new_first,
        new_second,
        grad_shared,
        new_shared,
        new_first_sh,
        new_second_sh,
    ) = finish(
        plan,
        where,
        scatter_blocks(count, blocks),
        (params, first_moment, second_moment),
        (shared, first_shared, second_shared),
    )
    return (
        result,
        d_resid,
        grad_params,
        grad_shared,
        new_params,
        new_shared,
        new_first,
        new_second,
        new_first_sh,
        new_second_sh,
    )


def solution(mesh):
    in_specs = (
        P("dp", None),
        P("dp"),
        P("dp", None),
        P(None, "tensor", "dp"),
        P(None, "dp"),
        P(None, "tensor", "dp"),
        P(None, "tensor", "dp"),
        P(None, "dp"),
        P(None, "dp"),
    )
    out_specs = (
        P("dp", None),
        P("dp", None),
        P(None, "tensor", "dp"),
        P(None, "dp"),
        P(None, "tensor", "dp"),
        P(None, "dp"),
        P(None, "tensor", "dp"),
        P(None, "tensor", "dp"),
        P(None, "dp"),
        P(None, "dp"),
    )
    return jax.shard_map(local, mesh=mesh, in_specs=in_specs, out_specs=out_specs, check_vma=False)
```

```python
from functools import partial
import math

import jax
import jax.numpy as jnp
from jax import lax
from jax.experimental import pallas as pl
from jax.experimental.pallas import tpu as pltpu
from jax.sharding import PartitionSpec as P


D = 512
FF = 2048
HEADS = 8
HEAD_DIM = 64
KERNEL = 31
SEQ_LEN = 128


NORM_EPS = 1e-05
BATCH_EPS = 1e-05
LEARN_RATE = 0.02
BETA_ONE = 0.9
BETA_TWO = 0.999
ADAM_EPS = 1e-08
WEIGHT_DECAY = 0.1
STEP_COUNT = 5
FLOAT_PIECES = (1, 6, 7, 9, 10, 11, 12, 13, 16)

LANES = 128
TILE = 16 * LANES
SHARED_ROWS = 16
BF16 = jnp.bfloat16
F32 = jnp.float32
ANY = pl.BlockSpec(memory_space=pl.ANY)
VMEM = pl.BlockSpec(memory_space=pltpu.VMEM)
SMEM = pl.BlockSpec(memory_space=pltpu.SMEM)


def round_up(value, multiple):
    return -(-value // multiple) * multiple


class Plan:
    def __init__(self, count, shard, shared_shard, shapes):
        self.count = count
        self.shard = shard
        self.shared_shard = shared_shard
        self.shapes = shapes
        self.rows_in = round_up(shard // LANES + 2, 8)
        self.rows = round_up(self.rows_in + 16, 16)
        self.block = self.rows + SHARED_ROWS
        self.half = self.block * 4 // 11 // 16 * 16
        self.sizes = (self.half, self.block - self.half)
        self.flat_rows = count * shard // LANES
        self.alloc_rows = round_up(((count - 1) * shard // TILE) * 16 + self.rows, 16)
        self.shared_rows = count * shared_shard // LANES
        self.bases = []
        at = 0
        for shape in shapes:
            self.bases.append(at // LANES)
            at += math.prod(shape)


def as_matrix(shape):
    return shape if len(shape) == 2 else (1, shape[0])


def split_flat(length):
    return [
        (at // LANES, slice(at, min(at + LANES, length)), min(LANES, length - at))
        for at in range(0, length, LANES)
    ]


def shift_body(plan, where_ref, x_ref, s_ref, a_ref, b_ref, rows_scr, scr):
    low, row, low_shared = where_ref[0], where_ref[1], where_ref[2]
    rows_in, rows = plan.rows_in, plan.rows
    whole = plan.shard // 1024

    def load(at, carry):
        part = x_ref[0, :, pl.ds(pl.multiple_of(at * 1024, 1024), 1024)]
        rows_scr[pl.ds(pl.multiple_of(at * 8, 8), 8), :] = part.reshape(8, LANES)
        return carry

    lax.fori_loop(0, whole, load, 0, unroll=12)
    rows_scr[whole * 8 :, :] = jnp.zeros((rows_in - whole * 8, LANES), F32)
    for at, cols, lanes in split_flat(plan.shard):
        if at >= whole * 8:
            rows_scr[at : at + 1, 0:lanes] = x_ref[0, :, cols]
    scr[rows - 32 :, :] = jnp.zeros((32, LANES), F32)
    scr[0:16, :] = jnp.zeros((16, LANES), F32)
    lane = lax.broadcasted_iota(jnp.int32, (rows_in, LANES), 1)
    rolled = pltpu.roll(rows_scr[...], low, 1)
    scr[pl.ds(row, rows_in), :] = jnp.where(lane >= low, rolled, 0.0)
    scr[pl.ds(row + rows_in, 1), :] = jnp.zeros((1, LANES), F32)
    scr[pl.ds(row + 1, rows_in), :] += jnp.where(lane < low, rolled, 0.0)
    half = plan.half
    a_ref[...] = scr[0:half, :].astype(BF16)
    b_ref[0 : rows - half, :] = scr[half:, :].astype(BF16)
    rows_scr[0:8, :] = jnp.zeros((8, LANES), F32)
    for at, cols, lanes in split_flat(plan.shared_shard):
        rows_scr[at : at + 1, 0:lanes] = s_ref[:, cols]
    lane = lax.broadcasted_iota(jnp.int32, (8, LANES), 1)
    rolled = pltpu.roll(rows_scr[0:8, :], low_shared, 1)
    scr[0:16, :] = jnp.zeros((16, LANES), F32)
    scr[0:8, :] = jnp.where(lane >= low_shared, rolled, 0.0)
    scr[1:9, :] += jnp.where(lane < low_shared, rolled, 0.0)
    b_ref[rows - half : rows - half + 16, :] = scr[0:16, :].astype(BF16)


def shift_out(plan, where, flat, shared):
    return pl.pallas_call(
        partial(shift_body, plan),
        out_shape=[jax.ShapeDtypeStruct((size, LANES), BF16) for size in plan.sizes],
        in_specs=[SMEM, VMEM, VMEM],
        out_specs=[VMEM] * 2,
        scratch_shapes=[
            pltpu.VMEM((plan.rows_in, LANES), F32),
            pltpu.VMEM((plan.rows, LANES), F32),
        ],
        name="shift_out",
    )(where, flat, shared)


def finish_body(plan, n_in, where_ref, *refs):
    blocks = refs[:n_in]
    p_ref, m_ref, v_ref, ps_ref, ms_ref, vs_ref = refs[n_in : n_in + 6]
    outs = refs[n_in + 6 : n_in + 14]
    acc, rows_scr = refs[n_in + 14 :]
    low, row, low_shared = where_ref[0], where_ref[1], where_ref[2]
    rows_in, rows = plan.rows_in, plan.rows
    each = n_in // 2
    for at, rows_of in enumerate((slice(0, plan.half), slice(plan.half, plan.block))):
        parts = [block[...].astype(F32) for block in blocks[at * each : at * each + each]]
        acc[rows_of, :] = sum(parts[1:], parts[0])
    lane = lax.broadcasted_iota(jnp.int32, (rows_in, LANES), 1)
    back = lax.rem(LANES - low, LANES)
    first = pltpu.roll(acc[pl.ds(row, rows_in), :], back, 1)
    second = pltpu.roll(acc[pl.ds(row + 1, rows_in), :], back, 1)
    rows_scr[...] = jnp.where(lane < LANES - low, first, second)

    def update(grad, at, ins, out):
        weights, one, two = (ref[at] for ref in ins)
        for ref, value in zip(out, (grad,) + adam_update(weights, one, two, grad)):
            ref[at] = value

    main_in, main_out = (p_ref, m_ref, v_ref), outs[0:4]
    whole = plan.shard // 1024

    def step(at, carry):
        grad = rows_scr[pl.ds(pl.multiple_of(at * 8, 8), 8), :].reshape(1, 1024)
        cols = pl.ds(pl.multiple_of(at * 1024, 1024), 1024)
        update(grad, (0, slice(None), cols), main_in, main_out)
        return carry

    lax.fori_loop(0, whole, step, 0, unroll=24)
    for at, cols, lanes in split_flat(plan.shard):
        if at >= whole * 8:
            update(rows_scr[at : at + 1, 0:lanes], (0, slice(None), cols), main_in, main_out)
    lane = lax.broadcasted_iota(jnp.int32, (8, LANES), 1)
    back = lax.rem(LANES - low_shared, LANES)
    first = pltpu.roll(acc[rows : rows + 8, :], back, 1)
    second = pltpu.roll(acc[rows + 1 : rows + 9, :], back, 1)
    rows_scr[0:8, :] = jnp.where(lane < LANES - low_shared, first, second)
    for at, cols, lanes in split_flat(plan.shared_shard):
        update(
            rows_scr[at : at + 1, 0:lanes],
            (slice(None), cols),
            (ps_ref, ms_ref, vs_ref),
            outs[4:8],
        )


def finish(plan, where, blocks, flats, shareds):
    flat = jax.ShapeDtypeStruct(flats[0].shape, F32)
    shared = jax.ShapeDtypeStruct(shareds[0].shape, F32)
    return pl.pallas_call(
        partial(finish_body, plan, len(blocks)),
        out_shape=[flat] * 4 + [shared] * 4,
        in_specs=[SMEM] + [VMEM] * (len(blocks) + 6),
        out_specs=[VMEM] * 8,
        scratch_shapes=[
            pltpu.VMEM((plan.block, LANES), F32),
            pltpu.VMEM((plan.rows_in, LANES), F32),
        ],
        name="finish",
    )(where, *blocks, *flats, *shareds)


def chunked(total):
    step = total
    while step > 256 and step % 2 == 0:
        step //= 2
    return step


def largest_step(total, limit):
    return max(step for step in range(1, limit + 1) if total % step == 0)


def widen(plan, first, second, owner, origin, flat):
    full = plan.shard // TILE
    start = pl.multiple_of((owner * plan.shard) // TILE * 16 - origin, 16)
    edge = plan.half // 16
    for src, begin, end, base in ((first, 1, edge, 0), (second, edge, full, edge)):
        step = largest_step(end - begin, 35)

        def move(k, carry, src=src, begin=begin, base=base, step=step):
            to = pl.multiple_of(start + begin * 16 + k * (step * 16), 16)
            frm = pl.multiple_of((begin - base) * 16 + k * (step * 16), 16)
            flat[pl.ds(to, step * 16), :] = src[pl.ds(frm, step * 16), :].astype(F32)
            return carry

        lax.fori_loop(0, (end - begin) // step, move, 0)
    for src, at, tile in (
        (first, 0, 0),
        (second, full - edge, full),
        (second, full + 1 - edge, full + 1),
    ):
        rows = pl.ds(pl.multiple_of(start + tile * 16, 16), 16)
        flat[rows, :] += src[at * 16 : at * 16 + 16, :].astype(F32)


def unpack_body(plan, which, n_in, low, high, with_shared, idx_ref, *refs):
    ins = refs[:n_in]
    outs = refs[n_in : n_in + len(which)]
    flat, shf = refs[-2:]
    origin = low * plan.shard // TILE * 16
    full = plan.shard // TILE
    zero = jnp.zeros((16, LANES), F32)
    for at in range(low, high + 1):
        start = at * plan.shard // TILE * 16 - origin
        for tile in (0, full, full + 1):
            flat[start + tile * 16 : start + tile * 16 + 16, :] = zero
    for at in range(plan.count):
        if n_in > 2:
            owner, first, second = idx_ref[at], ins[2 * at], ins[2 * at + 1]
        else:
            owner, first, second = at, ins[0].at[at], ins[1].at[at]

        widen(plan, first, second, owner, origin, flat)

    for at, out in zip(which, outs):
        base = plan.bases[at] - origin
        rows, width = as_matrix(plan.shapes[at])
        cols = width // LANES
        step = chunked(rows)
        for col in range(cols):
            span = slice(col * LANES, (col + 1) * LANES)
            if rows == 1:
                out[:, span] = flat[base + col : base + col + 1, :].astype(out.dtype)
            elif step == rows:
                out[:, span] = flat[pl.ds(base + col, rows, stride=cols), :].astype(out.dtype)
            else:

                def move(k, carry, col=col, base=base, cols=cols, step=step, out=out, span=span):
                    frm = pl.multiple_of(k * (step * cols), 8) + (base + col)
                    to = pl.multiple_of(k * step, step)
                    part = flat[pl.ds(frm, step, stride=cols), :]
                    out[pl.ds(to, step), span] = part.astype(out.dtype)
                    return carry

                lax.fori_loop(0, rows // step, move, 0)
    if with_shared:
        shared_out = refs[-3]
        shf[...] = jnp.zeros_like(shf)
        for at in range(plan.count):
            owner, second = (idx_ref[at], ins[2 * at + 1]) if n_in > 2 else (at, ins[1].at[at])
            rows = pl.ds((owner * plan.shared_shard) // LANES, 16)
            frm = plan.rows - plan.half
            shf[rows, :] += second[frm : frm + 16, :].astype(F32)
        cols = D // LANES
        for col in range(cols):
            shared_out[:, col * LANES : (col + 1) * LANES] = shf[pl.ds(col, 14, stride=cols), :]


def unpack(plan, idx, blocks, which, with_shared):
    low = plan.bases[which[0]] * LANES // plan.shard
    last = plan.bases[which[-1]] * LANES + math.prod(plan.shapes[which[-1]]) - 1
    high = last // plan.shard
    rows = high * plan.shard // TILE * 16 + plan.rows - low * plan.shard // TILE * 16
    outs = [
        jax.ShapeDtypeStruct(as_matrix(plan.shapes[at]), F32 if at in FLOAT_PIECES else BF16)
        for at in which
    ]
    if with_shared:
        outs.append(jax.ShapeDtypeStruct((14, D), F32))
    return pl.pallas_call(
        partial(unpack_body, plan, tuple(which), len(blocks), low, high, with_shared),
        out_shape=outs,
        in_specs=[SMEM] + [VMEM] * len(blocks),
        out_specs=[VMEM] * len(outs),
        scratch_shapes=[
            pltpu.VMEM((rows, LANES), F32),
            pltpu.VMEM((plan.shared_rows + 16, LANES), F32),
        ],
        compiler_params=pltpu.CompilerParams(vmem_limit_bytes=48 * 1024 * 1024),
        cost_estimate=pl.CostEstimate(
            flops=0, bytes_accessed=rows * 2048, transcendentals=0
        ),
    )(idx, *blocks)


def largest_step(total, limit):
    return max(step for step in range(1, limit + 1) if total % step == 0)


def pack_body(plan, idx_ref, *refs):
    n_in = len(plan.shapes) + 1
    ins = refs[:n_in]
    outs = refs[n_in : n_in + 2 * plan.count]
    flat, shf = refs[n_in + 2 * plan.count :]
    tail = plan.flat_rows // 8 * 8
    flat[tail:, :] = jnp.zeros((plan.alloc_rows - tail, LANES), F32)
    for shape, base, src in zip(plan.shapes, plan.bases, ins):
        rows, width = as_matrix(shape)
        cols = width // LANES
        step = chunked(rows)
        for col in range(cols):
            if step == rows:
                part = src[:, col * LANES : (col + 1) * LANES].astype(F32)
                if rows == 1:
                    flat[base + col : base + col + 1, :] = part
                else:
                    flat[pl.ds(base + col, rows, stride=cols), :] = part
            else:

                def move(k, carry, col=col, base=base, cols=cols, step=step, src=src):
                    at = pl.multiple_of(k * (step * cols), 8) + (base + col)
                    frm = pl.multiple_of(k * step, step)
                    flat[pl.ds(at, step, stride=cols), :] = src[
                        pl.ds(frm, step), col * LANES : (col + 1) * LANES
                    ].astype(F32)
                    return carry

                lax.fori_loop(0, rows // step, move, 0)
    shf[...] = jnp.zeros_like(shf)
    cols = D // LANES
    for col in range(cols):
        shf[pl.ds(col, 14, stride=cols), :] = ins[-1][:, col * LANES : (col + 1) * LANES]

    half = plan.half
    for at in range(plan.count):
        owner = idx_ref[at]
        start = pl.multiple_of((owner * plan.shard) // TILE * 16, 16)
        for out, begin, end in ((outs[2 * at], 0, half), (outs[2 * at + 1], half, plan.rows)):
            step = 16 * largest_step((end - begin) // 16, 36)

            def move(k, carry, out=out, begin=begin, step=step, start=start):
                to = pl.multiple_of(k * step, 16)
                frm = pl.multiple_of(start + begin + k * step, 16)
                out[pl.ds(to, step), :] = flat[pl.ds(frm, step), :].astype(BF16)
                return carry

            lax.fori_loop(0, (end - begin) // step, move, 0)
        rows = pl.ds((owner * plan.shared_shard) // LANES, 16)
        outs[2 * at + 1][plan.rows - half : plan.block - half, :] = shf[rows, :].astype(BF16)


def pack(plan, idx, piece_grads, shared_grad):
    pieces = [
        grad.reshape(as_matrix(shape)).astype(F32 if at in FLOAT_PIECES else BF16)
        for at, (grad, shape) in enumerate(zip(piece_grads, plan.shapes))
    ]
    halves = [jax.ShapeDtypeStruct((size, LANES), BF16) for size in plan.sizes]
    return pl.pallas_call(
        partial(pack_body, plan),
        out_shape=halves * plan.count,
        in_specs=[SMEM] + [VMEM] * (len(pieces) + 1),
        out_specs=[VMEM] * (2 * plan.count),
        scratch_shapes=[
            pltpu.VMEM((plan.alloc_rows, LANES), F32),
            pltpu.VMEM((plan.shared_rows + 16, LANES), F32),
        ],
        compiler_params=pltpu.CompilerParams(vmem_limit_bytes=48 * 1024 * 1024),
        name="pack",
    )(idx, *pieces, shared_grad)


def permute(value, count, target, axis="dp"):
    return lax.ppermute(value, axis, [(at, target(at)) for at in range(count)])


def gray(value):
    return value ^ (value >> 1)


def z_next(at):
    return gray((gray(at // 4) + 1) % 4) * 4 + at % 4


def block_order(count):
    me = lax.axis_index("dp")
    if count != 16:
        return jnp.arange(count, dtype=jnp.int32)
    z, x, core = me // 4, (me // 2) % 2, me % 2
    order = []
    for back in range(4):
        for flip_x in range(2):
            for flip_core in range(2):
                order.append(
                    gray((gray(z) + 4 - back) % 4) * 4 + (x ^ flip_x) * 2 + (core ^ flip_core)
                )
    return jnp.stack(order).astype(jnp.int32)


def across_core(value):
    return permute(value, 16, lambda at: at ^ 1)


def across_x(value):
    return permute(value, 16, lambda at: at ^ 2)


def along_z(value):
    return permute(value, 16, z_next)


def gather_blocks(count, own, alongside):
    if count != 16:
        return [lax.all_gather(half, "dp", axis=0) for half in own], alongside
    ring = [[half] for half in own]
    column = [[], []]
    for step in range(3):
        for part in range(2):
            upcoming, other = along_z(ring[part][-1]), across_x(ring[part][-1])
            if step == 0 and part == 0:
                upcoming, other, alongside = lax.optimization_barrier(
                    (upcoming, other, alongside)
                )
            elif part == 0:
                upcoming, other = lax.optimization_barrier((upcoming, other))
            else:
                upcoming, other, _ = lax.optimization_barrier((upcoming, other, ring[0][-1]))
            ring[part].append(upcoming)
            column[part].append(other)
    column[0].append(across_x(ring[0][3]))
    column[1].append(along_z(column[1][2]))
    blocks = []
    for step in range(4):
        for side in (ring, column):
            mine = [side[0][step], side[1][step]]
            blocks += mine + [across_core(half) for half in mine]
    return blocks, alongside


def add_blocks(*blocks):
    return sum(block.astype(F32) for block in blocks).astype(BF16)


def scatter_blocks(count, blocks):
    if count != 16:
        return [
            lax.psum_scatter(
                jnp.stack(blocks[part::2]).astype(F32), "dp", scatter_dimension=0, tiled=False
            )
            for part in range(2)
        ]

    def pair(back, flip_x, part):
        at = (back * 4 + flip_x * 2) * 2 + part
        return [blocks[at], across_core(blocks[at + 2])]

    sent = [pair(1, 1, part) for part in range(2)]
    *blocks, sent[0][1], sent[1][1] = lax.optimization_barrier((*blocks, sent[0][1], sent[1][1]))
    moved = (across_x(add_blocks(*sent[0])), along_z(add_blocks(*sent[1])))
    running = [add_blocks(*pair(1, 0, 0), moved[0]), add_blocks(*pair(1, 0, 1))]
    far = [add_blocks(*pair(2, 1, 0)), add_blocks(*pair(2, 1, 1), moved[1])]
    final, before = [], moved[0]
    for back in (2, 3, 0):
        for part in range(2):
            arrived, other, before = lax.optimization_barrier(
                (along_z(running[part]), across_x(far[part]), before)
            )
            before = arrived
            if back == 0:
                final += pair(0, 0, part) + [other, arrived]
                continue
            running[part] = add_blocks(*pair(back, 0, part), other, arrived)
            far[part] = add_blocks(*pair((back + 1) % 4, 1, part))
    return final


def dp_sum(value):
    count = lax.axis_size("dp")
    bit = 1
    while bit < count:
        steps = [bit, 2 * bit, 3 * bit] if 4 * bit <= count else [bit]
        parts = [permute(value, count, lambda at, step=step: at ^ step) for step in steps]
        value = sum(parts, value)
        bit *= 4 if len(steps) == 3 else 2
    return value


def tensor_total(partial_sum):
    own = partial_sum.astype(BF16)
    other = permute(own, lax.axis_size("tensor"), lambda at: at ^ 1, "tensor")
    return own.astype(F32) + other.astype(F32)


def mat_product(left, right):
    return jnp.dot(left, right, preferred_element_type=jnp.float32)


def left_transposed_matmul(left, right):
    return lax.dot_general(
        left, right, (((0,), (0,)), ((), ())), preferred_element_type=jnp.float32
    )


def right_trans_product(left, right):
    return lax.dot_general(
        left, right, (((1,), (1,)), ((), ())), preferred_element_type=jnp.float32
    )


def layer_norm(values, scaling, offset):
    centred = values - jnp.mean(values, axis=-1, keepdims=True)
    spread = jnp.mean(centred * centred, axis=-1, keepdims=True)
    return centred * lax.rsqrt(spread + NORM_EPS) * (1.0 + scaling) + offset


def norm_back(values, scaling, offset, d_output):
    _, pull_back = jax.vjp(layer_norm, values, scaling, offset)
    return pull_back(d_output)


def silu_slope(values):
    sigma_vals = jax.nn.sigmoid(values)
    return sigma_vals * (1.0 + values * (1.0 - sigma_vals))


def position_table(seq_len, model_width):
    column = jnp.arange(model_width)
    freq_index = (column // 2).astype(jnp.float32)
    rates = jnp.exp(freq_index * (-2.0 * math.log(10000.0) / model_width))
    parts = 2 * seq_len // 16
    coarse = (16 * (parts // 2 - 1 - jnp.arange(parts))).astype(jnp.float32)[:, None] * rates
    fine = (15 - jnp.arange(16)).astype(jnp.float32)[:, None] * rates
    even = column % 2 == 0
    sin_c, cos_c = jnp.sin(coarse), jnp.cos(coarse)
    first, second = lax.optimization_barrier(
        (jnp.where(even, sin_c, cos_c), jnp.where(even, cos_c, -sin_c))
    )
    sin_f, cos_f = lax.optimization_barrier((jnp.sin(fine), jnp.cos(fine)))
    table = first[:, None] * cos_f[None] + second[:, None] * sin_f[None]
    return table.reshape(2 * seq_len, model_width)[: 2 * seq_len - 1].astype(jnp.bfloat16)


def piece_shapes(model_width, ff_part, att_part, chan_part, kernel_len):
    feed_list = [(model_width, ff_part), (ff_part,), (ff_part, model_width)]
    attn_list = [
        (model_width, 3 * att_part),
        (model_width, att_part),
        (att_part, model_width),
        (att_part,),
        (att_part,),
    ]
    conv_list = [
        (model_width, 2 * chan_part),
        (2 * chan_part,),
        (kernel_len, chan_part),
        (chan_part,),
        (chan_part,),
        (chan_part,),
        (chan_part, model_width),
    ]
    return feed_list + attn_list + conv_list + feed_list


def rel_shift(position):
    leading = position.shape[:-2]
    seq_len = position.shape[-2]
    span_len = position.shape[-1]
    padded = jnp.pad(position, [(0, 0)] * len(leading) + [(0, 0), (0, 1)])
    flattened = padded.reshape(leading + (seq_len * (span_len + 1),))
    flattened = flattened[..., seq_len - 1 : seq_len - 1 + seq_len * span_len]
    return flattened.reshape(leading + (seq_len, span_len))[..., :seq_len]


def rel_unshift(grad_shifted):
    leading = grad_shifted.shape[:-2]
    seq_len = grad_shifted.shape[-1]
    span_len = 2 * seq_len - 1
    widened = jnp.pad(grad_shifted, [(0, 0)] * len(leading) + [(0, 0), (0, span_len - seq_len)])
    flattened = widened.reshape(leading + (seq_len * span_len,))
    flattened = jnp.pad(flattened, [(0, 0)] * len(leading) + [(seq_len - 1, 1)])
    return flattened.reshape(leading + (seq_len, span_len + 1))[..., :span_len]


def attention_scores(query_u, query_v, keys_b, pos_rows):
    content = jnp.einsum("bihd,bjhd->bhij", query_u, keys_b, preferred_element_type=jnp.float32)
    position = jnp.einsum("bihd,rhd->bhir", query_v, pos_rows, preferred_element_type=jnp.float32)
    return (content + rel_shift(position)) * (1.0 / math.sqrt(query_u.shape[-1]))


def key_mask(seq_lengths):
    return (jnp.arange(SEQ_LEN)[None, :] < seq_lengths[:, None])[:, None, None, :]


def conv_front(valid, pre_glu, tap_weights, tap_bias):
    chan_part = pre_glu.shape[-1] // 2
    gated = pre_glu[..., :chan_part] * jax.nn.sigmoid(pre_glu[..., chan_part:]) * valid[..., None]
    kernel_len = tap_weights.shape[0]
    margin = (kernel_len - 1) // 2
    filters = tap_weights.reshape(kernel_len, 1, chan_part)
    summed = lax.conv_general_dilated(
        gated,
        filters,
        (1,),
        [(margin, kernel_len - 1 - margin)],
        dimension_numbers=("NWC", "WIO", "NWC"),
        feature_group_count=chan_part,
        precision=lax.Precision.HIGHEST,
    )
    return summed + tap_bias


def batch_apply(conv_out, gamma_vec, beta_vec, mean_vec, inv_std):
    return jax.nn.silu((conv_out - mean_vec) * inv_std * (1.0 + gamma_vec) + beta_vec)


def feed_forward(resid, w_in, b_in, w_out, scaling, offset, b_out):
    normed = layer_norm(resid, scaling, offset).astype(jnp.bfloat16)
    hidden_pre = mat_product(normed, w_in) + b_in
    hidden = jax.nn.silu(hidden_pre).astype(jnp.bfloat16)
    branch = tensor_total(mat_product(hidden, w_out)) + b_out
    return (resid + 0.5 * branch, (normed, hidden_pre, hidden))


def feed_back(d_resid, resid, saved, w_in, w_out, scaling, offset):
    normed, hidden_pre, hidden = saved
    d_branch = 0.5 * d_resid
    grad_bout = jnp.sum(d_branch, axis=0)
    branch_gradient_second = d_branch.astype(jnp.bfloat16)
    grad_wout = left_transposed_matmul(hidden, branch_gradient_second)
    d_pre = right_trans_product(branch_gradient_second, w_out) * silu_slope(hidden_pre)
    grad_bin = jnp.sum(d_pre, axis=0)
    d_pre_b = d_pre.astype(jnp.bfloat16)
    grad_win = left_transposed_matmul(normed, d_pre_b)
    d_normed = tensor_total(right_trans_product(d_pre_b, w_in))
    d_input, grad_scale, grad_offset = norm_back(resid, scaling, offset, d_normed)
    return (
        d_resid + d_input,
        [grad_win, grad_bin, grad_wout],
        [grad_scale, grad_offset, grad_bout],
    )


def attention_forward(resid, weights, scaling, offset, b_out, lengths, table):
    w_qkv, w_pos, w_att, bias_u, bias_v = weights
    seq_count = lengths.shape[0]
    att_part = w_att.shape[0]
    head_count = att_part // HEAD_DIM

    def to_heads(block):
        return block.reshape(seq_count, SEQ_LEN, head_count, HEAD_DIM)

    normed = layer_norm(resid, scaling, offset).astype(jnp.bfloat16)
    qkv_rows = mat_product(normed, w_qkv)
    query = qkv_rows[:, :att_part]
    query_u = to_heads((query + bias_u).astype(jnp.bfloat16))
    query_v = to_heads((query + bias_v).astype(jnp.bfloat16))
    keys_b = to_heads(qkv_rows[:, att_part : 2 * att_part].astype(jnp.bfloat16))
    values_b = to_heads(qkv_rows[:, 2 * att_part :].astype(jnp.bfloat16))
    pos_rows = (
        mat_product(table, w_pos)
        .astype(jnp.bfloat16)
        .reshape(2 * SEQ_LEN - 1, head_count, HEAD_DIM)
    )
    scores = attention_scores(query_u, query_v, keys_b, pos_rows)
    exponent = jnp.where(key_mask(lengths), jnp.exp(scores), 0.0)
    totals = jnp.sum(exponent, axis=-1)
    log_total = jnp.log(totals)
    probs = (exponent / totals[..., None]).astype(jnp.bfloat16)
    context = jnp.einsum("bhij,bjhd->bihd", probs, values_b, preferred_element_type=jnp.float32)
    context_rows_second = context.reshape(seq_count * SEQ_LEN, att_part).astype(jnp.bfloat16)
    branch = tensor_total(mat_product(context_rows_second, w_att)) + b_out
    return (
        resid + branch,
        (normed, query_u, query_v, keys_b, values_b, pos_rows, log_total, context_rows_second),
    )


def attention_back(d_resid, resid, saved, weights, scaling, offset, lengths, table):
    normed, query_u, query_v, keys_b, values_b, pos_rows, log_total, context_rows_second = saved
    w_qkv, _, w_att, _, _ = weights
    seq_count = lengths.shape[0]
    att_part = w_att.shape[0]
    rows_total = seq_count * SEQ_LEN
    scale = 1.0 / math.sqrt(HEAD_DIM)
    grad_bout = jnp.sum(d_resid, axis=0)
    branch_gradient_second = d_resid.astype(jnp.bfloat16)
    attention_weight_gradient = left_transposed_matmul(context_rows_second, branch_gradient_second)
    d_context = (
        right_trans_product(branch_gradient_second, w_att)
        .astype(jnp.bfloat16)
        .reshape(query_u.shape)
    )
    scores = attention_scores(query_u, query_v, keys_b, pos_rows)
    probs = jnp.where(key_mask(lengths), jnp.exp(scores - log_total[..., None]), 0.0)
    probs_b = probs.astype(jnp.bfloat16)
    d_values = jnp.einsum("bhij,bihd->bjhd", probs_b, d_context, preferred_element_type=jnp.float32)
    d_probs = jnp.einsum("bihd,bjhd->bhij", d_context, values_b, preferred_element_type=jnp.float32)
    row_dot = jnp.sum(probs * d_probs, axis=-1, keepdims=True)
    d_scores = (probs * (d_probs - row_dot) * scale).astype(jnp.bfloat16)
    d_query_u = jnp.einsum("bhij,bjhd->bihd", d_scores, keys_b, preferred_element_type=jnp.float32)
    d_keys = jnp.einsum("bhij,bihd->bjhd", d_scores, query_u, preferred_element_type=jnp.float32)
    d_position = rel_unshift(d_scores)
    d_query_v = jnp.einsum(
        "bhir,rhd->bihd", d_position, pos_rows, preferred_element_type=jnp.float32
    )
    d_pos_rows = jnp.einsum(
        "bhir,bihd->rhd", d_position, query_v, preferred_element_type=jnp.float32
    )
    content_bias_gradient = jnp.sum(d_query_u, axis=(0, 1)).reshape(att_part)
    position_bias_gradient = jnp.sum(d_query_v, axis=(0, 1)).reshape(att_part)
    d_query = (d_query_u + d_query_v).reshape(rows_total, att_part)
    d_qkv = jnp.concatenate(
        [d_query, d_keys.reshape(rows_total, att_part), d_values.reshape(rows_total, att_part)],
        axis=1,
    ).astype(jnp.bfloat16)
    query_key_value_weight_gradient = left_transposed_matmul(normed, d_qkv)
    position_weight_gradient = lax.dot_general(
        table.astype(jnp.float32),
        d_pos_rows.reshape(2 * SEQ_LEN - 1, att_part),
        (((0,), (0,)), ((), ())),
        precision=lax.Precision.HIGHEST,
    )
    d_normed = tensor_total(right_trans_product(d_qkv, w_qkv))
    d_input, grad_scale, grad_offset = norm_back(resid, scaling, offset, d_normed)
    return (
        d_resid + d_input,
        [
            query_key_value_weight_gradient,
            position_weight_gradient,
            attention_weight_gradient,
            content_bias_gradient,
            position_bias_gradient,
        ],
        [grad_scale, grad_offset, grad_bout],
    )


def conv_forward(resid, weights, scaling, offset, b_out, valid):
    w_glu, b_glu, tap_weights, tap_bias, gamma_vec, beta_vec, w_conv = weights
    seq_count = valid.shape[0]
    chan_part = w_conv.shape[0]
    normed = layer_norm(resid, scaling, offset).astype(jnp.bfloat16)
    pre_glu = (mat_product(normed, w_glu) + b_glu).reshape(seq_count, SEQ_LEN, 2 * chan_part)
    conv_out = conv_front(valid, pre_glu, tap_weights, tap_bias)
    masked = conv_out * valid[..., None]
    stats = dp_sum(
        jnp.stack(
            [
                jnp.sum(masked, axis=(0, 1)),
                jnp.sum(masked * conv_out, axis=(0, 1)),
                jnp.broadcast_to(jnp.sum(valid), (chan_part,)),
            ]
        )
    )
    first_sum, square_sum, count_all = stats[0], stats[1], stats[2]
    mean_vec = first_sum / count_all
    inv_std = lax.rsqrt(square_sum / count_all - mean_vec * mean_vec + BATCH_EPS)
    activated = (
        batch_apply(conv_out, gamma_vec, beta_vec, mean_vec, inv_std)
        .reshape(seq_count * SEQ_LEN, chan_part)
        .astype(jnp.bfloat16)
    )
    branch = tensor_total(mat_product(activated, w_conv)) + b_out
    return (resid + branch, (normed, pre_glu, conv_out, mean_vec, inv_std, count_all, activated))


def conv_back(d_resid, resid, saved, weights, scaling, offset, valid):
    normed, pre_glu, conv_out, mean_vec, inv_std, count_all, activated = saved
    w_glu, _, tap_weights, tap_bias, gamma_vec, beta_vec, w_conv = weights
    grad_bout = jnp.sum(d_resid, axis=0)
    branch_gradient_second = d_resid.astype(jnp.bfloat16)
    grad_wconv = left_transposed_matmul(activated, branch_gradient_second)
    d_act = right_trans_product(branch_gradient_second, w_conv).reshape(conv_out.shape)
    _, pull_norm = jax.vjp(batch_apply, conv_out, gamma_vec, beta_vec, mean_vec, inv_std)
    d_conv, grad_gamma, grad_beta, d_mean, d_inv = pull_norm(d_act)
    sums = dp_sum(jnp.stack([d_mean, d_inv]))
    d_mean, d_inv = sums[0], sums[1]
    d_var = -0.5 * inv_std * inv_std * inv_std * d_inv
    d_first = (d_mean - 2.0 * mean_vec * d_var) / count_all
    d_square = d_var / count_all
    d_conv = d_conv + valid[..., None] * (d_first + 2.0 * conv_out * d_square)
    _, pull_front = jax.vjp(partial(conv_front, valid), pre_glu, tap_weights, tap_bias)
    d_pre, grad_taps, grad_tbias = pull_front(d_conv)
    d_pre = d_pre.reshape(-1, d_pre.shape[-1])
    grad_bglu = jnp.sum(d_pre, axis=0)
    d_pre_b = d_pre.astype(jnp.bfloat16)
    grad_wglu = left_transposed_matmul(normed, d_pre_b)
    d_normed = tensor_total(right_trans_product(d_pre_b, w_glu))
    d_input, grad_scale, grad_offset = norm_back(resid, scaling, offset, d_normed)
    return (
        d_resid + d_input,
        [grad_wglu, grad_bglu, grad_taps, grad_tbias, grad_gamma, grad_beta, grad_wconv],
        [grad_scale, grad_offset, grad_bout],
    )


def layer_forward(resid, pieces, vectors, lengths, valid, table):
    resid_a, keep_a = feed_forward(
        resid, pieces[0], pieces[1], pieces[2], vectors[0], vectors[1], vectors[2]
    )
    resid_b, keep_b = attention_forward(
        resid_a, pieces[3:8], vectors[3], vectors[4], vectors[5], lengths, table
    )
    resid_c, keep_c = conv_forward(resid_b, pieces[8:15], vectors[6], vectors[7], vectors[8], valid)
    resid_d, keep_d = feed_forward(
        resid_c, pieces[15], pieces[16], pieces[17], vectors[9], vectors[10], vectors[11]
    )
    output = layer_norm(resid_d, vectors[12], vectors[13])
    return (output, (resid, resid_a, resid_b, resid_c, resid_d), (keep_a, keep_b, keep_c, keep_d))


def layer_back(d_output, pieces, vectors, lengths, valid, table, resids, keeps):
    resid, resid_a, resid_b, resid_c, resid_d = resids
    d_resid_d, grad_fscale, grad_foffset = norm_back(resid_d, vectors[12], vectors[13], d_output)
    d_resid_c, grads_d, shared_d = feed_back(
        d_resid_d, resid_c, keeps[3], pieces[15], pieces[17], vectors[9], vectors[10]
    )
    d_resid_b, grads_c, shared_c = conv_back(
        d_resid_c, resid_b, keeps[2], pieces[8:15], vectors[6], vectors[7], valid
    )
    d_resid_a, grads_b, shared_b = attention_back(
        d_resid_b, resid_a, keeps[1], pieces[3:8], vectors[3], vectors[4], lengths, table
    )
    d_resid, grads_a, shared_a = feed_back(
        d_resid_a, resid, keeps[0], pieces[0], pieces[2], vectors[0], vectors[1]
    )
    piece_grads = grads_a + grads_b + grads_c + grads_d
    vector_grads = shared_a + shared_b + shared_c + shared_d + [grad_fscale, grad_foffset]
    return (d_resid, piece_grads, vector_grads)


def adam_update(weights, first, second, gradient_list):
    first_new = BETA_ONE * first + (1.0 - BETA_ONE) * gradient_list
    second_new = BETA_TWO * second + (1.0 - BETA_TWO) * gradient_list * gradient_list
    first_hat = first_new / (1.0 - BETA_ONE**STEP_COUNT)
    second_hat = second_new / (1.0 - BETA_TWO**STEP_COUNT)
    weights_new = weights - LEARN_RATE * (
        first_hat / (jnp.sqrt(second_hat) + ADAM_EPS) + WEIGHT_DECAY * weights
    )
    return (weights_new, first_new, second_new)


def local(
    tokens,
    lengths,
    cotangent,
    params,
    shared,
    first_moment,
    second_moment,
    first_shared,
    second_shared,
):
    part_count = lax.axis_size("tensor")
    shapes = piece_shapes(
        D, FF // part_count, HEADS * HEAD_DIM // part_count, D // part_count, KERNEL
    )
    count = lax.axis_size("dp")
    plan = Plan(count, params.shape[2], shared.shape[1], shapes)
    me = lax.axis_index("dp")
    start = me * plan.shard % TILE
    where = jnp.stack([start % LANES, start // LANES, me * plan.shared_shard % LANES]).astype(
        jnp.int32
    )
    order = block_order(count)
    own = shift_out(plan, where, params.reshape(1, 1, -1), shared)
    table = position_table(SEQ_LEN, D)
    gathered, table = gather_blocks(count, own, table)
    *unpacked, vector_rows = unpack(plan, order, gathered, range(len(shapes)), True)
    pieces = [piece.reshape(shape) for piece, shape in zip(unpacked, shapes)]
    vectors = [vector_rows[at] for at in range(14)]
    valid = (jnp.arange(SEQ_LEN)[None, :] < lengths[:, None]).astype(F32)
    resid = tokens.astype(F32)
    result, resids, keeps = layer_forward(resid, pieces, vectors, lengths, valid, table)
    d_resid, piece_grads, vector_grads = layer_back(
        cotangent, pieces, vectors, lengths, valid, table, resids, keeps
    )
    blocks = pack(plan, order, piece_grads, jnp.stack(vector_grads))
    (
        grad_params,
        new_params,
        new_first,
        new_second,
        grad_shared,
        new_shared,
        new_first_sh,
        new_second_sh,
    ) = finish(
        plan,
        where,
        scatter_blocks(count, blocks),
        (params, first_moment, second_moment),
        (shared, first_shared, second_shared),
    )
    return (
        result,
        d_resid,
        grad_params,
        grad_shared,
        new_params,
        new_shared,
        new_first,
        new_second,
        new_first_sh,
        new_second_sh,
    )


def solution(mesh):
    in_specs = (
        P("dp", None),
        P("dp"),
        P("dp", None),
        P(None, "tensor", "dp"),
        P(None, "dp"),
        P(None, "tensor", "dp"),
        P(None, "tensor", "dp"),
        P(None, "dp"),
        P(None, "dp"),
    )
    out_specs = (
        P("dp", None),
        P("dp", None),
        P(None, "tensor", "dp"),
        P(None, "dp"),
        P(None, "tensor", "dp"),
        P(None, "dp"),
        P(None, "tensor", "dp"),
        P(None, "tensor", "dp"),
        P(None, "dp"),
        P(None, "dp"),
    )
    return jax.shard_map(local, mesh=mesh, in_specs=in_specs, out_specs=out_specs, check_vma=False)
```
